128 devices in a mesh: batch: 8 (over y_lo, z), tensor: 16 (over y_hi, x, core).
Axes of the slice: x: 4, y: 4 (y_hi: 2, y_lo: 2; y = y_hi * 2 + y_lo), z: 4, core: 2. Of those that a mesh axis runs over, the one named last changes fastest.
Arguments:
- attn_values: bfloat16 [2048, 8192], P('batch', 'tensor'), may hold values from -6 to 6
- out_weight: bfloat16 [8192, 8192], P('tensor'), may hold values from -0.09375 to 0.09375
- residual_t: bfloat16 [8192, 2048], P('tensor', 'batch'), may hold values from -6 to 6
- projector: bfloat16 [8192, 4096], P('tensor'), may hold values from -0.0625 to 0.0625
- student_input: bfloat16 [2048, 4096], P('batch', 'tensor'), may hold values from -6 to 6
- norm_gain: float32 [4096], replicated, may hold values from 0.1 to 1.9
- w_gate: bfloat16 [4096, 8192], P('batch', 'tensor'), may hold values from -0.09375 to 0.09375
- w_up: bfloat16 [4096, 8192], P('batch', 'tensor'), may hold values from -0.09375 to 0.09375
- w_down: bfloat16 [4096, 8192], P('batch', 'tensor'), may hold values from -0.0625 to 0.0625
- route_index: int32 [8, 64], P('batch'), may hold values from -1 to 255, as said below
Outputs:
- teacher_hidden: bfloat16 [8192, 2048], P('tensor', 'batch')
- grad_gate: float32 [4096, 8192], P('batch', 'tensor')
- grad_up: float32 [4096, 8192], P('batch', 'tensor')
- grad_down: float32 [4096, 8192], P('batch', 'tensor')
The draws below stay inside these ranges and needn't reach their ends.
Inputs may be any that keep to these rules, and one draw needn't show every extreme that they name: `route_index`: in each batch group the live slots come first, hold distinct positions in increasing order, and the empty slots after them hold -1. The batch groups hold 256 live slots together, and some batch group has all 64 slots live.
All inputs are finite; a program needn't handle non-finite values.
Results may differ from the reference program's by a relative error of at most 0.025.
Values may be sent and summed in bfloat16 or wider, within the bound.
No kernel may reach another device: no remote copies, remote signals or barrier semaphores. Data moves between devices by JAX's collectives and lax.ppermute only.
A program may use at most 128 MiB of HBM per device.

```python
import math
import jax
import jax.numpy as jnp
from jax import lax

DT = 8192
D = 4096
FF = 8192
TOK = 256
CAP = 32
CAPMAX = 64
ROUTED = 256
TOKENS = 2048
N_BATCH = 8
N_TENSOR = 16


def draw_route_index(key, part):
    key_perm, key_spread, key_pos = jax.random.split(jax.random.fold_in(key, 71), 3)
    half_groups = N_BATCH // 2
    spread = jax.random.randint(key_spread, (half_groups,), 0, CAP + 1)
    spread = spread.at[0].set(CAP)
    counts = jnp.concatenate([CAP + spread, CAP - spread])
    order_groups = jax.random.permutation(key_perm, N_BATCH)
    counts = counts[order_groups]
    group_keys = jax.random.split(key_pos, N_BATCH)

    def one_group(group_key, live_count):
        shuffled = jax.random.permutation(group_key, TOK)[:CAPMAX]
        slot_ids = jnp.arange(CAPMAX, dtype=jnp.int32)
        chosen = jnp.where(slot_ids < live_count, shuffled, TOK)
        chosen = jnp.sort(chosen)
        return jnp.where(slot_ids < live_count, chosen, -1)
    return jax.vmap(one_group)(group_keys, counts).astype(jnp.int32)


def raised(array, stream_key, source, target, blocks, factor):
    owner, partner = [(jnp.arange(array.shape[dim]) // (array.shape[dim] // blocks)).reshape([-1 if axis == dim else 1 for axis in range(array.ndim)]) for dim in (source, target)]
    chosen = jax.random.permutation(stream_key, blocks)[partner]
    strong = (owner == chosen) | (owner == (partner + blocks // 2) % blocks)
    return jnp.where(strong, factor * array, array)


def steps_of(key, shape, shards, least, high):
    loudness, own = 1.0, jax.random.fold_in(key, 6)
    for position, shards_of in shards:
        heights = jnp.exp(jax.random.uniform(jax.random.fold_in(own, position), (shards_of,), jnp.float32, least / len(shards), high / len(shards)))
        loudness = loudness * jnp.repeat(heights, shape[position] // shards_of).reshape([-1 if axis == position else 1 for axis in range(len(shape))])
    return loudness


def bell_draw(own_key, shape, deviation, reach, cuts=(), kind=jnp.bfloat16):
    level = steps_of(own_key, shape, cuts, -0.22, 0.18) if cuts else 1.0
    values = jax.random.normal(own_key, shape, jnp.float32) * deviation * level
    return jnp.minimum(jnp.maximum(values, -reach), reach).astype(kind)


def gaussian_with(own_key, extent, scale, limit, shards, heavy, kind=jnp.bfloat16):
    drawn = scale * jax.random.normal(own_key, extent, jnp.float32)
    if shards:
        drawn = drawn * steps_of(own_key, extent, shards, -0.22, 0.18)
    return jnp.clip(raised(drawn, jax.random.fold_in(own_key, 3), *heavy), -limit, limit).astype(kind)


def setup_inputs(seed: int = 0) -> dict:
    arg_keys = jax.random.split(jax.random.key(seed), 11)
    attn_values = bell_draw(arg_keys[0], (TOKENS, DT), 1.0, 6.0, ((0, 8), (1, 16)))
    out_weight = gaussian_with(arg_keys[1], (DT, DT), DT ** -0.5, 0.09375, ((0, 16),), (0, 1, 16, 2.0))
    residual_t = bell_draw(arg_keys[2], (DT, TOKENS), 1.0, 6.0, ((0, 16), (1, 8)))
    projector = bell_draw(arg_keys[3], (DT, D), DT ** -0.5, 0.0625, ((0, 16),))
    student_input = bell_draw(arg_keys[4], (TOKENS, D), 1.0, 6.0, ((0, 8), (1, 16)))
    norm_gain = jnp.clip(1.0 + 0.18 * jax.random.normal(arg_keys[5], (D,), jnp.float32), 0.1, 1.9)
    w_gate = bell_draw(arg_keys[6], (D, FF), D ** -0.5, 0.09375, ((0, 8), (1, 16)))
    w_up = bell_draw(arg_keys[7], (D, FF), D ** -0.5, 0.09375, ((0, 8), (1, 16)))
    w_down = bell_draw(arg_keys[8], (D, FF), FF ** -0.5, 0.0625, ((0, 8), (1, 16)))
    route_index = draw_route_index(jax.random.fold_in(arg_keys[10], 71), 0)
    return {"attn_values": attn_values, "out_weight": out_weight, "residual_t": residual_t, "projector": projector, "student_input": student_input, "norm_gain": norm_gain, "w_gate": w_gate, "w_up": w_up, "w_down": w_down, "route_index": route_index}


epsilon = 1e-05

def reference(attn_values, out_weight, residual_t, projector, student_input, norm_gain, w_gate, w_up, w_down, route_index):
    shard_width = DT // N_TENSOR

    def teacher_step(running, shard_no):
        offset = (shard_no * shard_width).astype(jnp.int32)
        columns = lax.dynamic_slice_in_dim(attn_values, offset, shard_width, 1)
        rows_block = lax.dynamic_slice_in_dim(out_weight, offset, shard_width, 0)
        partial_sum = lax.dot_general(rows_block, columns, (((0,), (1,)), ((), ())), preferred_element_type=jnp.float32)
        rounded = lax.optimization_barrier(partial_sum.astype(jnp.bfloat16))
        return (running + rounded.astype(jnp.float32), None)
    summed, _ = lax.scan(teacher_step, jnp.zeros((DT, TOKENS), jnp.float32), jnp.arange(N_TENSOR, dtype=jnp.int32))
    teacher_hidden = (residual_t.astype(jnp.float32) + summed).astype(jnp.bfloat16)
    loss_scale = 1.0 / math.sqrt(ROUTED)

    def group_step(running, group_no):
        slot_pos = lax.dynamic_index_in_dim(route_index, group_no, 0, keepdims=False)
        present = slot_pos >= 0
        safe_slot = (jnp.maximum(slot_pos, 0) + group_no * TOK).astype(jnp.int32)
        routed_teacher = jnp.where(present[None, :], jnp.take(teacher_hidden, safe_slot, axis=1), 0).astype(jnp.bfloat16)
        target = lax.dot_general(routed_teacher, projector, (((0,), (0,)), ((), ())), preferred_element_type=jnp.float32)
        routed_input = jnp.where(present[:, None], jnp.take(student_input, safe_slot, axis=0), 0).astype(jnp.float32)
        mean_square = lax.optimization_barrier(jnp.mean(routed_input * routed_input, axis=1, keepdims=True))
        normed = (routed_input * lax.rsqrt(mean_square + epsilon) * norm_gain[None, :]).astype(jnp.bfloat16)
        gate_act = jnp.dot(normed, w_gate, preferred_element_type=jnp.float32)
        up_act = jnp.dot(normed, w_up, preferred_element_type=jnp.float32)
        sigma_gate = jax.nn.sigmoid(gate_act)
        hidden = (gate_act * sigma_gate * up_act).astype(jnp.bfloat16)
        student_out = lax.dot_general(hidden, w_down, (((1,), (1,)), ((), ())), preferred_element_type=jnp.float32)
        misfit = jnp.where(present[:, None], student_out - target, 0.0)
        grad_out = (misfit * loss_scale).astype(jnp.bfloat16)
        grad_hidden = jnp.dot(grad_out, w_down, preferred_element_type=jnp.float32)
        grad_gate_act = (grad_hidden * up_act * sigma_gate * (1.0 + gate_act * (1.0 - sigma_gate))).astype(jnp.bfloat16)
        grad_up_act = (grad_hidden * gate_act * sigma_gate).astype(jnp.bfloat16)
        dims = (((0,), (0,)), ((), ()))
        gate_part = lax.dot_general(normed, grad_gate_act, dims, preferred_element_type=jnp.float32)
        up_part = lax.dot_general(normed, grad_up_act, dims, preferred_element_type=jnp.float32)
        down_part = lax.dot_general(grad_out, hidden, dims, preferred_element_type=jnp.float32)
        parts = (gate_part, up_part, down_part)
        updated = tuple((acc + lax.optimization_barrier(part.astype(jnp.bfloat16)).astype(jnp.float32) for acc, part in zip(running, parts)))
        return (updated, None)
    zero_grad = jnp.zeros((D, FF), jnp.float32)
    grads, _ = lax.scan(group_step, (zero_grad, zero_grad, zero_grad), jnp.arange(N_BATCH, dtype=jnp.int32))
    return (teacher_hidden, grads[0], grads[1], grads[2])
```

```python
import math

import jax
import jax.numpy as jnp
from jax import lax
from jax.experimental import pallas as pl
from jax.experimental.pallas import tpu as pltpu
from jax.sharding import PartitionSpec as P

EPS = 1e-05
BF = jnp.bfloat16
F32 = jnp.float32
MIB = 1 << 20


def params(mib):
    return pltpu.CompilerParams(vmem_limit_bytes=mib * MIB)


def cost(flops, nbytes):
    return pl.CostEstimate(flops=flops, bytes_accessed=nbytes, transcendentals=0)


def dot(a, b, ca=1, cb=0):
    return lax.dot_general(a, b, (((ca,), (cb,)), ((), ())), preferred_element_type=F32)


def whole(shape):
    return pl.BlockSpec(shape, lambda *_: (0,) * len(shape))


def slot_rows(route, tokens):
    slots = route.shape[1]
    grid = (slots, slots)
    diagonal = lax.broadcasted_iota(jnp.int32, grid, 0) == lax.broadcasted_iota(jnp.int32, grid, 1)
    spread = jnp.broadcast_to(route.astype(F32), grid)
    column = jnp.sum(jnp.where(diagonal, spread, 0.0), axis=1, keepdims=True)
    lane = lax.broadcasted_iota(jnp.int32, (slots, tokens), 1).astype(F32)
    return jnp.where(lane == column, 1.0, 0.0).astype(BF)


def rows_kernel(route_ref, x_ref, out_ref):
    route = route_ref[...]
    slots, wide = route.shape[1], x_ref.shape[1]
    rows = dot(slot_rows(route, x_ref.shape[0]), x_ref[...]).astype(BF)
    half = slots // 2
    out_ref[0:half, 0:wide] = rows[0:half]
    out_ref[0:half, wide : 2 * wide] = rows[half:]
    live = jnp.sum(jnp.where(route >= 0, 1.0, 0.0), axis=1, keepdims=True)
    out_ref[half : half + 8, :] = jnp.broadcast_to(live, (8, 2 * wide)).astype(BF)


def teacher_kernel(route_ref, attn_ref, weight_ref, full_ref, routed_ref, left_ref):
    tokens = attn_ref.shape[0]
    slots = route_ref.shape[1]

    @pl.when(pl.program_id(0) == 0)
    def _():
        left_ref[0:tokens, :] = attn_ref[...]
        left_ref[tokens:, :] = dot(slot_rows(route_ref[...], tokens), attn_ref[...]).astype(BF)

    product = dot(left_ref[...], weight_ref[...]).astype(BF)
    full_ref[...] = product[0:tokens]
    routed_ref[0, 0:slots, :] = product[tokens:]


def up_kernel(
    group_ref, route_ref, got_ref, residual_ref, gain_ref, gate_ref, up_ref,
    out_ref, rows_ref, padded_ref,
):
    group = group_ref[0]
    slots = route_ref.shape[1]
    sources, _, wide = got_ref.shape
    groups = sources // 2
    half, side = slots // 2, wide // 2
    total = groups * out_ref.shape[1]

    routed = dot(slot_rows(route_ref[...], residual_ref.shape[1]), residual_ref[...], 1, 1)
    for s in range(sources):
        routed = routed + got_ref[s, 0:slots, :].astype(F32)
        g, d = s // 2, s % 2
        block = got_ref[s, slots : slots + half, :]
        padded_ref[g * slots : g * slots + half, d * side : (d + 1) * side] = block[:, 0:side]
        padded_ref[g * slots + half : (g + 1) * slots, d * side : (d + 1) * side] = block[:, side:]
    at = slots + half
    counts = [got_ref[2 * g, at : at + 8, 0:128].astype(F32)[0:1] for g in range(groups)]
    zero = jnp.zeros_like(counts[0])
    starts, own_start, own_count, run = [], zero, zero, zero
    for g in range(groups):
        starts.append(run)
        own_start = jnp.where(group == g, run, own_start)
        own_count = jnp.where(group == g, counts[g], own_count)
        run = run + counts[g]

    row = lax.broadcasted_iota(jnp.int32, (total, 2 * slots), 0)
    lane = lax.broadcasted_iota(jnp.int32, (total, 2 * slots), 1)
    second = lane >= slots
    slot = jnp.where(second, lane - slots, lane)
    slot_f = slot.astype(F32)
    shift = (row - slot).astype(F32)
    x = jnp.zeros((total, wide), F32)
    for q in range(groups // 2):
        start = jnp.where(second, starts[2 * q + 1], starts[2 * q])
        count = jnp.where(second, counts[2 * q + 1], counts[2 * q])
        chosen = jnp.where((shift == start) & (slot_f < count), 1.0, 0.0).astype(BF)
        x = x + dot(chosen, padded_ref[2 * q * slots : 2 * (q + 1) * slots, :])
    chosen = jnp.where((shift == own_start) & (slot_f < own_count) & (lane < slots), 1.0, 0.0)
    routed = routed.astype(BF)
    target_rows = dot(chosen[:, 0:slots].astype(BF), routed).astype(BF)

    square = jnp.sum(x * x, axis=1, keepdims=True)
    high = square.astype(BF)
    low = (square - high.astype(F32)).astype(BF)
    lane128 = lax.broadcasted_iota(jnp.int32, (total, 128), 1)
    squares = jnp.where(lane128 < 64, high.astype(F32), low.astype(F32)).astype(BF)
    scaled = (x * gain_ref[...]).astype(BF)
    rows_ref[...] = scaled
    gate = dot(scaled, gate_ref[...]).astype(BF)
    up = dot(scaled, up_ref[...]).astype(BF)
    per = out_ref.shape[1]
    for g in range(groups):
        own = slice(g * per, (g + 1) * per)
        out_ref[g, :, 0:wide] = gate[own]
        out_ref[g, :, wide : 2 * wide] = up[own]
        out_ref[g, :, 2 * wide : 3 * wide] = target_rows[own]
        out_ref[g, :, 3 * wide :] = squares[own]


def down_kernel(
    features, got_ref, down_ref, projector_ref,
    out_ref, gate_ref, up_ref, hidden_ref, scale_ref, target_ref,
):
    wide = hidden_ref.shape[1]

    @pl.when(pl.program_id(0) == 0)
    def _():
        total = got_ref[0].astype(F32)
        for g in range(1, got_ref.shape[0]):
            total = total + got_ref[g].astype(F32)
        square = total[:, 3 * wide : 3 * wide + 1] + total[:, 3 * wide + 64 : 3 * wide + 65]
        scale = lax.rsqrt(square * (1.0 / features) + EPS)
        gate = total[:, 0:wide] * scale
        up = total[:, wide : 2 * wide] * scale
        gate_ref[...] = gate
        up_ref[...] = up
        scale_ref[...] = jnp.broadcast_to(scale, scale_ref.shape)
        target_ref[...] = total[:, 2 * wide : 3 * wide].astype(BF)
        hidden_ref[...] = (gate * jax.nn.sigmoid(gate) * up).astype(BF)

    part = dot(hidden_ref[...], down_ref[...], 1, 1) - dot(target_ref[...], projector_ref[...])
    part = part.astype(BF)
    chunk = out_ref.shape[2]
    for i in range(out_ref.shape[0]):
        out_ref[i] = part[:, i * chunk : (i + 1) * chunk]


def misfit_kernel(scale, got_ref, out_ref):
    total = got_ref[0].astype(F32)
    for s in range(1, got_ref.shape[0]):
        total = total + got_ref[s].astype(F32)
    grad = (total * scale).astype(BF)
    for s in range(out_ref.shape[0]):
        out_ref[s] = grad


def back_kernel(got_ref, down_ref, gate_ref, up_ref, hidden_ref, scale_ref, out_ref, total_ref):
    step, chunk = pl.program_id(0), got_ref.shape[2]
    wide = hidden_ref.shape[1]

    @pl.when(step == 0)
    def _():
        total_ref[...] = jnp.zeros_like(total_ref)

    part = total_ref[...]
    for i in range(got_ref.shape[0]):
        part = part + dot(got_ref[i], down_ref[i * chunk : (i + 1) * chunk, :])
        out_ref[step, :, 3 * wide + i * chunk : 3 * wide + (i + 1) * chunk] = got_ref[i]
    total_ref[...] = part

    @pl.when(step == pl.num_programs(0) - 1)
    def _():
        grad = total_ref[...] * scale_ref[:, 0:1]
        gate, up = gate_ref[...], up_ref[...]
        sigma = jax.nn.sigmoid(gate)
        grad_gate = (grad * up * sigma * (1.0 + gate * (1.0 - sigma))).astype(BF)
        grad_up = (grad * gate * sigma).astype(BF)
        for g in range(out_ref.shape[0]):
            out_ref[g, :, 0:wide] = grad_gate
            out_ref[g, :, wide : 2 * wide] = grad_up
            out_ref[g, :, 2 * wide : 3 * wide] = hidden_ref[...]


def weights_kernel(rows_ref, got_ref, grad_ref, gate_ref, up_ref, down_ref):
    wide = gate_ref.shape[1]
    groups, per, _ = got_ref.shape

    def columns(i):
        return got_ref[:, :, i * wide : (i + 1) * wide].reshape(groups * per, wide)

    rows = rows_ref[...]
    gate_ref[...] = dot(rows, columns(0), 0, 0)
    up_ref[...] = dot(rows, columns(1), 0, 0)
    grad = grad_ref[...].reshape(groups * per, grad_ref.shape[2])
    down_ref[...] = dot(grad, columns(2), 0, 0)


def on_device(
    attn_values,
    out_weight,
    residual_t,
    projector,
    student_input,
    norm_gain,
    w_gate,
    w_up,
    w_down,
    route_index,
):
    groups, parts = lax.axis_size("batch"), lax.axis_size("tensor")
    slots = route_index.shape[1]
    tokens, wide = attn_values.shape
    side = student_input.shape[1]
    features = norm_gain.shape[0]
    live = tokens * groups // 8
    per = live // groups
    units = w_gate.shape[1]
    extra = slots // 2 + 8
    down_full = lax.all_gather(w_down, "batch", axis=0, tiled=True)

    rows = pl.pallas_call(
        rows_kernel,
        out_shape=jax.ShapeDtypeStruct((extra, 2 * side), BF),
        name="rows",
    )(route_index, student_input)
    pairs = [
        (b * parts + t, (t // 2) * parts + 2 * b + t % 2)
        for b in range(groups)
        for t in range(parts)
    ]
    rows = lax.ppermute(rows, ("batch", "tensor"), pairs)

    full, routed = pl.pallas_call(
        teacher_kernel,
        grid=(parts,),
        in_specs=[
            whole(route_index.shape),
            whole(attn_values.shape),
            pl.BlockSpec((wide, wide), lambda j: (0, j)),
        ],
        out_specs=[
            pl.BlockSpec((tokens, wide), lambda j: (j, 0)),
            pl.BlockSpec((1, slots + extra, wide), lambda j: (j, 0, 0)),
        ],
        out_shape=[
            jax.ShapeDtypeStruct((parts * tokens, wide), BF),
            jax.ShapeDtypeStruct((parts, slots + extra, wide), BF),
        ],
        scratch_shapes=[pltpu.VMEM((tokens + slots, wide), BF)],
        compiler_params=params(16),
        cost_estimate=cost(2 * (tokens + slots) * wide * wide * parts, 14 * MIB),
        name="teacher",
    )(route_index, attn_values, out_weight)
    summed = lax.psum_scatter(full, "tensor", scatter_dimension=0, tiled=True)
    teacher_hidden = (residual_t.astype(F32) + summed.astype(F32).T).astype(BF)

    routed = routed.at[:, slots:, :].set(jnp.broadcast_to(rows[None], (parts, *rows.shape)))
    routed = lax.all_to_all(routed, "tensor", 0, 0, tiled=True)

    group = lax.axis_index("batch")
    gain = lax.dynamic_slice_in_dim(norm_gain, group * wide, wide)[None]
    sent, scaled = pl.pallas_call(
        up_kernel,
        in_specs=[pl.BlockSpec(memory_space=pltpu.SMEM)]
        + [pl.BlockSpec(memory_space=pltpu.VMEM)] * 6,
        out_shape=[
            jax.ShapeDtypeStruct((groups, per, 3 * wide + 128), BF),
            jax.ShapeDtypeStruct((live, wide), BF),
        ],
        scratch_shapes=[pltpu.VMEM((groups * slots, wide), BF)],
        compiler_params=params(24),
        name="up",
    )(group.reshape(1), route_index, routed, residual_t, gain, w_gate, w_up)
    got = lax.all_to_all(sent, "batch", 0, 0, tiled=True)

    steps = features // wide
    chunk = features // parts
    each = parts // steps
    flat = jax.ShapeDtypeStruct((per, units), F32)
    misfit, gate, up, hidden, scale = pl.pallas_call(
        lambda *refs: down_kernel(features, *refs),
        grid=(steps,),
        in_specs=[
            whole(got.shape),
            pl.BlockSpec((wide, units), lambda j: (j, 0)),
            pl.BlockSpec((wide, wide), lambda j: (0, j)),
        ],
        out_specs=[pl.BlockSpec((each, per, chunk), lambda j: (j, 0, 0))]
        + [whole((per, units))] * 3
        + [whole((per, 128))],
        out_shape=[
            jax.ShapeDtypeStruct((parts, per, chunk), BF),
            flat,
            flat,
            jax.ShapeDtypeStruct((per, units), BF),
            jax.ShapeDtypeStruct((per, 128), F32),
        ],
        scratch_shapes=[pltpu.VMEM((per, wide), BF)],
        compiler_params=params(16),
        name="down",
    )(got, down_full, projector)
    misfit = lax.all_to_all(misfit, "tensor", 0, 0, tiled=True)
    loss_scale = 1.0 / math.sqrt(live)
    grad_out = pl.pallas_call(
        lambda *refs: misfit_kernel(loss_scale, *refs),
        out_shape=jax.ShapeDtypeStruct(misfit.shape, BF),
        name="misfit",
    )(misfit)
    grad_out = lax.all_to_all(grad_out, "tensor", 0, 0, tiled=True)

    sent = pl.pallas_call(
        back_kernel,
        grid=(steps,),
        in_specs=[
            pl.BlockSpec((each, per, chunk), lambda j: (j, 0, 0)),
            pl.BlockSpec((wide, units), lambda j: (j, 0)),
        ]
        + [whole((per, units))] * 3
        + [whole((per, 128))],
        out_specs=whole((groups, per, 4 * wide)),
        out_shape=jax.ShapeDtypeStruct((groups, per, 4 * wide), BF),
        scratch_shapes=[pltpu.VMEM((per, units), F32)],
        compiler_params=params(16),
        name="back",
    )(grad_out, down_full, gate, up, hidden, scale)
    got = lax.all_to_all(sent, "batch", 0, 0, tiled=True)

    tile = wide // 4
    grads = pl.pallas_call(
        weights_kernel,
        grid=(4,),
        in_specs=[
            pl.BlockSpec((live, tile), lambda j: (0, j)),
            whole(got.shape),
            pl.BlockSpec((groups, per, tile), lambda j: (0, 0, 3 * wide // tile + j)),
        ],
        out_specs=[pl.BlockSpec((tile, units), lambda j: (j, 0))] * 3,
        out_shape=[jax.ShapeDtypeStruct((wide, units), F32)] * 3,
        compiler_params=params(16),
        name="weights",
    )(scaled, got, got)
    return (teacher_hidden, *grads)


def solution(mesh):
    in_specs = (
        P("batch", "tensor"),
        P("tensor", None),
        P("tensor", "batch"),
        P("tensor", None),
        P("batch", "tensor"),
        P(),
        P("batch", "tensor"),
        P("batch", "tensor"),
        P("batch", "tensor"),
        P("batch", None),
    )
    out_specs = (P("tensor", "batch"),) + (P("batch", "tensor"),) * 3
    return jax.shard_map(
        on_device, mesh=mesh, in_specs=in_specs, out_specs=out_specs, check_vma=False
    )
```

```python
import math

import jax
import jax.numpy as jnp
from jax import lax
from jax.experimental import pallas as pl
from jax.experimental.pallas import tpu as pltpu
from jax.sharding import PartitionSpec as P

EPS = 1e-05
BF = jnp.bfloat16
F32 = jnp.float32
MIB = 1 << 20


def params(mib):
    return pltpu.CompilerParams(vmem_limit_bytes=mib * MIB)


def cost(flops, nbytes):
    return pl.CostEstimate(flops=flops, bytes_accessed=nbytes, transcendentals=0)


def dot(a, b, ca=1, cb=0):
    return lax.dot_general(a, b, (((ca,), (cb,)), ((), ())), preferred_element_type=F32)


def whole(shape):
    return pl.BlockSpec(shape, lambda *_: (0,) * len(shape))


def slot_rows(route, tokens):
    slots = route.shape[1]
    grid = (slots, slots)
    diagonal = lax.broadcasted_iota(jnp.int32, grid, 0) == lax.broadcasted_iota(jnp.int32, grid, 1)
    spread = jnp.broadcast_to(route.astype(F32), grid)
    column = jnp.sum(jnp.where(diagonal, spread, 0.0), axis=1, keepdims=True)
    lane = lax.broadcasted_iota(jnp.int32, (slots, tokens), 1).astype(F32)
    return jnp.where(lane == column, 1.0, 0.0).astype(BF)


def rows_kernel(route_ref, x_ref, out_ref):
    route = route_ref[...]
    slots, wide = route.shape[1], x_ref.shape[1]
    rows = dot(slot_rows(route, x_ref.shape[0]), x_ref[...]).astype(BF)
    half = slots // 2
    out_ref[0:half, 0:wide] = rows[0:half]
    out_ref[0:half, wide : 2 * wide] = rows[half:]
    live = jnp.sum(jnp.where(route >= 0, 1.0, 0.0), axis=1, keepdims=True)
    out_ref[half : half + 8, :] = jnp.broadcast_to(live, (8, 2 * wide)).astype(BF)


def teacher_kernel(
    core_ref, route_ref, attn_ref, weight_ref, keep_ref, send_ref, routed_ref, left_ref
):
    step = pl.program_id(0)
    tokens = attn_ref.shape[0]
    slots = route_ref.shape[1]

    @pl.when(step == 0)
    def _():
        left_ref[0:tokens, :] = attn_ref[...]
        left_ref[tokens:, :] = dot(slot_rows(route_ref[...], tokens), attn_ref[...]).astype(BF)

    product = dot(left_ref[...], weight_ref[...]).astype(BF)
    routed_ref[0, 0:slots, :] = product[tokens:]

    @pl.when(step % 2 == 0)
    def _():
        send_ref[...] = product[0:tokens]

    @pl.when(step % 2 == 1)
    def _():
        keep_ref[...] = product[0:tokens]


def core_sum_kernel(x_ref, keep_ref, got_ref, *out_refs):
    total = (keep_ref[...].astype(F32) + got_ref[...].astype(F32)).astype(BF)
    for j, out_ref in enumerate(out_refs):

        @pl.when(pl.program_id(0) // 2 == j)
        def _(out_ref=out_ref):
            out_ref[...] = total


def x_sum_kernel(y_ref, *refs):
    total = refs[0][...].astype(F32)
    for ref in refs[1:-2]:
        total = total + ref[...].astype(F32)
    for j, out_ref in enumerate(refs[-2:]):

        @pl.when(pl.program_id(0) == j)
        def _(out_ref=out_ref):
            out_ref[...] = total.astype(out_ref.dtype)


def residual_kernel(residual_ref, keep_ref, got_ref, out_ref):
    summed = keep_ref[...] + got_ref[...].astype(F32)
    out_ref[...] = (residual_ref[...].astype(F32) + summed.T).astype(BF)


def up_kernel(
    group_ref, route_ref, got_ref, residual_ref, gain_ref, gate_ref, up_ref,
    out_ref, rows_ref, chosen_ref, padded_ref,
):
    slots = route_ref.shape[1]
    sources, _, wide = got_ref.shape
    groups = sources // 2
    half, side = slots // 2, wide // 2
    per = out_ref.shape[1]
    total = groups * per

    routed = dot(slot_rows(route_ref[...], residual_ref.shape[1]), residual_ref[...], 1, 1)
    for s in range(sources):
        routed = routed + got_ref[s, 0:slots, :].astype(F32)
        g, d = s // 2, s % 2
        block = got_ref[s, slots : slots + half, :]
        padded_ref[g * slots : g * slots + half, d * side : (d + 1) * side] = block[:, 0:side]
        padded_ref[g * slots + half : (g + 1) * slots, d * side : (d + 1) * side] = block[:, side:]
    routed = routed.astype(BF)
    at = slots + half
    counts = [got_ref[2 * g, at : at + 8, 0 : 2 * slots].astype(F32)[0:1] for g in range(groups)]

    row = lax.broadcasted_iota(jnp.int32, (total, 2 * slots), 0)
    lane = lax.broadcasted_iota(jnp.int32, (total, 2 * slots), 1)
    second = lane >= slots
    slot = jnp.where(second, lane - slots, lane)
    slot_f = slot.astype(F32)
    shift = (row - slot).astype(F32)
    x = jnp.zeros((total, wide), F32)
    run = jnp.zeros_like(counts[0])
    for q in range(groups // 2):
        one, two = counts[2 * q], counts[2 * q + 1]
        start = jnp.where(second, run + one, run)
        count = jnp.where(second, two, one)
        run = run + one + two
        chosen = jnp.where((shift == start) & (slot_f < count), 1.0, 0.0).astype(BF)
        chosen_ref[:, 2 * q * slots : 2 * (q + 1) * slots] = chosen
        x = x + dot(chosen, padded_ref[2 * q * slots : 2 * (q + 1) * slots, :])

    square = jnp.sum(x * x, axis=1, keepdims=True)
    high = square.astype(BF)
    low = (square - high.astype(F32)).astype(BF)
    lane128 = lax.broadcasted_iota(jnp.int32, (total, 128), 1)
    squares = jnp.where(lane128 < 64, high.astype(F32), low.astype(F32)).astype(BF)
    scaled = (x * gain_ref[...]).astype(BF)
    rows_ref[...] = scaled
    gate = dot(scaled, gate_ref[...]).astype(BF)
    up = dot(scaled, up_ref[...]).astype(BF)
    at = 2 * wide + 128
    for g in range(groups):
        own = slice(g * per, (g + 1) * per)
        out_ref[g, :, 0:wide] = gate[own]
        out_ref[g, :, wide : 2 * wide] = up[own]
        out_ref[g, :, 2 * wide : at] = squares[own]
        for h in range(slots // per):
            out_ref[g, :, at + h * wide : at + (h + 1) * wide] = routed[h * per : (h + 1) * per]


def hidden_kernel(features, got_ref, out_ref, gate_ref, up_ref, scale_ref):
    wide = gate_ref.shape[1]
    at = 2 * wide + 128
    total = got_ref[0, :, 0:at].astype(F32)
    for g in range(1, got_ref.shape[0]):
        total = total + got_ref[g, :, 0:at].astype(F32)
    square = total[:, 2 * wide : 2 * wide + 1] + total[:, 2 * wide + 64 : 2 * wide + 65]
    scale = lax.rsqrt(square * (1.0 / features) + EPS)
    gate = total[:, 0:wide] * scale
    up = total[:, wide : 2 * wide] * scale
    gate_ref[...] = gate
    up_ref[...] = up
    scale_ref[...] = jnp.broadcast_to(scale, scale_ref.shape)
    hidden = (gate * jax.nn.sigmoid(gate) * up).astype(BF)
    for g in range(out_ref.shape[0]):
        out_ref[g] = hidden


def target_kernel(group_ref, got_ref, chosen_ref, projector_ref, out_ref, rows_ref):
    groups, per, _ = got_ref.shape
    wide = rows_ref.shape[1]
    parts = rows_ref.shape[0] // (groups * per)
    at = got_ref.shape[2] - parts * wide
    for g in range(groups):
        for h in range(parts):
            first = (g * parts + h) * per
            rows_ref[first : first + per, :] = got_ref[g, :, at + h * wide : at + (h + 1) * wide]
    rows = dot(chosen_ref[...], rows_ref[...]).astype(BF)
    out_ref[...] = dot(rows, projector_ref[...])


def down_kernel(got_ref, down_ref, target_ref, out_ref):
    rows, wide = target_ref.shape
    part = dot(got_ref[...].reshape(rows, wide), down_ref[...], 1, 1) - target_ref[...]
    out_ref[...] = part.astype(BF).reshape(out_ref.shape)


def misfit_kernel(scale, got_ref, out_ref):
    total = got_ref[0].astype(F32)
    for s in range(1, got_ref.shape[0]):
        total = total + got_ref[s].astype(F32)
    grad = (total * scale).astype(BF)
    for s in range(out_ref.shape[0]):
        out_ref[s] = grad


def back_kernel(got_ref, down_ref, out_ref):
    groups, per, wide = out_ref.shape
    part = dot(got_ref[...].reshape(groups * per, got_ref.shape[2]), down_ref[...])
    out_ref[...] = part.astype(BF).reshape(groups, per, wide)


def acts_kernel(got_ref, gate_ref, up_ref, scale_ref, out_ref):
    wide = gate_ref.shape[1]
    grad = got_ref[0].astype(F32)
    for g in range(1, got_ref.shape[0]):
        grad = grad + got_ref[g].astype(F32)
    grad = grad * scale_ref[:, 0:1]
    gate, up = gate_ref[...], up_ref[...]
    sigma = jax.nn.sigmoid(gate)
    grad_gate = (grad * up * sigma * (1.0 + gate * (1.0 - sigma))).astype(BF)
    grad_up = (grad * gate * sigma).astype(BF)
    for g in range(out_ref.shape[0]):
        out_ref[g, :, 0:wide] = grad_gate
        out_ref[g, :, wide : 2 * wide] = grad_up


def down_weights_kernel(grad_ref, hidden_ref, out_ref):
    rows = hidden_ref.shape[0] * hidden_ref.shape[1]
    wide = out_ref.shape[0]
    out_ref[...] = dot(grad_ref[...].reshape(rows, wide), hidden_ref[...].reshape(rows, -1), 0, 0)


def weights_kernel(rows_ref, got_ref, gate_ref, up_ref):
    wide = gate_ref.shape[1]
    acts = got_ref[...].reshape(got_ref.shape[0] * got_ref.shape[1], 2 * wide)
    gate_ref[...] = dot(rows_ref[...], acts[:, 0:wide], 0, 0)
    up_ref[...] = dot(rows_ref[...], acts[:, wide:], 0, 0)


def on_device(
    attn_values,
    out_weight,
    residual_t,
    projector,
    student_input,
    norm_gain,
    w_gate,
    w_up,
    w_down,
    route_index,
):
    groups, parts = lax.axis_size("batch"), lax.axis_size("tensor")
    slots = route_index.shape[1]
    tokens, wide = attn_values.shape
    side = student_input.shape[1]
    features = norm_gain.shape[0]
    live = tokens * groups // 8
    per = live // groups
    units = w_gate.shape[1]
    extra = slots // 2 + 8
    group, part = lax.axis_index("batch"), lax.axis_index("tensor")
    core, x_at, y_at = part & 1, (part >> 1) & 3, part >> 3
    shape = jax.ShapeDtypeStruct
    vmem = pl.BlockSpec(memory_space=pltpu.VMEM)

    rows = pl.pallas_call(
        rows_kernel,
        out_shape=shape((extra, 2 * side), BF),
        cost_estimate=cost(2 * slots * tokens * side, MIB // 4),
        name="rows",
    )(route_index, student_input)
    pairs = [
        (b * parts + t, (t // 2) * parts + 2 * b + t % 2)
        for b in range(groups)
        for t in range(parts)
    ]
    rows = lax.ppermute(rows, ("batch", "tensor"), pairs)

    def column(j, core):
        return 2 * (j >> 1) + jnp.where((j & 1) == 0, 1 - core[0], core[0])

    keep, send, routed = pl.pallas_call(
        teacher_kernel,
        grid_spec=pltpu.PrefetchScalarGridSpec(
            num_scalar_prefetch=1,
            grid=(parts,),
            in_specs=[
                pl.BlockSpec(route_index.shape, lambda j, core: (0, 0)),
                pl.BlockSpec(attn_values.shape, lambda j, core: (0, 0)),
                pl.BlockSpec((wide, wide), lambda j, core: (0, column(j, core))),
            ],
            out_specs=[
                pl.BlockSpec((tokens, wide), lambda j, core: (j >> 1, 0)),
                pl.BlockSpec((tokens, wide), lambda j, core: (j >> 1, 0)),
                pl.BlockSpec((1, slots + extra, wide), lambda j, core: (column(j, core), 0, 0)),
            ],
            scratch_shapes=[pltpu.VMEM((tokens + slots, wide), BF)],
        ),
        out_shape=[
            shape((parts // 2 * tokens, wide), BF),
            shape((parts // 2 * tokens, wide), BF),
            shape((parts, slots + extra, wide), BF),
        ],
        compiler_params=params(56),
        cost_estimate=cost(2 * (tokens + slots) * wide * wide * parts, 14 * MIB),
        name="teacher",
    )(core.reshape(1), route_index, attn_values, out_weight)

    routed = routed.at[:, slots:, :].set(jnp.broadcast_to(rows[None], (parts, *rows.shape)))
    routed = lax.all_to_all(routed, "tensor", 0, 0, tiled=True)

    def along(value, move):
        return lax.ppermute(value, "tensor", [(t, move(t // 8, (t // 2) % 4, t % 2)) for t in range(parts)])

    got = along(send, lambda y, x, c: y * 8 + x * 2 + 1 - c)
    block = shape((2 * tokens, wide), BF)
    sums = pl.pallas_call(
        core_sum_kernel,
        grid_spec=pltpu.PrefetchScalarGridSpec(
            num_scalar_prefetch=1,
            grid=(8,),
            in_specs=[
                pl.BlockSpec((tokens, wide), lambda g, x: ((g & 1) * 4 + ((x[0] + (g >> 1)) & 3), 0))
            ]
            * 2,
            out_specs=[
                pl.BlockSpec((tokens, wide), lambda g, x, j=j: (jnp.clip(g - 2 * j, 0, 1), 0))
                for j in range(4)
            ],
        ),
        out_shape=[block] * 4,
        compiler_params=params(16),
        cost_estimate=cost(MIB, 6 * MIB),
        name="core_sum",
    )(x_at.reshape(1), keep, got)
    others = [
        along(sums[j], lambda y, x, c, j=j: y * 8 + (x + j) % 4 * 2 + c) for j in range(1, 4)
    ]
    send, keep = pl.pallas_call(
        x_sum_kernel,
        grid_spec=pltpu.PrefetchScalarGridSpec(
            num_scalar_prefetch=1,
            grid=(2,),
            in_specs=[
                pl.BlockSpec((tokens, wide), lambda g, y: (jnp.where(g == 0, 1 - y[0], y[0]), 0))
            ]
            * 4,
            out_specs=[pl.BlockSpec((tokens, wide), lambda g, y: (0, 0))] * 2,
        ),
        out_shape=[shape((tokens, wide), BF), shape((tokens, wide), F32)],
        compiler_params=params(16),
        cost_estimate=cost(MIB, 3 * MIB),
        name="x_sum",
    )(y_at.reshape(1), sums[0], *others)
    got = along(send, lambda y, x, c: (1 - y) * 8 + x * 2 + c)
    teacher_hidden = pl.pallas_call(
        residual_kernel,
        out_shape=shape(residual_t.shape, BF),
        compiler_params=params(16),
        cost_estimate=cost(MIB, 2 * MIB),
        name="residual",
    )(residual_t, keep, got)

    packed = 2 * wide + 128 + slots // per * wide
    sent, scaled, chosen = pl.pallas_call(
        up_kernel,
        grid_spec=pltpu.PrefetchScalarGridSpec(
            num_scalar_prefetch=1,
            grid=(1,),
            in_specs=[
                vmem,
                vmem,
                vmem,
                pl.BlockSpec((1, wide), lambda i, group: (0, group[0])),
                vmem,
                vmem,
            ],
            out_specs=[vmem] * 3,
            scratch_shapes=[pltpu.VMEM((groups * slots, wide), BF)],
        ),
        out_shape=[
            shape((groups, per, packed), BF),
            shape((live, wide), BF),
            shape((live, groups * slots), BF),
        ],
        compiler_params=params(24),
        cost_estimate=cost(800 * MIB, 4 * MIB),
        name="up",
    )(group.reshape(1), route_index, routed, residual_t, norm_gain[None], w_gate, w_up)
    got = lax.all_to_all(sent, "batch", 0, 0, tiled=True)

    flat = shape((per, units), F32)
    hidden, gate, up, scale = pl.pallas_call(
        lambda *refs: hidden_kernel(features, *refs),
        out_shape=[shape((groups, per, units), BF), flat, flat, shape((per, 128), F32)],
        cost_estimate=cost(MIB, MIB),
        name="hidden",
    )(got)
    hidden = lax.all_to_all(hidden, "batch", 0, 0, tiled=True)
    target = pl.pallas_call(
        target_kernel,
        grid_spec=pltpu.PrefetchScalarGridSpec(
            num_scalar_prefetch=1,
            grid=(1,),
            in_specs=[vmem, vmem, pl.BlockSpec((wide, wide), lambda i, group: (0, group[0]))],
            out_specs=vmem,
            scratch_shapes=[pltpu.VMEM((groups * slots, wide), BF)],
        ),
        out_shape=shape((live, wide), F32),
        compiler_params=params(16),
        cost_estimate=cost(512 * MIB, 3 * MIB),
        name="target",
    )(group.reshape(1), got, chosen, projector)
    misfit = pl.pallas_call(
        down_kernel,
        out_shape=shape((parts, live // parts, wide), BF),
        compiler_params=params(16),
        cost_estimate=cost(256 * MIB, 2 * MIB),
        name="down",
    )(hidden, w_down, target)
    misfit = lax.all_to_all(misfit, "tensor", 0, 0, tiled=True)
    loss_scale = 1.0 / math.sqrt(live)
    grad_out = pl.pallas_call(
        lambda *refs: misfit_kernel(loss_scale, *refs),
        out_shape=shape(misfit.shape, BF),
        cost_estimate=cost(MIB, MIB),
        name="misfit",
    )(misfit)
    grad_out = lax.all_to_all(grad_out, "tensor", 0, 0, tiled=True)
    back = pl.pallas_call(
        back_kernel,
        out_shape=shape((groups, per, units), BF),
        compiler_params=params(16),
        cost_estimate=cost(256 * MIB, MIB),
        name="back",
    )(grad_out, w_down)
    back = lax.all_to_all(back, "batch", 0, 0, tiled=True)
    acts = pl.pallas_call(
        acts_kernel,
        out_shape=shape((groups, per, 2 * units), BF),
        cost_estimate=cost(MIB, MIB),
        name="acts",
    )(back, gate, up, scale)
    acts = lax.all_to_all(acts, "batch", 0, 0, tiled=True)
    grad_down = pl.pallas_call(
        down_weights_kernel,
        out_shape=shape((wide, units), F32),
        compiler_params=params(16),
        cost_estimate=cost(256 * MIB, 2 * MIB),
        name="down_weights",
    )(grad_out, hidden)
    grad_gate, grad_up = pl.pallas_call(
        weights_kernel,
        out_shape=[shape((wide, units), F32)] * 2,
        compiler_params=params(16),
        cost_estimate=cost(512 * MIB, 4 * MIB),
        name="weights",
    )(scaled, acts)
    return teacher_hidden, grad_gate, grad_up, grad_down


def solution(mesh):
    in_specs = (
        P("batch", "tensor"),
        P("tensor", None),
        P("tensor", "batch"),
        P("tensor", None),
        P("batch", "tensor"),
        P(),
        P("batch", "tensor"),
        P("batch", "tensor"),
        P("batch", "tensor"),
        P("batch", None),
    )
    out_specs = (P("tensor", "batch"),) + (P("batch", "tensor"),) * 3
    return jax.shard_map(
        on_device, mesh=mesh, in_specs=in_specs, out_specs=out_specs, check_vma=False
    )
```

```python
import math

import jax
import jax.numpy as jnp
from jax import lax
from jax.experimental import pallas as pl
from jax.experimental.pallas import tpu as pltpu
from jax.sharding import PartitionSpec as P

EPS = 1e-05
BF = jnp.bfloat16
F32 = jnp.float32
MIB = 1 << 20


def params(mib):
    return pltpu.CompilerParams(vmem_limit_bytes=mib * MIB)


def cost(flops, nbytes):
    return pl.CostEstimate(flops=flops, bytes_accessed=nbytes, transcendentals=0)


def dot(a, b, ca=1, cb=0):
    return lax.dot_general(a, b, (((ca,), (cb,)), ((), ())), preferred_element_type=F32)


def whole(shape):
    return pl.BlockSpec(shape, lambda *_: (0,) * len(shape))


def slot_rows(route, tokens):
    slots = route.shape[1]
    grid = (slots, slots)
    diagonal = lax.broadcasted_iota(jnp.int32, grid, 0) == lax.broadcasted_iota(jnp.int32, grid, 1)
    spread = jnp.broadcast_to(route.astype(F32), grid)
    column = jnp.sum(jnp.where(diagonal, spread, 0.0), axis=1, keepdims=True)
    lane = lax.broadcasted_iota(jnp.int32, (slots, tokens), 1).astype(F32)
    return jnp.where(lane == column, 1.0, 0.0).astype(BF)


def rows_kernel(route_ref, x_ref, out_ref):
    route = route_ref[...]
    slots, wide = route.shape[1], x_ref.shape[1]
    rows = dot(slot_rows(route, x_ref.shape[0]), x_ref[...]).astype(BF)
    half = slots // 2
    out_ref[0:half, 0:wide] = rows[0:half]
    out_ref[0:half, wide : 2 * wide] = rows[half:]
    live = jnp.sum(jnp.where(route >= 0, 1.0, 0.0), axis=1, keepdims=True)
    out_ref[half : half + 8, :] = jnp.broadcast_to(live, (8, 2 * wide)).astype(BF)


def teacher_kernel(
    core_ref, route_ref, attn_ref, mine_ref, other_ref, keep_ref, send_ref, routed_ref, left_ref
):
    tokens = attn_ref.shape[0]
    slots = route_ref.shape[1]

    @pl.when(pl.program_id(0) == 0)
    def _():
        left_ref[0:tokens, :] = attn_ref[...]
        left_ref[tokens:, :] = dot(slot_rows(route_ref[...], tokens), attn_ref[...]).astype(BF)

    core = core_ref[0]
    for weight_ref, out_ref, place in ((other_ref, send_ref, 1 - core), (mine_ref, keep_ref, core)):
        product = dot(left_ref[...], weight_ref[...]).astype(BF)
        out_ref[0] = product[0:tokens]
        routed_ref[place, 0:slots, :] = product[tokens:]


def pack_kernel(rows_ref, routed_ref, send_ref, out_ref, same_ref, sems):
    first = routed_ref.shape[1] - rows_ref.shape[0]
    copies = [
        pltpu.make_async_copy(
            rows_ref, out_ref.at[s, first : routed_ref.shape[1], :], sems.at[s]
        )
        for s in range(routed_ref.shape[0])
    ]
    for copy in copies:
        copy.start()
    for copy in copies:
        copy.wait()


def core_sum_kernel(x_ref, *refs):
    ways = len(refs) // 3
    for j in range(ways):
        total = refs[j][...].astype(F32) + refs[ways + j][...].astype(F32)
        refs[2 * ways + j][...] = total.astype(BF).reshape(refs[2 * ways + j].shape)


def x_sum_kernel(y_ref, *refs):
    ways = len(refs) // 2 - 1
    for i, out_ref in enumerate(refs[-2:]):
        total = refs[i * ways][...].astype(F32)
        for ref in refs[i * ways + 1 : (i + 1) * ways]:
            total = total + ref[...].astype(F32)
        out_ref[...] = total.astype(out_ref.dtype)


def residual_kernel(residual_ref, keep_ref, got_ref, out_ref):
    summed = keep_ref[0] + got_ref[0].astype(F32)
    out_ref[...] = (residual_ref[...].astype(F32) + summed.T).astype(BF)


def up_kernel(
    group_ref, route_ref, got_ref, residual_ref, gain_ref, gate_ref, up_ref, s1, s2, s3,
    out_ref, rows_ref, chosen_ref, t1, t2, t3, padded_ref, weights_ref, sems,
):
    loads = [
        pltpu.make_async_copy(ref, weights_ref.at[i], sems.at[i])
        for i, ref in enumerate((gate_ref, up_ref))
    ]
    for load in loads:
        load.start()
    slots = route_ref.shape[1]
    sources, _, wide = got_ref.shape
    groups = sources // 2
    half, side = slots // 2, wide // 2
    per = out_ref.shape[1]
    total = groups * per

    routed = dot(slot_rows(route_ref[...], residual_ref.shape[1]), residual_ref[...], 1, 1)
    for s in range(sources):
        routed = routed + got_ref[s, 0:slots, :].astype(F32)
        g, d = s // 2, s % 2
        block = got_ref[s, slots : slots + half, :]
        padded_ref[g * slots : g * slots + half, d * side : (d + 1) * side] = block[:, 0:side]
        padded_ref[g * slots + half : (g + 1) * slots, d * side : (d + 1) * side] = block[:, side:]
    routed = routed.astype(BF)
    at = slots + half
    counts = [got_ref[2 * g, at : at + 8, 0 : 2 * slots].astype(F32)[0:1] for g in range(groups)]

    row = lax.broadcasted_iota(jnp.int32, (total, 2 * slots), 0)
    lane = lax.broadcasted_iota(jnp.int32, (total, 2 * slots), 1)
    second = lane >= slots
    slot = jnp.where(second, lane - slots, lane)
    slot_f = slot.astype(F32)
    shift = (row - slot).astype(F32)
    x = jnp.zeros((total, wide), F32)
    run = jnp.zeros_like(counts[0])
    for q in range(groups // 2):
        one, two = counts[2 * q], counts[2 * q + 1]
        start = jnp.where(second, run + one, run)
        count = jnp.where(second, two, one)
        run = run + one + two
        chosen = jnp.where((shift == start) & (slot_f < count), 1.0, 0.0).astype(BF)
        chosen_ref[:, 2 * q * slots : 2 * (q + 1) * slots] = chosen
        x = x + dot(chosen, padded_ref[2 * q * slots : 2 * (q + 1) * slots, :])

    square = jnp.sum(x * x, axis=1, keepdims=True)
    high = square.astype(BF)
    low = (square - high.astype(F32)).astype(BF)
    lane128 = lax.broadcasted_iota(jnp.int32, (total, 128), 1)
    squares = jnp.where(lane128 < 64, high.astype(F32), low.astype(F32)).astype(BF)
    scaled = (x * gain_ref[...]).astype(BF)
    rows_ref[...] = scaled
    for load in loads:
        load.wait()
    gate = dot(scaled, weights_ref[0]).astype(BF)
    up = dot(scaled, weights_ref[1]).astype(BF)
    at = 2 * wide + 128
    for g in range(groups):
        own = slice(g * per, (g + 1) * per)
        out_ref[g, :, 0:wide] = gate[own]
        out_ref[g, :, wide : 2 * wide] = up[own]
        out_ref[g, :, 2 * wide : at] = squares[own]
        for h in range(slots // per):
            out_ref[g, :, at + h * wide : at + (h + 1) * wide] = routed[h * per : (h + 1) * per]


def hidden_kernel(features, got_ref, out_ref, gate_ref, up_ref, scale_ref):
    wide = gate_ref.shape[1]
    at = 2 * wide + 128
    total = got_ref[0, :, 0:at].astype(F32)
    for g in range(1, got_ref.shape[0]):
        total = total + got_ref[g, :, 0:at].astype(F32)
    square = total[:, 2 * wide : 2 * wide + 1] + total[:, 2 * wide + 64 : 2 * wide + 65]
    scale = lax.rsqrt(square * (1.0 / features) + EPS)
    gate = total[:, 0:wide] * scale
    up = total[:, wide : 2 * wide] * scale
    gate_ref[...] = gate
    up_ref[...] = up
    scale_ref[...] = jnp.broadcast_to(scale, scale_ref.shape)
    hidden = (gate * jax.nn.sigmoid(gate) * up).astype(BF)
    for g in range(out_ref.shape[0]):
        out_ref[g] = hidden


def target_kernel(group_ref, got_ref, chosen_ref, projector_ref, out_ref, rows_ref):
    groups, per, _ = got_ref.shape
    wide = rows_ref.shape[1]
    parts = rows_ref.shape[0] // (groups * per)
    at = got_ref.shape[2] - parts * wide
    for g in range(groups):
        for h in range(parts):
            first = (g * parts + h) * per
            rows_ref[first : first + per, :] = got_ref[g, :, at + h * wide : at + (h + 1) * wide]
    rows = dot(chosen_ref[...], rows_ref[...]).astype(BF)
    out_ref[...] = dot(rows, projector_ref[...])


def down_kernel(got_ref, down_ref, target_ref, passed_ref, out_ref, same_ref):
    rows, wide = target_ref.shape
    part = dot(got_ref[...].reshape(rows, wide), down_ref[...], 1, 1) - target_ref[...]
    out_ref[...] = part.astype(BF).reshape(out_ref.shape)


def misfit_kernel(scale, got_ref, out_ref):
    total = got_ref[0].astype(F32)
    for s in range(1, got_ref.shape[0]):
        total = total + got_ref[s].astype(F32)
    grad = (total * scale).astype(BF)
    for s in range(out_ref.shape[0]):
        out_ref[s] = grad


def back_kernel(got_ref, down_ref, passed_ref, out_ref, same_ref):
    groups, per, wide = out_ref.shape
    part = dot(got_ref[...].reshape(groups * per, got_ref.shape[2]), down_ref[...])
    out_ref[...] = part.astype(BF).reshape(groups, per, wide)


def acts_kernel(got_ref, gate_ref, up_ref, scale_ref, out_ref):
    wide = gate_ref.shape[1]
    grad = got_ref[0].astype(F32)
    for g in range(1, got_ref.shape[0]):
        grad = grad + got_ref[g].astype(F32)
    grad = grad * scale_ref[:, 0:1]
    gate, up = gate_ref[...], up_ref[...]
    sigma = jax.nn.sigmoid(gate)
    grad_gate = (grad * up * sigma * (1.0 + gate * (1.0 - sigma))).astype(BF)
    grad_up = (grad * gate * sigma).astype(BF)
    for g in range(out_ref.shape[0]):
        out_ref[g, :, 0:wide] = grad_gate
        out_ref[g, :, wide : 2 * wide] = grad_up


def down_weights_kernel(grad_ref, hidden_ref, out_ref):
    rows = hidden_ref.shape[0] * hidden_ref.shape[1]
    wide = out_ref.shape[0]
    out_ref[...] = dot(grad_ref[...].reshape(rows, wide), hidden_ref[...].reshape(rows, -1), 0, 0)


def weights_kernel(rows_ref, got_ref, gate_ref, up_ref):
    wide = gate_ref.shape[1]
    acts = got_ref[...].reshape(got_ref.shape[0] * got_ref.shape[1], 2 * wide)
    gate_ref[...] = dot(rows_ref[...], acts[:, 0:wide], 0, 0)
    up_ref[...] = dot(rows_ref[...], acts[:, wide:], 0, 0)


def on_device(
    attn_values,
    out_weight,
    residual_t,
    projector,
    student_input,
    norm_gain,
    w_gate,
    w_up,
    w_down,
    route_index,
):
    groups, parts = lax.axis_size("batch"), lax.axis_size("tensor")
    slots = route_index.shape[1]
    tokens, wide = attn_values.shape
    side = student_input.shape[1]
    features = norm_gain.shape[0]
    live = tokens * groups // 8
    per = live // groups
    units = w_gate.shape[1]
    extra = slots // 2 + 8
    group, part = lax.axis_index("batch"), lax.axis_index("tensor")
    core, x_at, y_at = part & 1, (part >> 1) & 3, part >> 3
    shape = jax.ShapeDtypeStruct
    vmem = pl.BlockSpec(memory_space=pltpu.VMEM)
    anywhere = pl.BlockSpec(memory_space=pl.ANY)
    w_gate, w_up, w_down, projector = (
        pltpu.with_memory_space_constraint(w, pltpu.HBM) for w in (w_gate, w_up, w_down, projector)
    )

    rows = pl.pallas_call(
        rows_kernel,
        out_shape=pltpu.HBM((extra, 2 * side), BF),
        cost_estimate=cost(2 * slots * tokens * side, MIB // 4),
        compiler_params=params(4),
        name="rows",
    )(route_index, student_input)
    pairs = [
        (b * parts + t, (t // 2) * parts + 2 * b + t % 2)
        for b in range(groups)
        for t in range(parts)
    ]
    rows = lax.ppermute(rows, ("batch", "tensor"), pairs)

    keep, send, routed = pl.pallas_call(
        teacher_kernel,
        grid_spec=pltpu.PrefetchScalarGridSpec(
            num_scalar_prefetch=1,
            grid=(parts // 2,),
            in_specs=[
                pl.BlockSpec(route_index.shape, lambda j, core: (0, 0)),
                pl.BlockSpec(attn_values.shape, lambda j, core: (0, 0)),
                pl.BlockSpec((wide, wide), lambda j, core: (0, 2 * j + core[0])),
                pl.BlockSpec((wide, wide), lambda j, core: (0, 2 * j + 1 - core[0])),
            ],
            out_specs=[
                pl.BlockSpec((1, tokens, wide), lambda j, core: (j, 0, 0)),
                pl.BlockSpec((1, tokens, wide), lambda j, core: (j, 0, 0)),
                pl.BlockSpec((2, slots + extra, wide), lambda j, core: (j, 0, 0)),
            ],
            scratch_shapes=[pltpu.VMEM((tokens + slots, wide), BF)],
        ),
        out_shape=[
            shape((parts // 2, tokens, wide), BF),
            shape((parts // 2, tokens, wide), BF),
            shape((parts, slots + extra, wide), BF),
        ],
        compiler_params=params(56),
        cost_estimate=cost(2 * (tokens + slots) * wide * wide * parts, 14 * MIB),
        name="teacher",
    )(core.reshape(1), route_index, attn_values, out_weight, out_weight)

    routed, send = pl.pallas_call(
        pack_kernel,
        in_specs=[vmem, anywhere, anywhere],
        out_specs=[anywhere] * 2,
        out_shape=[pltpu.HBM(routed.shape, BF), pltpu.HBM(send.shape, BF)],
        scratch_shapes=[pltpu.SemaphoreType.DMA((parts,))],
        input_output_aliases={1: 0, 2: 1},
        compiler_params=params(4),
        cost_estimate=cost(0, MIB),
        name="pack",
    )(rows, routed, send)
    routed = lax.all_to_all(routed, "tensor", 0, 0, tiled=True)

    def along(value, move):
        return lax.ppermute(value, "tensor", [(t, move(t // 8, (t // 2) % 4, t % 2)) for t in range(parts)])

    got = along(send, lambda y, x, c: y * 8 + x * 2 + 1 - c)
    strip = tokens // 2
    sums = pl.pallas_call(
        core_sum_kernel,
        grid_spec=pltpu.PrefetchScalarGridSpec(
            num_scalar_prefetch=1,
            grid=(2, tokens // strip),
            in_specs=[
                pl.BlockSpec((1, strip, wide), lambda y, i, x, j=j: (4 * y + ((x[0] + j) & 3), i, 0))
                for j in range(4)
            ]
            * 2,
            out_specs=[pl.BlockSpec((1, strip, wide), lambda y, i, x: (y, i, 0))] * 4,
        ),
        out_shape=[pltpu.HBM((2, tokens, wide), BF)] * 4,
        compiler_params=params(16),
        cost_estimate=cost(MIB, 6 * MIB),
        name="core_sum",
    )(x_at.reshape(1), *[keep] * 4, *[got] * 4)

    packed = 2 * wide + 128 + slots // per * wide
    sent, scaled, chosen, *moved = pl.pallas_call(
        up_kernel,
        grid_spec=pltpu.PrefetchScalarGridSpec(
            num_scalar_prefetch=1,
            grid=(1,),
            in_specs=[
                vmem,
                vmem,
                vmem,
                pl.BlockSpec((1, wide), lambda i, group: (0, group[0])),
            ]
            + [anywhere] * 5,
            out_specs=[vmem] * 3 + [anywhere] * 3,
            scratch_shapes=[
                pltpu.VMEM((groups * slots, wide), BF),
                pltpu.VMEM((2, wide, units), BF),
                pltpu.SemaphoreType.DMA((2,)),
            ],
        ),
        out_shape=[
            pltpu.HBM((groups, per, packed), BF),
            pltpu.HBM((live, wide), BF),
            pltpu.HBM((live, groups * slots), BF),
        ]
        + [pltpu.HBM((2, tokens, wide), BF)] * 3,
        input_output_aliases={7: 3, 8: 4, 9: 5},
        compiler_params=params(16),
        cost_estimate=cost(800 * MIB, 4 * MIB),
        name="up",
    )(group.reshape(1), route_index, routed, residual_t, norm_gain[None], w_gate, w_up, *sums[1:])
    others = [
        along(moved[j - 1], lambda y, x, c, j=j: y * 8 + (x + j) % 4 * 2 + c) for j in range(1, 4)
    ]
    send, keep = pl.pallas_call(
        x_sum_kernel,
        grid_spec=pltpu.PrefetchScalarGridSpec(
            num_scalar_prefetch=1,
            grid=(tokens // strip,),
            in_specs=[pl.BlockSpec((1, strip, wide), lambda i, y: (1 - y[0], i, 0))] * 4
            + [pl.BlockSpec((1, strip, wide), lambda i, y: (y[0], i, 0))] * 4,
            out_specs=[pl.BlockSpec((1, strip, wide), lambda i, y: (0, i, 0))] * 2,
        ),
        out_shape=[pltpu.HBM((1, tokens, wide), BF), pltpu.HBM((1, tokens, wide), F32)],
        compiler_params=params(16),
        cost_estimate=cost(MIB, 3 * MIB),
        name="x_sum",
    )(y_at.reshape(1), *[sums[0], *others] * 2)

    got = lax.all_to_all(sent, "batch", 0, 0, tiled=True)

    flat = shape((per, units), F32)
    hidden, gate, up, scale = pl.pallas_call(
        lambda *refs: hidden_kernel(features, *refs),
        out_shape=[pltpu.HBM((groups, per, units), BF), flat, flat, shape((per, 128), F32)],
        cost_estimate=cost(MIB, MIB),
        compiler_params=params(8),
        name="hidden",
    )(got)
    hidden = lax.all_to_all(hidden, "batch", 0, 0, tiled=True)
    target = pl.pallas_call(
        target_kernel,
        grid_spec=pltpu.PrefetchScalarGridSpec(
            num_scalar_prefetch=1,
            grid=(1,),
            in_specs=[vmem, vmem, pl.BlockSpec((wide, wide), lambda i, group: (0, group[0]))],
            out_specs=vmem,
            scratch_shapes=[pltpu.VMEM((groups * slots, wide), BF)],
        ),
        out_shape=shape((live, wide), F32),
        compiler_params=params(16),
        cost_estimate=cost(512 * MIB, 3 * MIB),
        name="target",
    )(group.reshape(1), got, chosen, projector)
    misfit, send = pl.pallas_call(
        down_kernel,
        in_specs=[vmem] * 3 + [anywhere],
        out_specs=[vmem, anywhere],
        out_shape=[shape((parts, live // parts, wide), BF), pltpu.HBM(send.shape, BF)],
        input_output_aliases={3: 1},
        compiler_params=params(16),
        cost_estimate=cost(256 * MIB, 2 * MIB),
        name="down",
    )(hidden, w_down, target, send)
    got = along(send, lambda y, x, c: (1 - y) * 8 + x * 2 + c)
    teacher_hidden = pl.pallas_call(
        residual_kernel,
        out_shape=shape(residual_t.shape, BF),
        compiler_params=params(16),
        cost_estimate=cost(MIB, 2 * MIB),
        name="residual",
    )(residual_t, keep, got)
    misfit = lax.all_to_all(misfit, "tensor", 0, 0, tiled=True)
    loss_scale = 1.0 / math.sqrt(live)
    grad_out = pl.pallas_call(
        lambda *refs: misfit_kernel(loss_scale, *refs),
        out_shape=shape(misfit.shape, BF),
        cost_estimate=cost(MIB, MIB),
        compiler_params=params(8),
        name="misfit",
    )(misfit)
    grad_out = lax.all_to_all(grad_out, "tensor", 0, 0, tiled=True)
    back, teacher_hidden = pl.pallas_call(
        back_kernel,
        in_specs=[vmem] * 2 + [anywhere],
        out_specs=[vmem, anywhere],
        out_shape=[shape((groups, per, units), BF), shape(residual_t.shape, BF)],
        input_output_aliases={2: 1},
        compiler_params=params(16),
        cost_estimate=cost(256 * MIB, MIB),
        name="back",
    )(grad_out, w_down, teacher_hidden)
    back = lax.all_to_all(back, "batch", 0, 0, tiled=True)
    acts = pl.pallas_call(
        acts_kernel,
        out_shape=shape((groups, per, 2 * units), BF),
        cost_estimate=cost(MIB, MIB),
        compiler_params=params(8),
        name="acts",
    )(back, gate, up, scale)
    acts = lax.all_to_all(acts, "batch", 0, 0, tiled=True)
    grad_down = pl.pallas_call(
        down_weights_kernel,
        out_shape=shape((wide, units), F32),
        compiler_params=params(16),
        cost_estimate=cost(256 * MIB, 2 * MIB),
        name="down_weights",
    )(grad_out, hidden)
    grad_gate, grad_up = pl.pallas_call(
        weights_kernel,
        out_shape=[shape((wide, units), F32)] * 2,
        compiler_params=params(16),
        cost_estimate=cost(512 * MIB, 4 * MIB),
        name="weights",
    )(scaled, acts)
    return teacher_hidden, grad_gate, grad_up, grad_down


def solution(mesh):
    in_specs = (
        P("batch", "tensor"),
        P("tensor", None),
        P("tensor", "batch"),
        P("tensor", None),
        P("batch", "tensor"),
        P(),
        P("batch", "tensor"),
        P("batch", "tensor"),
        P("batch", "tensor"),
        P("batch", None),
    )
    out_specs = (P("tensor", "batch"),) + (P("batch", "tensor"),) * 3
    return jax.shard_map(
        on_device, mesh=mesh, in_specs=in_specs, out_specs=out_specs, check_vma=False
    )
```

```python
import math

import jax
import jax.numpy as jnp
from jax import lax
from jax.experimental import pallas as pl
from jax.experimental.pallas import tpu as pltpu
from jax.sharding import PartitionSpec as P

EPS = 1e-05
BF = jnp.bfloat16
F32 = jnp.float32
MIB = 1 << 20


def params(mib):
    return pltpu.CompilerParams(vmem_limit_bytes=mib * MIB)


def cost(flops, nbytes):
    return pl.CostEstimate(flops=flops // 1024, bytes_accessed=nbytes // 1024, transcendentals=0)


def dot(a, b, ca=1, cb=0):
    return lax.dot_general(a, b, (((ca,), (cb,)), ((), ())), preferred_element_type=F32)


def whole(shape):
    return pl.BlockSpec(shape, lambda *_: (0,) * len(shape))


def slot_rows(route, tokens):
    slots = route.shape[1]
    grid = (slots, slots)
    diagonal = lax.broadcasted_iota(jnp.int32, grid, 0) == lax.broadcasted_iota(jnp.int32, grid, 1)
    spread = jnp.broadcast_to(route.astype(F32), grid)
    column = jnp.sum(jnp.where(diagonal, spread, 0.0), axis=1, keepdims=True)
    lane = lax.broadcasted_iota(jnp.int32, (slots, tokens), 1).astype(F32)
    return jnp.where(lane == column, 1.0, 0.0).astype(BF)


def rows_kernel(route_ref, x_ref, out_ref):
    route = route_ref[...]
    slots, wide = route.shape[1], x_ref.shape[1]
    rows = dot(slot_rows(route, x_ref.shape[0]), x_ref[...]).astype(BF)
    half = slots // 2
    out_ref[0:half, 0:wide] = rows[0:half]
    out_ref[0:half, wide : 2 * wide] = rows[half:]
    live = jnp.sum(jnp.where(route >= 0, 1.0, 0.0), axis=1, keepdims=True)
    out_ref[half : half + 8, :] = jnp.broadcast_to(live, (8, 2 * wide)).astype(BF)


def teacher_kernel(
    core_ref, route_ref, attn_ref, mine_ref, other_ref, after_ref,
    keep_ref, send_ref, keep_routed_ref, send_routed_ref, left_ref,
):
    tokens = attn_ref.shape[0]

    @pl.when(pl.program_id(0) == 0)
    def _():
        left_ref[0:tokens, :] = attn_ref[...]
        left_ref[tokens:, :] = dot(slot_rows(route_ref[...], tokens), attn_ref[...]).astype(BF)

    for weight_ref, out_ref, routed_ref in (
        (other_ref, send_ref, send_routed_ref),
        (mine_ref, keep_ref, keep_routed_ref),
    ):
        product = dot(left_ref[...], weight_ref[...]).astype(BF)
        out_ref[0] = product[0:tokens]
        routed_ref[0] = product[tokens:]


def copies_kernel(rows_ref, out_ref, sems):
    copies = [
        pltpu.make_async_copy(rows_ref, out_ref.at[s], sems.at[s]) for s in range(out_ref.shape[0])
    ]
    for copy in copies:
        copy.start()
    for copy in copies:
        copy.wait()


def core_sum_kernel(x_ref, *refs):
    ways = len(refs) // 3
    for j in range(ways):
        total = refs[j][...].astype(F32) + refs[ways + j][...].astype(F32)
        refs[2 * ways + j][...] = total.astype(BF).reshape(refs[2 * ways + j].shape)


def x_sum_kernel(y_ref, *refs):
    ways = len(refs) // 2 - 1
    for i, out_ref in enumerate(refs[-2:]):
        total = refs[i * ways][...].astype(F32)
        for ref in refs[i * ways + 1 : (i + 1) * ways]:
            total = total + ref[...].astype(F32)
        out_ref[...] = total.astype(out_ref.dtype)


def routed_sum_kernel(y_ref, route_ref, residual_ref, *refs):
    x_sum_kernel(y_ref, *refs)
    hot = slot_rows(route_ref[...], residual_ref.shape[1])
    refs[-1][0] = refs[-1][0] + dot(hot, residual_ref[...], 1, 1)


def residual_kernel(residual_ref, keep_ref, got_ref, out_ref):
    summed = keep_ref[0] + got_ref[0].astype(F32)
    out_ref[...] = (residual_ref[...].astype(F32) + summed.T).astype(BF)


def up_kernel(
    group_ref, got_ref, gain_ref, gate_ref, up_ref, after_ref, passed_ref,
    out_ref, rows_ref, chosen_ref, same_ref, padded_ref, weights_ref, sems,
):
    loads = [
        pltpu.make_async_copy(ref, weights_ref.at[i], sems.at[i])
        for i, ref in enumerate((gate_ref, up_ref))
    ]
    for load in loads:
        load.start()
    sources, height, wide = got_ref.shape
    groups = sources // 2
    half, side = height - 8, wide // 2
    slots = 2 * half
    per = out_ref.shape[1]
    total = groups * per

    for s in range(sources):
        g, d = s // 2, s % 2
        block = got_ref[s, 0:half, :]
        padded_ref[g * slots : g * slots + half, d * side : (d + 1) * side] = block[:, 0:side]
        padded_ref[g * slots + half : (g + 1) * slots, d * side : (d + 1) * side] = block[:, side:]
    at = half
    counts = [got_ref[2 * g, at : at + 8, 0 : 2 * slots].astype(F32)[0:1] for g in range(groups)]

    row = lax.broadcasted_iota(jnp.int32, (total, 2 * slots), 0)
    lane = lax.broadcasted_iota(jnp.int32, (total, 2 * slots), 1)
    second = lane >= slots
    slot = jnp.where(second, lane - slots, lane)
    slot_f = slot.astype(F32)
    shift = (row - slot).astype(F32)
    x = jnp.zeros((total, wide), F32)
    run = jnp.zeros_like(counts[0])
    for q in range(groups // 2):
        one, two = counts[2 * q], counts[2 * q + 1]
        start = jnp.where(second, run + one, run)
        count = jnp.where(second, two, one)
        run = run + one + two
        chosen = jnp.where((shift == start) & (slot_f < count), 1.0, 0.0).astype(BF)
        chosen_ref[:, 2 * q * slots : 2 * (q + 1) * slots] = chosen
        x = x + dot(chosen, padded_ref[2 * q * slots : 2 * (q + 1) * slots, :])

    square = jnp.sum(x * x, axis=1, keepdims=True)
    high = square.astype(BF)
    low = (square - high.astype(F32)).astype(BF)
    lane128 = lax.broadcasted_iota(jnp.int32, (total, 128), 1)
    squares = jnp.where(lane128 < 64, high.astype(F32), low.astype(F32)).astype(BF)
    scaled = (x * gain_ref[...]).astype(BF)
    rows_ref[...] = scaled
    for load in loads:
        load.wait()
    gate = dot(scaled, weights_ref[0]).astype(BF)
    up = dot(scaled, weights_ref[1]).astype(BF)
    at = 2 * wide + 128
    for g in range(groups):
        own = slice(g * per, (g + 1) * per)
        out_ref[g, :, 0:wide] = gate[own]
        out_ref[g, :, wide : 2 * wide] = up[own]
        out_ref[g, :, 2 * wide : at] = squares[own]


def hidden_kernel(
    features, got_ref, keep_ref, other_ref, s1, s2, s3,
    out_ref, gate_ref, up_ref, scale_ref, t1, t2, t3,
):
    per, wide = gate_ref.shape
    at = got_ref.shape[2]
    total = got_ref[0, :, 0:at].astype(F32)
    for g in range(1, got_ref.shape[0]):
        total = total + got_ref[g, :, 0:at].astype(F32)
    square = total[:, 2 * wide : 2 * wide + 1] + total[:, 2 * wide + 64 : 2 * wide + 65]
    scale = lax.rsqrt(square * (1.0 / features) + EPS)
    gate = total[:, 0:wide] * scale
    up = total[:, wide : 2 * wide] * scale
    gate_ref[...] = gate
    up_ref[...] = up
    scale_ref[...] = jnp.broadcast_to(scale, scale_ref.shape)
    hidden = (gate * jax.nn.sigmoid(gate) * up).astype(BF)
    routed = (keep_ref[0] + other_ref[0].astype(F32)).astype(BF)
    for g in range(out_ref.shape[0]):
        out_ref[g, 0:per, :] = hidden
        out_ref[g, per:, :] = routed


def down_kernel(
    group_ref, got_ref, down_ref, chosen_ref, projector_ref, out_ref, hidden_ref, rows_ref
):
    groups = got_ref.shape[0]
    per = hidden_ref.shape[0] // groups
    slots = got_ref.shape[1] - per
    for g in range(groups):
        hidden_ref[g * per : (g + 1) * per, :] = got_ref[g, 0:per, :]
        rows_ref[g * slots : (g + 1) * slots, :] = got_ref[g, per:, :]
    rows = dot(chosen_ref[...], rows_ref[...]).astype(BF)
    part = dot(hidden_ref[...], down_ref[...], 1, 1) - dot(rows, projector_ref[...])
    out_ref[...] = part.astype(BF).reshape(out_ref.shape)


def misfit_kernel(scale, got_ref, passed_ref, out_ref, same_ref):
    total = got_ref[0].astype(F32)
    for s in range(1, got_ref.shape[0]):
        total = total + got_ref[s].astype(F32)
    grad = (total * scale).astype(BF)
    for s in range(out_ref.shape[0]):
        out_ref[s] = grad


def back_kernel(got_ref, down_ref, out_ref):
    groups, per, wide = out_ref.shape
    part = dot(got_ref[...].reshape(groups * per, got_ref.shape[2]), down_ref[...])
    out_ref[...] = part.astype(BF).reshape(groups, per, wide)


def acts_kernel(got_ref, gate_ref, up_ref, scale_ref, out_ref):
    wide = gate_ref.shape[1]
    grad = got_ref[0].astype(F32)
    for g in range(1, got_ref.shape[0]):
        grad = grad + got_ref[g].astype(F32)
    grad = grad * scale_ref[:, 0:1]
    gate, up = gate_ref[...], up_ref[...]
    sigma = jax.nn.sigmoid(gate)
    grad_gate = (grad * up * sigma * (1.0 + gate * (1.0 - sigma))).astype(BF)
    grad_up = (grad * gate * sigma).astype(BF)
    for g in range(out_ref.shape[0]):
        out_ref[g, :, 0:wide] = grad_gate
        out_ref[g, :, wide : 2 * wide] = grad_up


def down_weights_kernel(grad_ref, hidden_ref, out_ref):
    rows, units = hidden_ref.shape
    out_ref[...] = dot(grad_ref[...].reshape(rows, out_ref.shape[0]), hidden_ref[...], 0, 0)


def weights_kernel(rows_ref, got_ref, gate_ref, up_ref):
    wide = gate_ref.shape[1]
    acts = got_ref[...].reshape(got_ref.shape[0] * got_ref.shape[1], 2 * wide)
    gate_ref[...] = dot(rows_ref[...], acts[:, 0:wide], 0, 0)
    up_ref[...] = dot(rows_ref[...], acts[:, wide:], 0, 0)


def on_device(
    attn_values,
    out_weight,
    residual_t,
    projector,
    student_input,
    norm_gain,
    w_gate,
    w_up,
    w_down,
    route_index,
):
    groups, parts = lax.axis_size("batch"), lax.axis_size("tensor")
    slots = route_index.shape[1]
    tokens, wide = attn_values.shape
    side = student_input.shape[1]
    features = norm_gain.shape[0]
    live = tokens * groups // 8
    per = live // groups
    units = w_gate.shape[1]
    extra = slots // 2 + 8
    group, part = lax.axis_index("batch"), lax.axis_index("tensor")
    core, x_at, y_at = part & 1, (part >> 1) & 3, part >> 3
    shape = jax.ShapeDtypeStruct
    vmem = pl.BlockSpec(memory_space=pltpu.VMEM)
    anywhere = pl.BlockSpec(memory_space=pl.ANY)
    out_weight, w_gate, w_up, w_down, projector = (
        pltpu.with_memory_space_constraint(w, pltpu.HBM)
        for w in (out_weight, w_gate, w_up, w_down, projector)
    )

    rows = pl.pallas_call(
        rows_kernel,
        out_shape=pltpu.HBM((extra, 2 * side), BF),
        cost_estimate=cost(2 * slots * tokens * side, MIB // 4),
        compiler_params=params(4),
        name="rows",
    )(route_index, student_input)
    pairs = [
        (b * parts + t, (t // 2) * parts + 2 * b + t % 2)
        for b in range(groups)
        for t in range(parts)
    ]
    rows = lax.ppermute(rows, ("batch", "tensor"), pairs)

    copies = pl.pallas_call(
        copies_kernel,
        in_specs=[vmem],
        out_specs=anywhere,
        out_shape=pltpu.HBM((parts, *rows.shape), BF),
        scratch_shapes=[pltpu.SemaphoreType.DMA((parts,))],
        compiler_params=params(4),
        cost_estimate=cost(0, MIB // 2),
        name="copies",
    )(rows)
    every = lax.all_to_all(copies, "tensor", 0, 0, tiled=True)

    keep, send, keep_routed, send_routed = pl.pallas_call(
        teacher_kernel,
        grid_spec=pltpu.PrefetchScalarGridSpec(
            num_scalar_prefetch=1,
            grid=(parts // 2,),
            in_specs=[
                pl.BlockSpec(route_index.shape, lambda j, core: (0, 0)),
                pl.BlockSpec(attn_values.shape, lambda j, core: (0, 0)),
                pl.BlockSpec((wide, wide), lambda j, core: (0, 2 * j + core[0])),
                pl.BlockSpec((wide, wide), lambda j, core: (0, 2 * j + 1 - core[0])),
                anywhere,
            ],
            out_specs=[pl.BlockSpec((1, tokens, wide), lambda j, core: (j, 0, 0))] * 2
            + [pl.BlockSpec((1, slots, wide), lambda j, core: (j, 0, 0))] * 2,
            scratch_shapes=[pltpu.VMEM((tokens + slots, wide), BF)],
        ),
        out_shape=[pltpu.HBM((parts // 2, tokens, wide), BF)] * 2
        + [pltpu.HBM((parts // 2, slots, wide), BF)] * 2,
        compiler_params=params(16),
        cost_estimate=cost(2 * (tokens + slots) * wide * wide * parts, 14 * MIB),
        name="teacher",
    )(core.reshape(1), route_index, attn_values, out_weight, out_weight, copies)

    def along(value, move):
        return lax.ppermute(value, "tensor", [(t, move(t // 8, (t // 2) % 4, t % 2)) for t in range(parts)])

    def core_sum(keep, send, strip):
        got = along(send, lambda y, x, c: y * 8 + x * 2 + 1 - c)
        height = keep.shape[1]
        block = (1, strip, wide)
        return pl.pallas_call(
            core_sum_kernel,
            grid_spec=pltpu.PrefetchScalarGridSpec(
                num_scalar_prefetch=1,
                grid=(2, height // strip),
                in_specs=[
                    pl.BlockSpec(block, lambda y, i, x, j=j: (4 * y + ((x[0] + j) & 3), i, 0))
                    for j in range(4)
                ]
                * 2,
                out_specs=[pl.BlockSpec(block, lambda y, i, x: (y, i, 0))] * 4,
            ),
            out_shape=[pltpu.HBM((2, height, wide), BF)] * 4,
            compiler_params=params(16),
            cost_estimate=cost(MIB, 24 * height * wide * 2),
            name="core_sum",
        )(x_at.reshape(1), *[keep] * 4, *[got] * 4)

    def along_x(own, moved):
        return [own] + [
            along(moved[j - 1], lambda y, x, c, j=j: y * 8 + (x + j) % 4 * 2 + c)
            for j in range(1, 4)
        ]

    def along_y(send):
        return along(send, lambda y, x, c: (1 - y) * 8 + x * 2 + c)

    def y_blocks(strip):
        block = (1, strip, wide)
        return [pl.BlockSpec(block, lambda i, y: (1 - y[0], i, 0))] * 4 + [
            pl.BlockSpec(block, lambda i, y: (y[0], i, 0))
        ] * 4

    routed_sums = core_sum(keep_routed, send_routed, slots)
    own, *moved = routed_sums
    send_routed, keep_routed = pl.pallas_call(
        routed_sum_kernel,
        grid_spec=pltpu.PrefetchScalarGridSpec(
            num_scalar_prefetch=1,
            grid=(1,),
            in_specs=[vmem, vmem] + y_blocks(slots),
            out_specs=[pl.BlockSpec((1, slots, wide), lambda i, y: (0, 0, 0))] * 2,
        ),
        out_shape=[pltpu.HBM((1, slots, wide), BF), pltpu.HBM((1, slots, wide), F32)],
        compiler_params=params(8),
        cost_estimate=cost(MIB, MIB),
        name="routed_sum",
    )(y_at.reshape(1), route_index, residual_t, *along_x(own, moved) * 2)
    other_routed = along_y(send_routed)

    packed = 2 * wide + 128
    sent, scaled, chosen, send = pl.pallas_call(
        up_kernel,
        grid_spec=pltpu.PrefetchScalarGridSpec(
            num_scalar_prefetch=1,
            grid=(1,),
            in_specs=[vmem, pl.BlockSpec((1, wide), lambda i, group: (0, group[0]))]
            + [anywhere] * 4,
            out_specs=[vmem] * 3 + [anywhere],
            scratch_shapes=[
                pltpu.VMEM((groups * slots, wide), BF),
                pltpu.VMEM((2, wide, units), BF),
                pltpu.SemaphoreType.DMA((2,)),
            ],
        ),
        out_shape=[
            pltpu.HBM((groups, per, packed), BF),
            pltpu.HBM((live, wide), BF),
            pltpu.HBM((live, groups * slots), BF),
            pltpu.HBM(send.shape, BF),
        ],
        input_output_aliases={6: 3},
        compiler_params=params(16),
        cost_estimate=cost(800 * MIB, 4 * MIB),
        name="up",
    )(group.reshape(1), every, norm_gain[None], w_gate, w_up, routed_sums[0], send)
    got = lax.all_to_all(sent, "batch", 0, 0, tiled=True)

    strip = tokens // 2
    own, *moved = core_sum(keep, send, strip)
    flat = shape((per, units), F32)
    both, gate, up, scale, *moved = pl.pallas_call(
        lambda *refs: hidden_kernel(features, *refs),
        in_specs=[vmem] * 3 + [anywhere] * 3,
        out_specs=[vmem] * 4 + [anywhere] * 3,
        out_shape=[pltpu.HBM((groups, per + slots, units), BF), flat, flat, shape((per, 128), F32)]
        + [pltpu.HBM((2, tokens, wide), BF)] * 3,
        input_output_aliases={3: 4, 4: 5, 5: 6},
        compiler_params=params(8),
        cost_estimate=cost(MIB, MIB),
        name="hidden",
    )(got, keep_routed, other_routed, *moved)
    both = lax.all_to_all(both, "batch", 0, 0, tiled=True)
    misfit, hidden = pl.pallas_call(
        down_kernel,
        grid_spec=pltpu.PrefetchScalarGridSpec(
            num_scalar_prefetch=1,
            grid=(1,),
            in_specs=[vmem] * 3 + [pl.BlockSpec((wide, wide), lambda i, group: (0, group[0]))],
            out_specs=[vmem] * 2,
            scratch_shapes=[pltpu.VMEM((groups * slots, wide), BF)],
        ),
        out_shape=[
            pltpu.HBM((parts, live // parts, wide), BF),
            pltpu.HBM((live, units), BF),
        ],
        compiler_params=params(16),
        cost_estimate=cost(768 * MIB, 4 * MIB),
        name="down",
    )(group.reshape(1), both, w_down, chosen, projector)
    misfit = lax.all_to_all(misfit, "tensor", 0, 0, tiled=True)
    loss_scale = 1.0 / math.sqrt(live)
    send, keep = pl.pallas_call(
        x_sum_kernel,
        grid_spec=pltpu.PrefetchScalarGridSpec(
            num_scalar_prefetch=1,
            grid=(tokens // strip,),
            in_specs=y_blocks(strip),
            out_specs=[pl.BlockSpec((1, strip, wide), lambda i, y: (0, i, 0))] * 2,
        ),
        out_shape=[pltpu.HBM((1, tokens, wide), BF), pltpu.HBM((1, tokens, wide), F32)],
        compiler_params=params(16),
        cost_estimate=cost(MIB, 3 * MIB),
        name="x_sum",
    )(y_at.reshape(1), *along_x(own, moved) * 2)
    grad_out, send = pl.pallas_call(
        lambda *refs: misfit_kernel(loss_scale, *refs),
        in_specs=[vmem, anywhere],
        out_specs=[vmem, anywhere],
        out_shape=[pltpu.HBM(misfit.shape, BF), pltpu.HBM(send.shape, BF)],
        input_output_aliases={1: 1},
        compiler_params=params(8),
        cost_estimate=cost(MIB, MIB),
        name="misfit",
    )(misfit, send)
    other = along_y(send)
    grad_out = lax.all_to_all(grad_out, "tensor", 0, 0, tiled=True)

    back = pl.pallas_call(
        back_kernel,
        out_shape=pltpu.HBM((groups, per, units), BF),
        compiler_params=params(16),
        cost_estimate=cost(256 * MIB, MIB),
        name="back",
    )(grad_out, w_down)
    back = lax.all_to_all(back, "batch", 0, 0, tiled=True)
    acts = pl.pallas_call(
        acts_kernel,
        out_shape=pltpu.HBM((groups, per, 2 * units), BF),
        compiler_params=params(8),
        cost_estimate=cost(MIB, MIB),
        name="acts",
    )(back, gate, up, scale)
    acts = lax.all_to_all(acts, "batch", 0, 0, tiled=True)
    teacher_hidden = pl.pallas_call(
        residual_kernel,
        out_shape=shape(residual_t.shape, BF),
        compiler_params=params(8),
        cost_estimate=cost(MIB, 2 * MIB),
        name="residual",
    )(residual_t, keep, other)
    grad_down = pl.pallas_call(
        down_weights_kernel,
        out_shape=shape((wide, units), F32),
        compiler_params=params(16),
        cost_estimate=cost(256 * MIB, 2 * MIB),
        name="down_weights",
    )(grad_out, hidden)
    grad_gate, grad_up = pl.pallas_call(
        weights_kernel,
        out_shape=[shape((wide, units), F32)] * 2,
        compiler_params=params(16),
        cost_estimate=cost(512 * MIB, 4 * MIB),
        name="weights",
    )(scaled, acts)
    return teacher_hidden, grad_gate, grad_up, grad_down


def solution(mesh):
    in_specs = (
        P("batch", "tensor"),
        P("tensor", None),
        P("tensor", "batch"),
        P("tensor", None),
        P("batch", "tensor"),
        P(),
        P("batch", "tensor"),
        P("batch", "tensor"),
        P("batch", "tensor"),
        P("batch", None),
    )
    out_specs = (P("tensor", "batch"),) + (P("batch", "tensor"),) * 3
    return jax.shard_map(
        on_device, mesh=mesh, in_specs=in_specs, out_specs=out_specs, check_vma=False
    )
```

```python
import math

import jax
import jax.numpy as jnp
from jax import lax
from jax.experimental import pallas as pl
from jax.experimental.pallas import tpu as pltpu
from jax.sharding import PartitionSpec as P

EPS = 1e-05
BF = jnp.bfloat16
F32 = jnp.float32
MIB = 1 << 20


def params(mib):
    return pltpu.CompilerParams(vmem_limit_bytes=mib * MIB)


def cost(flops, nbytes):
    return pl.CostEstimate(flops=flops // 1024, bytes_accessed=nbytes // 1024, transcendentals=0)


def dot(a, b, ca=1, cb=0):
    return lax.dot_general(a, b, (((ca,), (cb,)), ((), ())), preferred_element_type=F32)


def whole(shape):
    return pl.BlockSpec(shape, lambda *_: (0,) * len(shape))


def slot_rows(route, tokens):
    slots = route.shape[1]
    grid = (slots, slots)
    diagonal = lax.broadcasted_iota(jnp.int32, grid, 0) == lax.broadcasted_iota(jnp.int32, grid, 1)
    spread = jnp.broadcast_to(route.astype(F32), grid)
    column = jnp.sum(jnp.where(diagonal, spread, 0.0), axis=1, keepdims=True)
    lane = lax.broadcasted_iota(jnp.int32, (slots, tokens), 1).astype(F32)
    return jnp.where(lane == column, 1.0, 0.0).astype(BF)


def rows_kernel(route_ref, x_ref, out_ref):
    route = route_ref[...]
    slots, wide = route.shape[1], x_ref.shape[1]
    rows = dot(slot_rows(route, x_ref.shape[0]), x_ref[...]).astype(BF)
    half = slots // 2
    out_ref[0:half, 0:wide] = rows[0:half]
    out_ref[0:half, wide : 2 * wide] = rows[half:]
    live = jnp.sum(jnp.where(route >= 0, 1.0, 0.0), axis=1, keepdims=True)
    out_ref[half : half + 8, :] = jnp.broadcast_to(live, (8, 2 * wide)).astype(BF)


def routed_kernel(core_ref, route_ref, attn_ref, weight_ref, keep_ref, send_ref, left_ref):
    @pl.when(pl.program_id(0) == 0)
    def _():
        hot = slot_rows(route_ref[...], attn_ref.shape[0])
        left_ref[...] = dot(hot, attn_ref[...]).astype(BF)

    wide = keep_ref.shape[2]
    product = dot(left_ref[...], weight_ref[...]).astype(BF)
    first = core_ref[0] == 0
    keep_ref[0] = jnp.where(first, product[:, 0:wide], product[:, wide:])
    send_ref[0] = jnp.where(first, product[:, wide:], product[:, 0:wide])


def teacher_kernel(core_ref, attn_ref, mine_ref, other_ref, after_ref, keep_ref, send_ref):
    for weight_ref, out_ref in ((other_ref, send_ref), (mine_ref, keep_ref)):
        out_ref[0] = dot(attn_ref[...], weight_ref[...]).astype(BF)


def copies_kernel(rows_ref, passed_ref, out_ref, same_ref, sems):
    copies = [
        pltpu.make_async_copy(rows_ref, out_ref.at[s], sems.at[s]) for s in range(out_ref.shape[0])
    ]
    for copy in copies:
        copy.start()
    for copy in copies:
        copy.wait()


def core_sum_kernel(x_ref, *refs):
    ways = len(refs) // 3
    for j in range(ways):
        total = refs[j][...].astype(F32) + refs[ways + j][...].astype(F32)
        refs[2 * ways + j][...] = total.astype(BF).reshape(refs[2 * ways + j].shape)


def x_sum_kernel(y_ref, *refs):
    ways = len(refs) // 2 - 1
    for i, out_ref in enumerate(refs[-2:]):
        total = refs[i * ways][...].astype(F32)
        for ref in refs[i * ways + 1 : (i + 1) * ways]:
            total = total + ref[...].astype(F32)
        out_ref[...] = total.astype(out_ref.dtype)


def routed_sum_kernel(y_ref, route_ref, residual_ref, *refs):
    x_sum_kernel(y_ref, *refs)
    hot = slot_rows(route_ref[...], residual_ref.shape[1])
    refs[-1][0] = refs[-1][0] + dot(hot, residual_ref[...], 1, 1)


def residual_kernel(residual_ref, keep_ref, got_ref, out_ref):
    summed = keep_ref[0] + got_ref[0].astype(F32)
    out_ref[...] = (residual_ref[...].astype(F32) + summed.T).astype(BF)


def up_kernel(
    group_ref, got_ref, gain_ref, gate_ref, up_ref, passed_ref,
    out_ref, rows_ref, chosen_ref, same_ref, padded_ref, weights_ref, sems,
):
    loads = [
        pltpu.make_async_copy(ref, weights_ref.at[i], sems.at[i])
        for i, ref in enumerate((gate_ref, up_ref))
    ]
    for load in loads:
        load.start()
    sources, height, wide = got_ref.shape
    groups = sources // 2
    half, side = height - 8, wide // 2
    slots = 2 * half
    per = out_ref.shape[1]
    total = groups * per

    for s in range(sources):
        g, d = s // 2, s % 2
        block = got_ref[s, 0:half, :]
        padded_ref[g * slots : g * slots + half, d * side : (d + 1) * side] = block[:, 0:side]
        padded_ref[g * slots + half : (g + 1) * slots, d * side : (d + 1) * side] = block[:, side:]
    at = half
    counts = [got_ref[2 * g, at : at + 8, 0 : 2 * slots].astype(F32)[0:1] for g in range(groups)]

    row = lax.broadcasted_iota(jnp.int32, (total, 2 * slots), 0)
    lane = lax.broadcasted_iota(jnp.int32, (total, 2 * slots), 1)
    second = lane >= slots
    slot = jnp.where(second, lane - slots, lane)
    slot_f = slot.astype(F32)
    shift = (row - slot).astype(F32)
    x = jnp.zeros((total, wide), F32)
    run = jnp.zeros_like(counts[0])
    for q in range(groups // 2):
        one, two = counts[2 * q], counts[2 * q + 1]
        start = jnp.where(second, run + one, run)
        count = jnp.where(second, two, one)
        run = run + one + two
        chosen = jnp.where((shift == start) & (slot_f < count), 1.0, 0.0).astype(BF)
        chosen_ref[:, 2 * q * slots : 2 * (q + 1) * slots] = chosen
        x = x + dot(chosen, padded_ref[2 * q * slots : 2 * (q + 1) * slots, :])

    square = jnp.sum(x * x, axis=1, keepdims=True)
    high = square.astype(BF)
    low = (square - high.astype(F32)).astype(BF)
    lane128 = lax.broadcasted_iota(jnp.int32, (total, 128), 1)
    squares = jnp.where(lane128 < 64, high.astype(F32), low.astype(F32)).astype(BF)
    scaled = (x * gain_ref[...]).astype(BF)
    rows_ref[...] = scaled
    for load in loads:
        load.wait()
    gate = dot(scaled, weights_ref[0]).astype(BF)
    up = dot(scaled, weights_ref[1]).astype(BF)
    at = 2 * wide + 128
    for g in range(groups):
        own = slice(g * per, (g + 1) * per)
        out_ref[g, :, 0:wide] = gate[own]
        out_ref[g, :, wide : 2 * wide] = up[own]
        out_ref[g, :, 2 * wide : at] = squares[own]


def hidden_kernel(
    features, got_ref, keep_ref, other_ref, passed_ref,
    out_ref, gate_ref, up_ref, scale_ref, same_ref,
):
    per, wide = gate_ref.shape
    at = got_ref.shape[2]
    total = got_ref[0, :, 0:at].astype(F32)
    for g in range(1, got_ref.shape[0]):
        total = total + got_ref[g, :, 0:at].astype(F32)
    square = total[:, 2 * wide : 2 * wide + 1] + total[:, 2 * wide + 64 : 2 * wide + 65]
    scale = lax.rsqrt(square * (1.0 / features) + EPS)
    gate = total[:, 0:wide] * scale
    up = total[:, wide : 2 * wide] * scale
    gate_ref[...] = gate
    up_ref[...] = up
    scale_ref[...] = jnp.broadcast_to(scale, scale_ref.shape)
    hidden = (gate * jax.nn.sigmoid(gate) * up).astype(BF)
    routed = (keep_ref[0] + other_ref[0].astype(F32)).astype(BF)
    for g in range(out_ref.shape[0]):
        out_ref[g, 0:per, :] = hidden
        out_ref[g, per:, :] = routed


def down_kernel(
    group_ref, got_ref, down_ref, chosen_ref, projector_ref, after_ref,
    out_ref, hidden_ref, rows_ref,
):
    groups = got_ref.shape[0]
    per = hidden_ref.shape[0] // groups
    slots = got_ref.shape[1] - per
    for g in range(groups):
        hidden_ref[g * per : (g + 1) * per, :] = got_ref[g, 0:per, :]
        rows_ref[g * slots : (g + 1) * slots, :] = got_ref[g, per:, :]
    rows = dot(chosen_ref[...], rows_ref[...]).astype(BF)
    part = dot(hidden_ref[...], down_ref[...], 1, 1) - dot(rows, projector_ref[...])
    out_ref[...] = part.astype(BF).reshape(out_ref.shape)


def misfit_kernel(scale, got_ref, out_ref):
    total = got_ref[0].astype(F32)
    for s in range(1, got_ref.shape[0]):
        total = total + got_ref[s].astype(F32)
    grad = (total * scale).astype(BF)
    for s in range(out_ref.shape[0]):
        out_ref[s] = grad


def back_kernel(got_ref, down_ref, after_ref, out_ref):
    groups, per, wide = out_ref.shape
    part = dot(got_ref[...].reshape(groups * per, got_ref.shape[2]), down_ref[...])
    out_ref[...] = part.astype(BF).reshape(groups, per, wide)


def acts_kernel(got_ref, gate_ref, up_ref, scale_ref, passed_ref, out_ref, same_ref):
    wide = gate_ref.shape[1]
    grad = got_ref[0].astype(F32)
    for g in range(1, got_ref.shape[0]):
        grad = grad + got_ref[g].astype(F32)
    grad = grad * scale_ref[:, 0:1]
    gate, up = gate_ref[...], up_ref[...]
    sigma = jax.nn.sigmoid(gate)
    grad_gate = (grad * up * sigma * (1.0 + gate * (1.0 - sigma))).astype(BF)
    grad_up = (grad * gate * sigma).astype(BF)
    for g in range(out_ref.shape[0]):
        out_ref[g, :, 0:wide] = grad_gate
        out_ref[g, :, wide : 2 * wide] = grad_up


def down_weights_kernel(grad_ref, hidden_ref, out_ref):
    rows, units = hidden_ref.shape
    out_ref[...] = dot(grad_ref[...].reshape(rows, out_ref.shape[0]), hidden_ref[...], 0, 0)


def weights_kernel(rows_ref, got_ref, gate_ref, up_ref):
    wide = gate_ref.shape[1]
    acts = got_ref[...].reshape(got_ref.shape[0] * got_ref.shape[1], 2 * wide)
    gate_ref[...] = dot(rows_ref[...], acts[:, 0:wide], 0, 0)
    up_ref[...] = dot(rows_ref[...], acts[:, wide:], 0, 0)


def on_device(
    attn_values,
    out_weight,
    residual_t,
    projector,
    student_input,
    norm_gain,
    w_gate,
    w_up,
    w_down,
    route_index,
):
    groups, parts = lax.axis_size("batch"), lax.axis_size("tensor")
    slots = route_index.shape[1]
    tokens, wide = attn_values.shape
    side = student_input.shape[1]
    features = norm_gain.shape[0]
    live = tokens * groups // 8
    per = live // groups
    units = w_gate.shape[1]
    extra = slots // 2 + 8
    group, part = lax.axis_index("batch"), lax.axis_index("tensor")
    core, x_at, y_at = part & 1, (part >> 1) & 3, part >> 3
    shape = jax.ShapeDtypeStruct
    vmem = pl.BlockSpec(memory_space=pltpu.VMEM)
    anywhere = pl.BlockSpec(memory_space=pl.ANY)

    def hbm(value):
        return pltpu.with_memory_space_constraint(value, pltpu.HBM)

    out_weight, w_gate, w_up, w_down, projector, student_input, route_index = (
        hbm(w) for w in (out_weight, w_gate, w_up, w_down, projector, student_input, route_index)
    )

    rows = pl.pallas_call(
        rows_kernel,
        out_shape=pltpu.HBM((extra, 2 * side), BF),
        cost_estimate=cost(2 * slots * tokens * side, MIB // 4),
        compiler_params=params(4),
        name="rows",
    )(route_index, student_input)
    pairs = [
        (b * parts + t, (t // 2) * parts + 2 * b + t % 2)
        for b in range(groups)
        for t in range(parts)
    ]
    rows = lax.ppermute(rows, ("batch", "tensor"), pairs)

    keep_routed, send_routed = pl.pallas_call(
        routed_kernel,
        grid_spec=pltpu.PrefetchScalarGridSpec(
            num_scalar_prefetch=1,
            grid=(parts // 2,),
            in_specs=[
                pl.BlockSpec(route_index.shape, lambda j, core: (0, 0)),
                pl.BlockSpec(attn_values.shape, lambda j, core: (0, 0)),
                pl.BlockSpec((wide, 2 * wide), lambda j, core: (0, j)),
            ],
            out_specs=[pl.BlockSpec((1, slots, wide), lambda j, core: (j, 0, 0))] * 2,
            scratch_shapes=[pltpu.VMEM((slots, wide), BF)],
        ),
        out_shape=[pltpu.HBM((parts // 2, slots, wide), BF)] * 2,
        compiler_params=params(16),
        cost_estimate=cost(2 * slots * wide * wide * parts, 10 * MIB),
        name="routed",
    )(core.reshape(1), route_index, attn_values, out_weight)
    copies, send_routed = pl.pallas_call(
        copies_kernel,
        in_specs=[vmem, anywhere],
        out_specs=[anywhere] * 2,
        out_shape=[pltpu.HBM((parts, *rows.shape), BF), pltpu.HBM(send_routed.shape, BF)],
        scratch_shapes=[pltpu.SemaphoreType.DMA((parts,))],
        input_output_aliases={1: 1},
        compiler_params=params(4),
        cost_estimate=cost(0, MIB // 2),
        name="copies",
    )(rows, send_routed)
    every = lax.all_to_all(copies, "tensor", 0, 0, tiled=True)

    def along(value, move):
        return lax.ppermute(value, "tensor", [(t, move(t // 8, (t // 2) % 4, t % 2)) for t in range(parts)])

    def core_sum(keep, send, strip):
        got = along(send, lambda y, x, c: y * 8 + x * 2 + 1 - c)
        height = keep.shape[1]
        block = (1, strip, wide)
        return pl.pallas_call(
            core_sum_kernel,
            grid_spec=pltpu.PrefetchScalarGridSpec(
                num_scalar_prefetch=1,
                grid=(2, height // strip),
                in_specs=[
                    pl.BlockSpec(block, lambda y, i, x, j=j: (4 * y + ((x[0] + j) & 3), i, 0))
                    for j in range(4)
                ]
                * 2,
                out_specs=[pl.BlockSpec(block, lambda y, i, x: (y, i, 0))] * 4,
            ),
            out_shape=[pltpu.HBM((2, height, wide), BF)] * 4,
            compiler_params=params(16),
            cost_estimate=cost(MIB, 24 * height * wide * 2),
            name="core_sum",
        )(x_at.reshape(1), *[hbm(keep)] * 4, *[got] * 4)

    def along_x(own, moved):
        return [own] + [
            along(moved[j - 1], lambda y, x, c, j=j: y * 8 + (x + j) % 4 * 2 + c)
            for j in range(1, 4)
        ]

    def along_y(send):
        return along(send, lambda y, x, c: (1 - y) * 8 + x * 2 + c)

    def y_blocks(strip):
        block = (1, strip, wide)
        return [pl.BlockSpec(block, lambda i, y: (1 - y[0], i, 0))] * 4 + [
            pl.BlockSpec(block, lambda i, y: (y[0], i, 0))
        ] * 4

    own, *moved = core_sum(keep_routed, send_routed, slots)
    send_routed, keep_routed = pl.pallas_call(
        routed_sum_kernel,
        grid_spec=pltpu.PrefetchScalarGridSpec(
            num_scalar_prefetch=1,
            grid=(1,),
            in_specs=[vmem, vmem] + y_blocks(slots),
            out_specs=[pl.BlockSpec((1, slots, wide), lambda i, y: (0, 0, 0))] * 2,
        ),
        out_shape=[pltpu.HBM((1, slots, wide), BF), pltpu.HBM((1, slots, wide), F32)],
        compiler_params=params(8),
        cost_estimate=cost(MIB, MIB),
        name="routed_sum",
    )(y_at.reshape(1), route_index, residual_t, *along_x(own, moved) * 2)
    packed = 2 * wide + 128
    sent, scaled, chosen, send_routed = pl.pallas_call(
        up_kernel,
        grid_spec=pltpu.PrefetchScalarGridSpec(
            num_scalar_prefetch=1,
            grid=(1,),
            in_specs=[vmem, pl.BlockSpec((1, wide), lambda i, group: (0, group[0]))]
            + [anywhere] * 3,
            out_specs=[vmem] * 3 + [anywhere],
            scratch_shapes=[
                pltpu.VMEM((groups * slots, wide), BF),
                pltpu.VMEM((2, wide, units), BF),
                pltpu.SemaphoreType.DMA((2,)),
            ],
        ),
        out_shape=[
            pltpu.HBM((groups, per, packed), BF),
            pltpu.HBM((live, wide), BF),
            pltpu.HBM((live, groups * slots), BF),
            pltpu.HBM(send_routed.shape, BF),
        ],
        input_output_aliases={5: 3},
        compiler_params=params(16),
        cost_estimate=cost(800 * MIB, 4 * MIB),
        name="up",
    )(group.reshape(1), every, norm_gain[None], w_gate, w_up, send_routed)
    other_routed = along_y(send_routed)
    got = lax.all_to_all(sent, "batch", 0, 0, tiled=True)

    keep, send = pl.pallas_call(
        teacher_kernel,
        grid_spec=pltpu.PrefetchScalarGridSpec(
            num_scalar_prefetch=1,
            grid=(parts // 2,),
            in_specs=[
                pl.BlockSpec(attn_values.shape, lambda j, core: (0, 0)),
                pl.BlockSpec((wide, wide), lambda j, core: (0, 2 * j + core[0])),
                pl.BlockSpec((wide, wide), lambda j, core: (0, 2 * j + 1 - core[0])),
                anywhere,
            ],
            out_specs=[pl.BlockSpec((1, tokens, wide), lambda j, core: (j, 0, 0))] * 2,
        ),
        out_shape=[pltpu.HBM((parts // 2, tokens, wide), BF)] * 2,
        compiler_params=params(16),
        cost_estimate=cost(2 * tokens * wide * wide * parts, 12 * MIB),
        name="teacher",
    )(core.reshape(1), attn_values, out_weight, out_weight, hbm(sent))
    strip = tokens // 2
    flat = shape((per, units), F32)
    both, gate, up, scale, send = pl.pallas_call(
        lambda *refs: hidden_kernel(features, *refs),
        in_specs=[vmem] * 3 + [anywhere],
        out_specs=[vmem] * 4 + [anywhere],
        out_shape=[
            pltpu.HBM((groups, per + slots, units), BF),
            flat,
            flat,
            shape((per, 128), F32),
            pltpu.HBM(send.shape, BF),
        ],
        input_output_aliases={3: 4},
        compiler_params=params(8),
        cost_estimate=cost(MIB, MIB),
        name="hidden",
    )(got, keep_routed, other_routed, send)
    own, *moved = core_sum(keep, send, strip)
    both = lax.all_to_all(both, "batch", 0, 0, tiled=True)
    misfit, hidden = pl.pallas_call(
        down_kernel,
        grid_spec=pltpu.PrefetchScalarGridSpec(
            num_scalar_prefetch=1,
            grid=(1,),
            in_specs=[vmem] * 3
            + [pl.BlockSpec((wide, wide), lambda i, group: (0, group[0])), anywhere],
            out_specs=[vmem] * 2,
            scratch_shapes=[pltpu.VMEM((groups * slots, wide), BF)],
        ),
        out_shape=[
            pltpu.HBM((parts, live // parts, wide), BF),
            pltpu.HBM((live, units), BF),
        ],
        compiler_params=params(16),
        cost_estimate=cost(768 * MIB, 4 * MIB),
        name="down",
    )(group.reshape(1), both, w_down, hbm(chosen), projector, hbm(own))
    misfit = lax.all_to_all(misfit, "tensor", 0, 0, tiled=True)
    loss_scale = 1.0 / math.sqrt(live)
    send, keep = pl.pallas_call(
        x_sum_kernel,
        grid_spec=pltpu.PrefetchScalarGridSpec(
            num_scalar_prefetch=1,
            grid=(tokens // strip,),
            in_specs=y_blocks(strip),
            out_specs=[pl.BlockSpec((1, strip, wide), lambda i, y: (0, i, 0))] * 2,
        ),
        out_shape=[pltpu.HBM((1, tokens, wide), BF), pltpu.HBM((1, tokens, wide), F32)],
        compiler_params=params(16),
        cost_estimate=cost(MIB, 3 * MIB),
        name="x_sum",
    )(y_at.reshape(1), *along_x(own, moved) * 2)
    grad_out = pl.pallas_call(
        lambda *refs: misfit_kernel(loss_scale, *refs),
        out_shape=pltpu.HBM(misfit.shape, BF),
        compiler_params=params(8),
        cost_estimate=cost(MIB, MIB),
        name="misfit",
    )(misfit)
    other = along_y(send)
    grad_out = lax.all_to_all(grad_out, "tensor", 0, 0, tiled=True)

    back = pl.pallas_call(
        back_kernel,
        in_specs=[vmem] * 2 + [anywhere],
        out_shape=pltpu.HBM((groups, per, units), BF),
        compiler_params=params(16),
        cost_estimate=cost(256 * MIB, MIB),
        name="back",
    )(grad_out, w_down, hbm(send))
    back = lax.all_to_all(back, "batch", 0, 0, tiled=True)
    teacher_hidden = pl.pallas_call(
        residual_kernel,
        out_shape=pltpu.HBM(residual_t.shape, BF),
        compiler_params=params(8),
        cost_estimate=cost(MIB, 2 * MIB),
        name="residual",
    )(residual_t, keep, other)
    acts, teacher_hidden = pl.pallas_call(
        acts_kernel,
        in_specs=[vmem] * 4 + [anywhere],
        out_specs=[vmem, anywhere],
        out_shape=[
            pltpu.HBM((groups, per, 2 * units), BF),
            pltpu.HBM(residual_t.shape, BF),
        ],
        input_output_aliases={4: 1},
        compiler_params=params(8),
        cost_estimate=cost(MIB, MIB),
        name="acts",
    )(back, gate, up, scale, teacher_hidden)
    acts = lax.all_to_all(acts, "batch", 0, 0, tiled=True)
    grad_down = pl.pallas_call(
        down_weights_kernel,
        out_shape=shape((wide, units), F32),
        compiler_params=params(16),
        cost_estimate=cost(256 * MIB, 2 * MIB),
        name="down_weights",
    )(grad_out, hidden)
    grad_gate, grad_up = pl.pallas_call(
        weights_kernel,
        out_shape=[shape((wide, units), F32)] * 2,
        compiler_params=params(16),
        cost_estimate=cost(512 * MIB, 4 * MIB),
        name="weights",
    )(hbm(scaled), acts)
    return teacher_hidden, grad_gate, grad_up, grad_down


def solution(mesh):
    in_specs = (
        P("batch", "tensor"),
        P("tensor", None),
        P("tensor", "batch"),
        P("tensor", None),
        P("batch", "tensor"),
        P(),
        P("batch", "tensor"),
        P("batch", "tensor"),
        P("batch", "tensor"),
        P("batch", None),
    )
    out_specs = (P("tensor", "batch"),) + (P("batch", "tensor"),) * 3
    return jax.shard_map(
        on_device, mesh=mesh, in_specs=in_specs, out_specs=out_specs, check_vma=False
    )
```

```python
import math

import jax
import jax.numpy as jnp
from jax import lax
from jax.experimental import pallas as pl
from jax.experimental.pallas import tpu as pltpu
from jax.sharding import PartitionSpec as P

EPS = 1e-05
BF = jnp.bfloat16
F32 = jnp.float32
MIB = 1 << 20


def params(mib):
    return pltpu.CompilerParams(vmem_limit_bytes=mib * MIB)


def cost(flops, nbytes):
    return pl.CostEstimate(flops=flops // 1024, bytes_accessed=nbytes // 1024, transcendentals=0)


def dot(a, b, ca=1, cb=0):
    return lax.dot_general(a, b, (((ca,), (cb,)), ((), ())), preferred_element_type=F32)


def whole(shape):
    return pl.BlockSpec(shape, lambda *_: (0,) * len(shape))


def slot_rows(route, tokens):
    slots = route.shape[1]
    grid = (slots, slots)
    diagonal = lax.broadcasted_iota(jnp.int32, grid, 0) == lax.broadcasted_iota(jnp.int32, grid, 1)
    spread = jnp.broadcast_to(route.astype(F32), grid)
    column = jnp.sum(jnp.where(diagonal, spread, 0.0), axis=1, keepdims=True)
    lane = lax.broadcasted_iota(jnp.int32, (slots, tokens), 1).astype(F32)
    return jnp.where(lane == column, 1.0, 0.0).astype(BF)


def rows_kernel(route_ref, x_ref, out_ref):
    route = route_ref[...]
    slots, wide = route.shape[1], x_ref.shape[1]
    rows = dot(slot_rows(route, x_ref.shape[0]), x_ref[...]).astype(BF)
    half = slots // 2
    out_ref[0:half, 0:wide] = rows[0:half]
    out_ref[0:half, wide : 2 * wide] = rows[half:]
    live = jnp.sum(jnp.where(route >= 0, 1.0, 0.0), axis=1, keepdims=True)
    out_ref[half : half + 8, :] = jnp.broadcast_to(live, (8, 2 * wide)).astype(BF)


def teacher_kernel(
    core_ref, route_ref, attn_ref, mine_ref, other_ref,
    keep_ref, send_ref, keep_routed_ref, send_routed_ref, left_ref,
):
    tokens = attn_ref.shape[0]

    @pl.when(pl.program_id(0) == 0)
    def _():
        left_ref[0:tokens, :] = attn_ref[...]
        left_ref[tokens:, :] = dot(slot_rows(route_ref[...], tokens), attn_ref[...]).astype(BF)

    for weight_ref, out_ref, routed_ref in (
        (other_ref, send_ref, send_routed_ref),
        (mine_ref, keep_ref, keep_routed_ref),
    ):
        product = dot(left_ref[...], weight_ref[...]).astype(BF)
        out_ref[0] = product[0:tokens]
        routed_ref[0] = product[tokens:]


def copies_kernel(rows_ref, p1, p2, out_ref, q1, q2, sems):
    copies = [
        pltpu.make_async_copy(rows_ref, out_ref.at[s], sems.at[s]) for s in range(out_ref.shape[0])
    ]
    for copy in copies:
        copy.start()
    for copy in copies:
        copy.wait()


def core_sum_kernel(x_ref, *refs):
    ways = len(refs) // 3
    for j in range(ways):
        total = refs[j][...].astype(F32) + refs[ways + j][...].astype(F32)
        refs[2 * ways + j][...] = total.astype(BF).reshape(refs[2 * ways + j].shape)


def x_sum_kernel(*refs):
    total = refs[0][...].astype(F32)
    for ref in refs[1:-1]:
        total = total + ref[...].astype(F32)
    refs[-1][...] = total.astype(refs[-1].dtype)


def routed_sum_kernel(y_ref, route_ref, residual_ref, after_ref, *refs):
    ways = len(refs) // 2 - 1
    x_sum_kernel(*refs[0:ways], refs[-2])
    x_sum_kernel(*refs[ways : 2 * ways], refs[-1])
    hot = slot_rows(route_ref[...], residual_ref.shape[1])
    refs[-1][0] = refs[-1][0] + dot(hot, residual_ref[...], 1, 1)


def residual_kernel(residual_ref, keep_ref, got_ref, out_ref):
    summed = keep_ref[0] + got_ref[0].astype(F32)
    out_ref[...] = (residual_ref[...].astype(F32) + summed.T).astype(BF)


def up_kernel(
    group_ref, got_ref, gain_ref, gate_ref, up_ref, p1, p2, p3, p4,
    out_ref, rows_ref, chosen_ref, q1, q2, q3, q4, padded_ref, weights_ref, sems,
):
    loads = [
        pltpu.make_async_copy(ref, weights_ref.at[i], sems.at[i])
        for i, ref in enumerate((gate_ref, up_ref))
    ]
    for load in loads:
        load.start()
    sources, height, wide = got_ref.shape
    groups = sources // 2
    half, side = height - 8, wide // 2
    slots = 2 * half
    per = out_ref.shape[1]
    total = groups * per

    for s in range(sources):
        g, d = s // 2, s % 2
        block = got_ref[s, 0:half, :]
        padded_ref[g * slots : g * slots + half, d * side : (d + 1) * side] = block[:, 0:side]
        padded_ref[g * slots + half : (g + 1) * slots, d * side : (d + 1) * side] = block[:, side:]
    at = half
    counts = [got_ref[2 * g, at : at + 8, 0 : 2 * slots].astype(F32)[0:1] for g in range(groups)]

    row = lax.broadcasted_iota(jnp.int32, (total, 2 * slots), 0)
    lane = lax.broadcasted_iota(jnp.int32, (total, 2 * slots), 1)
    second = lane >= slots
    slot = jnp.where(second, lane - slots, lane)
    slot_f = slot.astype(F32)
    shift = (row - slot).astype(F32)
    x = jnp.zeros((total, wide), F32)
    run = jnp.zeros_like(counts[0])
    for q in range(groups // 2):
        one, two = counts[2 * q], counts[2 * q + 1]
        start = jnp.where(second, run + one, run)
        count = jnp.where(second, two, one)
        run = run + one + two
        chosen = jnp.where((shift == start) & (slot_f < count), 1.0, 0.0).astype(BF)
        chosen_ref[:, 2 * q * slots : 2 * (q + 1) * slots] = chosen
        x = x + dot(chosen, padded_ref[2 * q * slots : 2 * (q + 1) * slots, :])

    square = jnp.sum(x * x, axis=1, keepdims=True)
    high = square.astype(BF)
    low = (square - high.astype(F32)).astype(BF)
    lane128 = lax.broadcasted_iota(jnp.int32, (total, 128), 1)
    squares = jnp.where(lane128 < 64, high.astype(F32), low.astype(F32)).astype(BF)
    scaled = (x * gain_ref[...]).astype(BF)
    rows_ref[...] = scaled
    for load in loads:
        load.wait()
    gate = dot(scaled, weights_ref[0]).astype(BF)
    up = dot(scaled, weights_ref[1]).astype(BF)
    at = 2 * wide + 128
    for g in range(groups):
        own = slice(g * per, (g + 1) * per)
        out_ref[g, :, 0:wide] = gate[own]
        out_ref[g, :, wide : 2 * wide] = up[own]
        out_ref[g, :, 2 * wide : at] = squares[own]


def hidden_kernel(
    features, got_ref, keep_ref, other_ref, p1, p2, p3, p4,
    out_ref, gate_ref, up_ref, scale_ref, q1, q2, q3, q4,
):
    per, wide = gate_ref.shape
    at = got_ref.shape[2]
    total = got_ref[0, :, 0:at].astype(F32)
    for g in range(1, got_ref.shape[0]):
        total = total + got_ref[g, :, 0:at].astype(F32)
    square = total[:, 2 * wide : 2 * wide + 1] + total[:, 2 * wide + 64 : 2 * wide + 65]
    scale = lax.rsqrt(square * (1.0 / features) + EPS)
    gate = total[:, 0:wide] * scale
    up = total[:, wide : 2 * wide] * scale
    gate_ref[...] = gate
    up_ref[...] = up
    scale_ref[...] = jnp.broadcast_to(scale, scale_ref.shape)
    hidden = (gate * jax.nn.sigmoid(gate) * up).astype(BF)
    routed = (keep_ref[0] + other_ref[0].astype(F32)).astype(BF)
    for g in range(out_ref.shape[0]):
        out_ref[g, 0:per, :] = hidden
        out_ref[g, per:, :] = routed


def down_kernel(
    group_ref, got_ref, down_ref, chosen_ref, projector_ref, after_ref,
    out_ref, hidden_ref, rows_ref,
):
    groups = got_ref.shape[0]
    per = hidden_ref.shape[0] // groups
    slots = got_ref.shape[1] - per
    for g in range(groups):
        hidden_ref[g * per : (g + 1) * per, :] = got_ref[g, 0:per, :]
        rows_ref[g * slots : (g + 1) * slots, :] = got_ref[g, per:, :]
    rows = dot(chosen_ref[...], rows_ref[...]).astype(BF)
    part = dot(hidden_ref[...], down_ref[...], 1, 1) - dot(rows, projector_ref[...])
    out_ref[...] = part.astype(BF).reshape(out_ref.shape)


def misfit_kernel(scale, got_ref, out_ref):
    total = got_ref[0].astype(F32)
    for s in range(1, got_ref.shape[0]):
        total = total + got_ref[s].astype(F32)
    grad = (total * scale).astype(BF)
    for s in range(out_ref.shape[0]):
        out_ref[s] = grad


def back_kernel(got_ref, down_ref, passed_ref, out_ref, same_ref):
    groups, per, wide = out_ref.shape
    part = dot(got_ref[...].reshape(groups * per, got_ref.shape[2]), down_ref[...])
    out_ref[...] = part.astype(BF).reshape(groups, per, wide)


def acts_kernel(got_ref, gate_ref, up_ref, scale_ref, out_ref):
    wide = gate_ref.shape[1]
    grad = got_ref[0].astype(F32)
    for g in range(1, got_ref.shape[0]):
        grad = grad + got_ref[g].astype(F32)
    grad = grad * scale_ref[:, 0:1]
    gate, up = gate_ref[...], up_ref[...]
    sigma = jax.nn.sigmoid(gate)
    grad_gate = (grad * up * sigma * (1.0 + gate * (1.0 - sigma))).astype(BF)
    grad_up = (grad * gate * sigma).astype(BF)
    for g in range(out_ref.shape[0]):
        out_ref[g, :, 0:wide] = grad_gate
        out_ref[g, :, wide : 2 * wide] = grad_up


def down_weights_kernel(grad_ref, hidden_ref, out_ref):
    rows, units = hidden_ref.shape
    out_ref[...] = dot(grad_ref[...].reshape(rows, out_ref.shape[0]), hidden_ref[...], 0, 0)


def weights_kernel(rows_ref, got_ref, gate_ref, up_ref):
    wide = gate_ref.shape[1]
    acts = got_ref[...].reshape(got_ref.shape[0] * got_ref.shape[1], 2 * wide)
    gate_ref[...] = dot(rows_ref[...], acts[:, 0:wide], 0, 0)
    up_ref[...] = dot(rows_ref[...], acts[:, wide:], 0, 0)


def on_device(
    attn_values,
    out_weight,
    residual_t,
    projector,
    student_input,
    norm_gain,
    w_gate,
    w_up,
    w_down,
    route_index,
):
    groups, parts = lax.axis_size("batch"), lax.axis_size("tensor")
    slots = route_index.shape[1]
    tokens, wide = attn_values.shape
    side = student_input.shape[1]
    features = norm_gain.shape[0]
    live = tokens * groups // 8
    per = live // groups
    units = w_gate.shape[1]
    extra = slots // 2 + 8
    group, part = lax.axis_index("batch"), lax.axis_index("tensor")
    core, x_at, y_at = part & 1, (part >> 1) & 3, part >> 3
    shape = jax.ShapeDtypeStruct
    vmem = pl.BlockSpec(memory_space=pltpu.VMEM)
    anywhere = pl.BlockSpec(memory_space=pl.ANY)

    def hbm(value):
        return pltpu.with_memory_space_constraint(value, pltpu.HBM)

    out_weight, w_gate, w_up, projector, student_input, route_index = (
        hbm(w) for w in (out_weight, w_gate, w_up, projector, student_input, route_index)
    )

    rows = pl.pallas_call(
        rows_kernel,
        out_shape=pltpu.HBM((extra, 2 * side), BF),
        cost_estimate=cost(2 * slots * tokens * side, MIB // 4),
        compiler_params=params(4),
        name="rows",
    )(route_index, student_input)
    pairs = [
        (b * parts + t, (t // 2) * parts + 2 * b + t % 2)
        for b in range(groups)
        for t in range(parts)
    ]
    rows = lax.ppermute(rows, ("batch", "tensor"), pairs)

    keep, send, keep_routed, send_routed = pl.pallas_call(
        teacher_kernel,
        grid_spec=pltpu.PrefetchScalarGridSpec(
            num_scalar_prefetch=1,
            grid=(parts // 2,),
            in_specs=[
                pl.BlockSpec(route_index.shape, lambda j, core: (0, 0)),
                pl.BlockSpec(attn_values.shape, lambda j, core: (0, 0)),
                pl.BlockSpec((wide, wide), lambda j, core: (0, 2 * j + core[0])),
                pl.BlockSpec((wide, wide), lambda j, core: (0, 2 * j + 1 - core[0])),
            ],
            out_specs=[pl.BlockSpec((1, tokens, wide), lambda j, core: (j, 0, 0))] * 2
            + [pl.BlockSpec((1, slots, wide), lambda j, core: (j, 0, 0))] * 2,
            scratch_shapes=[pltpu.VMEM((tokens + slots, wide), BF)],
        ),
        out_shape=[pltpu.HBM((parts // 2, tokens, wide), BF)] * 2
        + [pltpu.HBM((parts // 2, slots, wide), BF)] * 2,
        compiler_params=params(16),
        cost_estimate=cost(2 * (tokens + slots) * wide * wide * parts, 14 * MIB),
        name="teacher",
    )(core.reshape(1), route_index, hbm(attn_values), out_weight, out_weight)
    copies, send_routed, send = pl.pallas_call(
        copies_kernel,
        in_specs=[vmem] + [anywhere] * 2,
        out_specs=[anywhere] * 3,
        out_shape=[
            pltpu.HBM((parts, *rows.shape), BF),
            pltpu.HBM(send_routed.shape, BF),
            pltpu.HBM(send.shape, BF),
        ],
        scratch_shapes=[pltpu.SemaphoreType.DMA((parts,))],
        input_output_aliases={1: 1, 2: 2},
        compiler_params=params(4),
        cost_estimate=cost(0, MIB // 2),
        name="copies",
    )(rows, send_routed, send)
    every = lax.all_to_all(copies, "tensor", 0, 0, tiled=True)

    def along(value, move):
        return lax.ppermute(value, "tensor", [(t, move(t // 8, (t // 2) % 4, t % 2)) for t in range(parts)])

    def core_sum(keep, send, strip):
        got = along(send, lambda y, x, c: y * 8 + x * 2 + 1 - c)
        height = keep.shape[1]
        block = (1, strip, wide)
        return pl.pallas_call(
            core_sum_kernel,
            grid_spec=pltpu.PrefetchScalarGridSpec(
                num_scalar_prefetch=1,
                grid=(2, height // strip),
                in_specs=[
                    pl.BlockSpec(block, lambda y, i, x, j=j: (4 * y + ((x[0] + j) & 3), i, 0))
                    for j in range(4)
                ]
                * 2,
                out_specs=[pl.BlockSpec(block, lambda y, i, x: (y, i, 0))] * 4,
            ),
            out_shape=[pltpu.HBM((2, height, wide), BF)] * 4,
            compiler_params=params(16),
            cost_estimate=cost(MIB, 24 * height * wide * 2),
            name="core_sum",
        )(x_at.reshape(1), *[hbm(keep)] * 4, *[got] * 4)

    def along_x(own, moved):
        return [own] + [
            along(moved[j - 1], lambda y, x, c, j=j: y * 8 + (x + j) % 4 * 2 + c)
            for j in range(1, 4)
        ]

    def along_y(send):
        return along(send, lambda y, x, c: (1 - y) * 8 + x * 2 + c)

    def y_blocks(strip):
        block = (1, strip, wide)
        return [pl.BlockSpec(block, lambda i, y: (1 - y[0], i, 0))] * 4 + [
            pl.BlockSpec(block, lambda i, y: (y[0], i, 0))
        ] * 4

    strip = tokens // 4
    got = along(send, lambda y, x, c: y * 8 + x * 2 + 1 - c)
    blocks = [
        pl.BlockSpec(
            (1, strip, wide), lambda n, x, y, i=i, j=j: (4 * ((y[0] + i) & 1) + ((x[0] + j) & 3), n, 0)
        )
        for i in (1, 0)
        for j in range(4)
    ]
    sums = pl.pallas_call(
        lambda x_ref, *refs: core_sum_kernel(*refs),
        grid_spec=pltpu.PrefetchScalarGridSpec(
            num_scalar_prefetch=2,
            grid=(tokens // strip,),
            in_specs=blocks * 2,
            out_specs=[pl.BlockSpec((1, strip, wide), lambda n, x, y: (0, n, 0))] * 8,
        ),
        out_shape=[pltpu.HBM((1, tokens, wide), BF)] * 8,
        compiler_params=params(16),
        cost_estimate=cost(MIB, 6 * MIB),
        name="core_sum",
    )(x_at.reshape(1), y_at.reshape(1), *[hbm(keep)] * 8, *[got] * 8)
    others, own = sums[:4], sums[4:]

    routed, *moved = core_sum(keep_routed, send_routed, slots)
    send_routed, keep_routed = pl.pallas_call(
        routed_sum_kernel,
        grid_spec=pltpu.PrefetchScalarGridSpec(
            num_scalar_prefetch=1,
            grid=(1,),
            in_specs=[vmem, vmem, anywhere] + y_blocks(slots),
            out_specs=[pl.BlockSpec((1, slots, wide), lambda i, y: (0, 0, 0))] * 2,
        ),
        out_shape=[pltpu.HBM((1, slots, wide), BF), pltpu.HBM((1, slots, wide), F32)],
        compiler_params=params(8),
        cost_estimate=cost(MIB, MIB),
        name="routed_sum",
    )(y_at.reshape(1), route_index, residual_t, hbm(own[0]), *along_x(routed, moved) * 2)

    def x_sum(own, moved, kind):
        return pl.pallas_call(
            x_sum_kernel,
            grid=(2,),
            in_specs=[pl.BlockSpec((1, tokens // 2, wide), lambda n: (0, n, 0))] * 4,
            out_specs=pl.BlockSpec((1, tokens // 2, wide), lambda n: (0, n, 0)),
            out_shape=pltpu.HBM((1, tokens, wide), kind),
            compiler_params=params(8),
            cost_estimate=cost(MIB, 2 * MIB),
            name="x_sum",
        )(*along_x(own, moved))

    packed = 2 * wide + 128
    sent, scaled, chosen, send_routed, *moved = pl.pallas_call(
        up_kernel,
        grid_spec=pltpu.PrefetchScalarGridSpec(
            num_scalar_prefetch=1,
            grid=(1,),
            in_specs=[vmem, pl.BlockSpec((1, wide), lambda i, group: (0, group[0]))]
            + [anywhere] * 6,
            out_specs=[vmem] * 3 + [anywhere] * 4,
            scratch_shapes=[
                pltpu.VMEM((groups * slots, wide), BF),
                pltpu.VMEM((2, wide, units), BF),
                pltpu.SemaphoreType.DMA((2,)),
            ],
        ),
        out_shape=[
            pltpu.HBM((groups, per, packed), BF),
            pltpu.HBM((live, wide), BF),
            pltpu.HBM((live, groups * slots), BF),
            pltpu.HBM(send_routed.shape, BF),
        ]
        + [pltpu.HBM((1, tokens, wide), BF)] * 3,
        input_output_aliases={5: 3, 6: 4, 7: 5, 8: 6},
        compiler_params=params(16),
        cost_estimate=cost(800 * MIB, 4 * MIB),
        name="up",
    )(group.reshape(1), every, norm_gain[None], w_gate, w_up, send_routed, *others[1:])
    other_routed = along_y(send_routed)
    got = lax.all_to_all(sent, "batch", 0, 0, tiled=True)

    flat = shape((per, units), F32)
    send = x_sum(others[0], moved, BF)
    both, gate, up, scale, send, *moved = pl.pallas_call(
        lambda *refs: hidden_kernel(features, *refs),
        in_specs=[vmem] * 3 + [anywhere] * 4,
        out_specs=[vmem] * 4 + [anywhere] * 4,
        out_shape=[
            pltpu.HBM((groups, per + slots, units), BF),
            flat,
            flat,
            shape((per, 128), F32),
        ]
        + [pltpu.HBM((1, tokens, wide), BF)] * 4,
        input_output_aliases={3: 4, 4: 5, 5: 6, 6: 7},
        compiler_params=params(8),
        cost_estimate=cost(MIB, MIB),
        name="hidden",
    )(got, keep_routed, other_routed, send, *own[1:])
    other = along_y(send)
    keep = x_sum(own[0], moved, F32)
    both = lax.all_to_all(both, "batch", 0, 0, tiled=True)
    misfit, hidden = pl.pallas_call(
        down_kernel,
        grid_spec=pltpu.PrefetchScalarGridSpec(
            num_scalar_prefetch=1,
            grid=(1,),
            in_specs=[vmem] * 3
            + [pl.BlockSpec((wide, wide), lambda i, group: (0, group[0])), anywhere],
            out_specs=[vmem] * 2,
            scratch_shapes=[pltpu.VMEM((groups * slots, wide), BF)],
        ),
        out_shape=[
            pltpu.HBM((parts, live // parts, wide), BF),
            pltpu.HBM((live, units), BF),
        ],
        compiler_params=params(16),
        cost_estimate=cost(768 * MIB, 4 * MIB),
        name="down",
    )(group.reshape(1), both, w_down, chosen, projector, hbm(keep))
    misfit = lax.all_to_all(misfit, "tensor", 0, 0, tiled=True)
    loss_scale = 1.0 / math.sqrt(live)
    grad_out = pl.pallas_call(
        lambda *refs: misfit_kernel(loss_scale, *refs),
        out_shape=pltpu.HBM(misfit.shape, BF),
        compiler_params=params(8),
        cost_estimate=cost(MIB, MIB),
        name="misfit",
    )(misfit)
    grad_out = lax.all_to_all(grad_out, "tensor", 0, 0, tiled=True)

    teacher_hidden = pl.pallas_call(
        residual_kernel,
        out_shape=pltpu.HBM(residual_t.shape, BF),
        compiler_params=params(8),
        cost_estimate=cost(MIB, 2 * MIB),
        name="residual",
    )(residual_t, keep, other)
    back, teacher_hidden = pl.pallas_call(
        back_kernel,
        in_specs=[vmem] * 2 + [anywhere],
        out_specs=[vmem, anywhere],
        out_shape=[shape((groups, per, units), BF), pltpu.HBM(residual_t.shape, BF)],
        input_output_aliases={2: 1},
        compiler_params=params(16),
        cost_estimate=cost(256 * MIB, MIB),
        name="back",
    )(grad_out, w_down, teacher_hidden)
    back = lax.all_to_all(back, "batch", 0, 0, tiled=True)
    acts = pl.pallas_call(
        acts_kernel,
        out_shape=pltpu.HBM((groups, per, 2 * units), BF),
        compiler_params=params(8),
        cost_estimate=cost(MIB, MIB),
        name="acts",
    )(back, gate, up, scale)
    acts = lax.all_to_all(acts, "batch", 0, 0, tiled=True)
    grad_down = pl.pallas_call(
        down_weights_kernel,
        out_shape=shape((wide, units), F32),
        compiler_params=params(16),
        cost_estimate=cost(256 * MIB, 2 * MIB),
        name="down_weights",
    )(grad_out, hidden)
    grad_gate, grad_up = pl.pallas_call(
        weights_kernel,
        out_shape=[shape((wide, units), F32)] * 2,
        compiler_params=params(16),
        cost_estimate=cost(512 * MIB, 4 * MIB),
        name="weights",
    )(scaled, acts)
    return teacher_hidden, grad_gate, grad_up, grad_down


def solution(mesh):
    in_specs = (
        P("batch", "tensor"),
        P("tensor", None),
        P("tensor", "batch"),
        P("tensor", None),
        P("batch", "tensor"),
        P(),
        P("batch", "tensor"),
        P("batch", "tensor"),
        P("batch", "tensor"),
        P("batch", None),
    )
    out_specs = (P("tensor", "batch"),) + (P("batch", "tensor"),) * 3
    return jax.shard_map(
        on_device, mesh=mesh, in_specs=in_specs, out_specs=out_specs, check_vma=False
    )
```

```python
import math

import jax
import jax.numpy as jnp
from jax import lax
from jax.experimental import pallas as pl
from jax.experimental.pallas import tpu as pltpu
from jax.sharding import PartitionSpec as P

EPS = 1e-05
BF = jnp.bfloat16
F32 = jnp.float32
MIB = 1 << 20


def params(mib):
    return pltpu.CompilerParams(vmem_limit_bytes=mib * MIB)


def cost(flops, nbytes):
    return pl.CostEstimate(flops=flops // 1024, bytes_accessed=nbytes // 1024, transcendentals=0)


def dot(a, b, ca=1, cb=0):
    return lax.dot_general(a, b, (((ca,), (cb,)), ((), ())), preferred_element_type=F32)


def whole(shape):
    return pl.BlockSpec(shape, lambda *_: (0,) * len(shape))


def slot_rows(route, tokens):
    slots = route.shape[1]
    grid = (slots, slots)
    diagonal = lax.broadcasted_iota(jnp.int32, grid, 0) == lax.broadcasted_iota(jnp.int32, grid, 1)
    spread = jnp.broadcast_to(route.astype(F32), grid)
    column = jnp.sum(jnp.where(diagonal, spread, 0.0), axis=1, keepdims=True)
    lane = lax.broadcasted_iota(jnp.int32, (slots, tokens), 1).astype(F32)
    return jnp.where(lane == column, 1.0, 0.0).astype(BF)


def rows_kernel(route_ref, x_ref, out_ref):
    route = route_ref[...]
    slots, wide = route.shape[1], x_ref.shape[1]
    rows = dot(slot_rows(route, x_ref.shape[0]), x_ref[...]).astype(BF)
    half = slots // 2
    out_ref[0:half, 0:wide] = rows[0:half]
    out_ref[0:half, wide : 2 * wide] = rows[half:]
    live = jnp.sum(jnp.where(route >= 0, 1.0, 0.0), axis=1, keepdims=True)
    out_ref[half : half + 8, :] = jnp.broadcast_to(live, (8, 2 * wide)).astype(BF)


def teacher_kernel(
    core_ref, route_ref, attn_ref, mine_ref, other_ref,
    keep_ref, send_ref, keep_routed_ref, send_routed_ref, left_ref,
):
    tokens = attn_ref.shape[0]

    @pl.when(pl.program_id(0) == 0)
    def _():
        left_ref[0:tokens, :] = attn_ref[...]
        left_ref[tokens:, :] = dot(slot_rows(route_ref[...], tokens), attn_ref[...]).astype(BF)

    for weight_ref, out_ref, routed_ref in (
        (other_ref, send_ref, send_routed_ref),
        (mine_ref, keep_ref, keep_routed_ref),
    ):
        product = dot(left_ref[...], weight_ref[...]).astype(BF)
        out_ref[0] = product[0:tokens]
        routed_ref[0] = product[tokens:]


def copies_kernel(rows_ref, p1, p2, out_ref, q1, q2, sems):
    copies = [
        pltpu.make_async_copy(rows_ref, out_ref.at[s], sems.at[s]) for s in range(out_ref.shape[0])
    ]
    for copy in copies:
        copy.start()
    for copy in copies:
        copy.wait()


def core_sum_kernel(x_ref, *refs):
    ways = len(refs) // 3
    for j in range(ways):
        total = refs[j][...].astype(F32) + refs[ways + j][...].astype(F32)
        refs[2 * ways + j][...] = total.astype(BF).reshape(refs[2 * ways + j].shape)


def x_sum_kernel(*refs):
    total = refs[0][...].astype(F32)
    for ref in refs[1:-1]:
        total = total + ref[...].astype(F32)
    refs[-1][...] = total.astype(refs[-1].dtype)


def routed_sum_kernel(y_ref, route_ref, residual_ref, after_ref, *refs):
    ways = len(refs) // 2 - 1
    x_sum_kernel(*refs[0:ways], refs[-2])
    x_sum_kernel(*refs[ways : 2 * ways], refs[-1])
    hot = slot_rows(route_ref[...], residual_ref.shape[1])
    refs[-1][0] = refs[-1][0] + dot(hot, residual_ref[...], 1, 1)


def halves_kernel(x_ref, *refs):
    ins, (keep_a, send_a, keep_b, send_b) = refs[:8], refs[8:]
    sums = [(ins[m][0].astype(F32) + ins[4 + m][0].astype(F32)).astype(BF) for m in range(4)]
    for half, ref, order in ((0, keep_a, (0, 3)), (0, send_a, (1, 2)), (1, keep_b, (0, 1)), (1, send_b, (3, 2))):
        for i, m in enumerate(order):
            ref[i, 0] = sums[m][half]


def first_sum_kernel(keep_a, got_a, keep_b, got_b, own_a, on_a, own_b, on_b):
    for keep, got, own, on in ((keep_a, got_a, own_a, on_a), (keep_b, got_b, own_b, on_b)):
        own[...] = keep[0].astype(F32) + got[0].astype(F32)
        on[...] = (keep[1].astype(F32) + got[1].astype(F32)).astype(BF)


def second_sum_kernel(y_ref, *refs):
    ins, (send_ref, keep_ref) = refs[:8], refs[8:]
    for half in range(2):
        own, got, other_own, other_got = ins[4 * half : 4 * half + 4]
        send_ref[half] = (other_own[0] + other_got[0].astype(F32)).astype(BF)
        keep_ref[half] = own[0] + got[0].astype(F32)


def residual_kernel(residual_ref, keep_ref, got_ref, out_ref):
    summed = (keep_ref[...] + got_ref[...].astype(F32)).reshape(-1, keep_ref.shape[2])
    out_ref[...] = (residual_ref[...].astype(F32) + summed.T).astype(BF)


def up_kernel(
    group_ref, got_ref, gain_ref, gate_ref, up_ref, p1, p2, p3,
    out_ref, rows_ref, chosen_ref, q1, q2, q3, padded_ref, weights_ref, sems,
):
    loads = [
        pltpu.make_async_copy(ref, weights_ref.at[i], sems.at[i])
        for i, ref in enumerate((gate_ref, up_ref))
    ]
    for load in loads:
        load.start()
    sources, height, wide = got_ref.shape
    groups = sources // 2
    half, side = height - 8, wide // 2
    slots = 2 * half
    per = out_ref.shape[1]
    total = groups * per

    for s in range(sources):
        g, d = s // 2, s % 2
        block = got_ref[s, 0:half, :]
        padded_ref[g * slots : g * slots + half, d * side : (d + 1) * side] = block[:, 0:side]
        padded_ref[g * slots + half : (g + 1) * slots, d * side : (d + 1) * side] = block[:, side:]
    at = half
    counts = [got_ref[2 * g, at : at + 8, 0 : 2 * slots].astype(F32)[0:1] for g in range(groups)]

    row = lax.broadcasted_iota(jnp.int32, (total, 2 * slots), 0)
    lane = lax.broadcasted_iota(jnp.int32, (total, 2 * slots), 1)
    second = lane >= slots
    slot = jnp.where(second, lane - slots, lane)
    slot_f = slot.astype(F32)
    shift = (row - slot).astype(F32)
    x = jnp.zeros((total, wide), F32)
    run = jnp.zeros_like(counts[0])
    for q in range(groups // 2):
        one, two = counts[2 * q], counts[2 * q + 1]
        start = jnp.where(second, run + one, run)
        count = jnp.where(second, two, one)
        run = run + one + two
        chosen = jnp.where((shift == start) & (slot_f < count), 1.0, 0.0).astype(BF)
        chosen_ref[:, 2 * q * slots : 2 * (q + 1) * slots] = chosen
        x = x + dot(chosen, padded_ref[2 * q * slots : 2 * (q + 1) * slots, :])

    square = jnp.sum(x * x, axis=1, keepdims=True)
    high = square.astype(BF)
    low = (square - high.astype(F32)).astype(BF)
    lane128 = lax.broadcasted_iota(jnp.int32, (total, 128), 1)
    squares = jnp.where(lane128 < 64, high.astype(F32), low.astype(F32)).astype(BF)
    scaled = (x * gain_ref[...]).astype(BF)
    rows_ref[...] = scaled
    for load in loads:
        load.wait()
    gate = dot(scaled, weights_ref[0]).astype(BF)
    up = dot(scaled, weights_ref[1]).astype(BF)
    at = 2 * wide + 128
    for g in range(groups):
        own = slice(g * per, (g + 1) * per)
        out_ref[g, :, 0:wide] = gate[own]
        out_ref[g, :, wide : 2 * wide] = up[own]
        out_ref[g, :, 2 * wide : at] = squares[own]


def hidden_kernel(
    features, got_ref, keep_ref, other_ref, p1, p2,
    out_ref, gate_ref, up_ref, scale_ref, q1, q2,
):
    per, wide = gate_ref.shape
    at = got_ref.shape[2]
    total = got_ref[0, :, 0:at].astype(F32)
    for g in range(1, got_ref.shape[0]):
        total = total + got_ref[g, :, 0:at].astype(F32)
    square = total[:, 2 * wide : 2 * wide + 1] + total[:, 2 * wide + 64 : 2 * wide + 65]
    scale = lax.rsqrt(square * (1.0 / features) + EPS)
    gate = total[:, 0:wide] * scale
    up = total[:, wide : 2 * wide] * scale
    gate_ref[...] = gate
    up_ref[...] = up
    scale_ref[...] = jnp.broadcast_to(scale, scale_ref.shape)
    hidden = (gate * jax.nn.sigmoid(gate) * up).astype(BF)
    routed = (keep_ref[0] + other_ref[0].astype(F32)).astype(BF)
    for g in range(out_ref.shape[0]):
        out_ref[g, 0:per, :] = hidden
        out_ref[g, per:, :] = routed


def down_kernel(
    group_ref, got_ref, down_ref, chosen_ref, projector_ref, after_ref,
    out_ref, hidden_ref, rows_ref,
):
    groups = got_ref.shape[0]
    per = hidden_ref.shape[0] // groups
    slots = got_ref.shape[1] - per
    for g in range(groups):
        hidden_ref[g * per : (g + 1) * per, :] = got_ref[g, 0:per, :]
        rows_ref[g * slots : (g + 1) * slots, :] = got_ref[g, per:, :]
    rows = dot(chosen_ref[...], rows_ref[...]).astype(BF)
    part = dot(hidden_ref[...], down_ref[...], 1, 1) - dot(rows, projector_ref[...])
    out_ref[...] = part.astype(BF).reshape(out_ref.shape)


def misfit_kernel(scale, got_ref, out_ref):
    total = got_ref[0].astype(F32)
    for s in range(1, got_ref.shape[0]):
        total = total + got_ref[s].astype(F32)
    grad = (total * scale).astype(BF)
    for s in range(out_ref.shape[0]):
        out_ref[s] = grad


def back_kernel(got_ref, down_ref, passed_ref, out_ref, same_ref):
    groups, per, wide = out_ref.shape
    part = dot(got_ref[...].reshape(groups * per, got_ref.shape[2]), down_ref[...])
    out_ref[...] = part.astype(BF).reshape(groups, per, wide)


def acts_kernel(got_ref, gate_ref, up_ref, scale_ref, out_ref):
    wide = gate_ref.shape[1]
    grad = got_ref[0].astype(F32)
    for g in range(1, got_ref.shape[0]):
        grad = grad + got_ref[g].astype(F32)
    grad = grad * scale_ref[:, 0:1]
    gate, up = gate_ref[...], up_ref[...]
    sigma = jax.nn.sigmoid(gate)
    grad_gate = (grad * up * sigma * (1.0 + gate * (1.0 - sigma))).astype(BF)
    grad_up = (grad * gate * sigma).astype(BF)
    for g in range(out_ref.shape[0]):
        out_ref[g, :, 0:wide] = grad_gate
        out_ref[g, :, wide : 2 * wide] = grad_up


def down_weights_kernel(grad_ref, hidden_ref, out_ref):
    rows, units = hidden_ref.shape
    out_ref[...] = dot(grad_ref[...].reshape(rows, out_ref.shape[0]), hidden_ref[...], 0, 0)


def weights_kernel(rows_ref, got_ref, gate_ref, up_ref):
    wide = gate_ref.shape[1]
    acts = got_ref[...].reshape(got_ref.shape[0] * got_ref.shape[1], 2 * wide)
    gate_ref[...] = dot(rows_ref[...], acts[:, 0:wide], 0, 0)
    up_ref[...] = dot(rows_ref[...], acts[:, wide:], 0, 0)


def on_device(
    attn_values,
    out_weight,
    residual_t,
    projector,
    student_input,
    norm_gain,
    w_gate,
    w_up,
    w_down,
    route_index,
):
    groups, parts = lax.axis_size("batch"), lax.axis_size("tensor")
    slots = route_index.shape[1]
    tokens, wide = attn_values.shape
    side = student_input.shape[1]
    features = norm_gain.shape[0]
    live = tokens * groups // 8
    per = live // groups
    units = w_gate.shape[1]
    extra = slots // 2 + 8
    group, part = lax.axis_index("batch"), lax.axis_index("tensor")
    core, x_at, y_at = part & 1, (part >> 1) & 3, part >> 3
    shape = jax.ShapeDtypeStruct
    vmem = pl.BlockSpec(memory_space=pltpu.VMEM)
    anywhere = pl.BlockSpec(memory_space=pl.ANY)

    def hbm(value):
        return pltpu.with_memory_space_constraint(value, pltpu.HBM)

    out_weight, w_gate, w_up, projector, student_input, route_index = (
        hbm(w) for w in (out_weight, w_gate, w_up, projector, student_input, route_index)
    )

    rows = pl.pallas_call(
        rows_kernel,
        out_shape=pltpu.HBM((extra, 2 * side), BF),
        cost_estimate=cost(2 * slots * tokens * side, MIB // 4),
        compiler_params=params(4),
        name="rows",
    )(route_index, student_input)
    pairs = [
        (b * parts + t, (t // 2) * parts + 2 * b + t % 2)
        for b in range(groups)
        for t in range(parts)
    ]
    rows = lax.ppermute(rows, ("batch", "tensor"), pairs)

    keep, send, keep_routed, send_routed = pl.pallas_call(
        teacher_kernel,
        grid_spec=pltpu.PrefetchScalarGridSpec(
            num_scalar_prefetch=1,
            grid=(parts // 2,),
            in_specs=[
                pl.BlockSpec(route_index.shape, lambda j, core: (0, 0)),
                pl.BlockSpec(attn_values.shape, lambda j, core: (0, 0)),
                pl.BlockSpec((wide, wide), lambda j, core: (0, 2 * j + core[0])),
                pl.BlockSpec((wide, wide), lambda j, core: (0, 2 * j + 1 - core[0])),
            ],
            out_specs=[pl.BlockSpec((1, tokens, wide), lambda j, core: (j, 0, 0))] * 2
            + [pl.BlockSpec((1, slots, wide), lambda j, core: (j, 0, 0))] * 2,
            scratch_shapes=[pltpu.VMEM((tokens + slots, wide), BF)],
        ),
        out_shape=[pltpu.HBM((parts // 2, tokens, wide), BF)] * 2
        + [pltpu.HBM((parts // 2, slots, wide), BF)] * 2,
        compiler_params=params(16),
        cost_estimate=cost(2 * (tokens + slots) * wide * wide * parts, 14 * MIB),
        name="teacher",
    )(core.reshape(1), route_index, hbm(attn_values), out_weight, out_weight)
    copies, send_routed, send = pl.pallas_call(
        copies_kernel,
        in_specs=[vmem] + [anywhere] * 2,
        out_specs=[anywhere] * 3,
        out_shape=[
            pltpu.HBM((parts, *rows.shape), BF),
            pltpu.HBM(send_routed.shape, BF),
            pltpu.HBM(send.shape, BF),
        ],
        scratch_shapes=[pltpu.SemaphoreType.DMA((parts,))],
        input_output_aliases={1: 1, 2: 2},
        compiler_params=params(4),
        cost_estimate=cost(0, MIB // 2),
        name="copies",
    )(rows, send_routed, send)
    every = lax.all_to_all(copies, "tensor", 0, 0, tiled=True)

    def along(value, move):
        return lax.ppermute(value, "tensor", [(t, move(t // 8, (t // 2) % 4, t % 2)) for t in range(parts)])

    def core_sum(keep, send, strip):
        got = along(send, lambda y, x, c: y * 8 + x * 2 + 1 - c)
        height = keep.shape[1]
        block = (1, strip, wide)
        return pl.pallas_call(
            core_sum_kernel,
            grid_spec=pltpu.PrefetchScalarGridSpec(
                num_scalar_prefetch=1,
                grid=(2, height // strip),
                in_specs=[
                    pl.BlockSpec(block, lambda y, i, x, j=j: (4 * y + ((x[0] + j) & 3), i, 0))
                    for j in range(4)
                ]
                * 2,
                out_specs=[pl.BlockSpec(block, lambda y, i, x: (y, i, 0))] * 4,
            ),
            out_shape=[pltpu.HBM((2, height, wide), BF)] * 4,
            compiler_params=params(16),
            cost_estimate=cost(MIB, 24 * height * wide * 2),
            name="core_sum",
        )(x_at.reshape(1), *[hbm(keep)] * 4, *[got] * 4)

    def along_x(own, moved):
        return [own] + [
            along(moved[j - 1], lambda y, x, c, j=j: y * 8 + (x + j) % 4 * 2 + c)
            for j in range(1, 4)
        ]

    def along_y(send):
        return along(send, lambda y, x, c: (1 - y) * 8 + x * 2 + c)

    def y_blocks(strip):
        block = (1, strip, wide)
        return [pl.BlockSpec(block, lambda i, y: (1 - y[0], i, 0))] * 4 + [
            pl.BlockSpec(block, lambda i, y: (y[0], i, 0))
        ] * 4

    half, strip = tokens // 2, tokens // 4
    got = along(send, lambda y, x, c: y * 8 + x * 2 + 1 - c)
    halves = (parts // 2, 2, half, wide)
    pair = pltpu.HBM((2, 2, half, wide), BF)
    keep_a, send_a, keep_b, send_b = pl.pallas_call(
        halves_kernel,
        grid_spec=pltpu.PrefetchScalarGridSpec(
            num_scalar_prefetch=1,
            grid=(2, half // strip),
            in_specs=[
                pl.BlockSpec(
                    (1, 2, strip, wide),
                    lambda y, n, x, m=m: (4 * y + lax.bitwise_xor(x[0], jnp.int32(m)), 0, n, 0),
                )
                for m in range(4)
            ]
            * 2,
            out_specs=[pl.BlockSpec((2, 1, strip, wide), lambda y, n, x: (0, y, n, 0))] * 4,
        ),
        out_shape=[pair] * 4,
        compiler_params=params(16),
        cost_estimate=cost(MIB, 6 * MIB),
        name="halves",
    )(x_at.reshape(1), *[hbm(keep.reshape(halves))] * 4, *[got.reshape(halves)] * 4)

    routed, *moved = core_sum(keep_routed, send_routed, slots)
    send_routed, keep_routed = pl.pallas_call(
        routed_sum_kernel,
        grid_spec=pltpu.PrefetchScalarGridSpec(
            num_scalar_prefetch=1,
            grid=(1,),
            in_specs=[vmem, vmem, anywhere] + y_blocks(slots),
            out_specs=[pl.BlockSpec((1, slots, wide), lambda i, y: (0, 0, 0))] * 2,
        ),
        out_shape=[pltpu.HBM((1, slots, wide), BF), pltpu.HBM((1, slots, wide), F32)],
        compiler_params=params(8),
        cost_estimate=cost(MIB, MIB),
        name="routed_sum",
    )(y_at.reshape(1), route_index, residual_t, hbm(keep_a), *along_x(routed, moved) * 2)

    def along_x_by(value, mask):
        return along(value, lambda y, x, c: y * 8 + (x ^ mask) * 2 + c)

    packed = 2 * wide + 128
    sent, scaled, chosen, send_routed, send_a, send_b = pl.pallas_call(
        up_kernel,
        grid_spec=pltpu.PrefetchScalarGridSpec(
            num_scalar_prefetch=1,
            grid=(1,),
            in_specs=[vmem, pl.BlockSpec((1, wide), lambda i, group: (0, group[0]))]
            + [anywhere] * 5,
            out_specs=[vmem] * 3 + [anywhere] * 3,
            scratch_shapes=[
                pltpu.VMEM((groups * slots, wide), BF),
                pltpu.VMEM((2, wide, units), BF),
                pltpu.SemaphoreType.DMA((2,)),
            ],
        ),
        out_shape=[
            pltpu.HBM((groups, per, packed), BF),
            pltpu.HBM((live, wide), BF),
            pltpu.HBM((live, groups * slots), BF),
            pltpu.HBM(send_routed.shape, BF),
        ]
        + [pair] * 2,
        input_output_aliases={5: 3, 6: 4, 7: 5},
        compiler_params=params(16),
        cost_estimate=cost(800 * MIB, 4 * MIB),
        name="up",
    )(group.reshape(1), every, norm_gain[None], w_gate, w_up, send_routed, send_a, send_b)
    other_routed = along_y(send_routed)
    got = lax.all_to_all(sent, "batch", 0, 0, tiled=True)

    flat = shape((per, units), F32)
    block = pl.BlockSpec((2, 2, strip, wide), lambda n: (0, 0, n, 0))
    line = pl.BlockSpec((2, strip, wide), lambda n: (0, n, 0))
    own_a, on_a, own_b, on_b = pl.pallas_call(
        first_sum_kernel,
        grid=(half // strip,),
        in_specs=[block] * 4,
        out_specs=[line] * 4,
        out_shape=[pltpu.HBM((2, half, wide), F32), pltpu.HBM((2, half, wide), BF)] * 2,
        compiler_params=params(16),
        cost_estimate=cost(MIB, 3 * MIB),
        name="first_sum",
    )(keep_a, along_x_by(send_a, 1), keep_b, along_x_by(send_b, 3))
    both, gate, up, scale, on_a, on_b = pl.pallas_call(
        lambda *refs: hidden_kernel(features, *refs),
        in_specs=[vmem] * 3 + [anywhere] * 2,
        out_specs=[vmem] * 4 + [anywhere] * 2,
        out_shape=[
            pltpu.HBM((groups, per + slots, units), BF),
            flat,
            flat,
            shape((per, 128), F32),
        ]
        + [pltpu.HBM((2, half, wide), BF)] * 2,
        input_output_aliases={3: 4, 4: 5},
        compiler_params=params(8),
        cost_estimate=cost(MIB, MIB),
        name="hidden",
    )(got, keep_routed, other_routed, on_a, on_b)
    got_a, got_b = along_x_by(on_a, 3), along_x_by(on_b, 1)
    here = pl.BlockSpec((1, strip, wide), lambda n, y: (y[0], n, 0))
    there = pl.BlockSpec((1, strip, wide), lambda n, y: (1 - y[0], n, 0))
    send, keep = pl.pallas_call(
        second_sum_kernel,
        grid_spec=pltpu.PrefetchScalarGridSpec(
            num_scalar_prefetch=1,
            grid=(half // strip,),
            in_specs=[here, here, there, there] * 2,
            out_specs=[pl.BlockSpec((2, strip, wide), lambda n, y: (0, n, 0))] * 2,
        ),
        out_shape=[pltpu.HBM((2, half, wide), BF), pltpu.HBM((2, half, wide), F32)],
        compiler_params=params(16),
        cost_estimate=cost(MIB, 3 * MIB),
        name="second_sum",
    )(y_at.reshape(1), *[own_a, got_a] * 2, *[own_b, got_b] * 2)
    other = along_y(send)
    both = lax.all_to_all(both, "batch", 0, 0, tiled=True)
    misfit, hidden = pl.pallas_call(
        down_kernel,
        grid_spec=pltpu.PrefetchScalarGridSpec(
            num_scalar_prefetch=1,
            grid=(1,),
            in_specs=[vmem] * 3
            + [pl.BlockSpec((wide, wide), lambda i, group: (0, group[0])), anywhere],
            out_specs=[vmem] * 2,
            scratch_shapes=[pltpu.VMEM((groups * slots, wide), BF)],
        ),
        out_shape=[
            pltpu.HBM((parts, live // parts, wide), BF),
            pltpu.HBM((live, units), BF),
        ],
        compiler_params=params(16),
        cost_estimate=cost(768 * MIB, 4 * MIB),
        name="down",
    )(group.reshape(1), both, w_down, chosen, projector, hbm(keep))
    misfit = lax.all_to_all(misfit, "tensor", 0, 0, tiled=True)
    loss_scale = 1.0 / math.sqrt(live)
    grad_out = pl.pallas_call(
        lambda *refs: misfit_kernel(loss_scale, *refs),
        out_shape=pltpu.HBM(misfit.shape, BF),
        compiler_params=params(8),
        cost_estimate=cost(MIB, MIB),
        name="misfit",
    )(misfit)
    grad_out = lax.all_to_all(grad_out, "tensor", 0, 0, tiled=True)

    teacher_hidden = pl.pallas_call(
        residual_kernel,
        out_shape=pltpu.HBM(residual_t.shape, BF),
        compiler_params=params(8),
        cost_estimate=cost(MIB, 2 * MIB),
        name="residual",
    )(residual_t, keep, other)
    back, teacher_hidden = pl.pallas_call(
        back_kernel,
        in_specs=[vmem] * 2 + [anywhere],
        out_specs=[vmem, anywhere],
        out_shape=[shape((groups, per, units), BF), pltpu.HBM(residual_t.shape, BF)],
        input_output_aliases={2: 1},
        compiler_params=params(16),
        cost_estimate=cost(256 * MIB, MIB),
        name="back",
    )(grad_out, w_down, teacher_hidden)
    back = lax.all_to_all(back, "batch", 0, 0, tiled=True)
    acts = pl.pallas_call(
        acts_kernel,
        out_shape=pltpu.HBM((groups, per, 2 * units), BF),
        compiler_params=params(8),
        cost_estimate=cost(MIB, MIB),
        name="acts",
    )(back, gate, up, scale)
    acts = lax.all_to_all(acts, "batch", 0, 0, tiled=True)
    grad_down = pl.pallas_call(
        down_weights_kernel,
        out_shape=shape((wide, units), F32),
        compiler_params=params(16),
        cost_estimate=cost(256 * MIB, 2 * MIB),
        name="down_weights",
    )(grad_out, hidden)
    grad_gate, grad_up = pl.pallas_call(
        weights_kernel,
        out_shape=[shape((wide, units), F32)] * 2,
        compiler_params=params(16),
        cost_estimate=cost(512 * MIB, 4 * MIB),
        name="weights",
    )(scaled, acts)
    return teacher_hidden, grad_gate, grad_up, grad_down


def solution(mesh):
    in_specs = (
        P("batch", "tensor"),
        P("tensor", None),
        P("tensor", "batch"),
        P("tensor", None),
        P("batch", "tensor"),
        P(),
        P("batch", "tensor"),
        P("batch", "tensor"),
        P("batch", "tensor"),
        P("batch", None),
    )
    out_specs = (P("tensor", "batch"),) + (P("batch", "tensor"),) * 3
    return jax.shard_map(
        on_device, mesh=mesh, in_specs=in_specs, out_specs=out_specs, check_vma=False
    )
```

```python
import math

import jax
import jax.numpy as jnp
from jax import lax
from jax.experimental import pallas as pl
from jax.experimental.pallas import tpu as pltpu
from jax.sharding import PartitionSpec as P

EPS = 1e-05
BF = jnp.bfloat16
F32 = jnp.float32
MIB = 1 << 20


def params(mib):
    return pltpu.CompilerParams(vmem_limit_bytes=mib * MIB)


def cost(flops, nbytes):
    return pl.CostEstimate(flops=flops // 1024, bytes_accessed=nbytes // 1024, transcendentals=0)


def dot(a, b, ca=1, cb=0):
    return lax.dot_general(a, b, (((ca,), (cb,)), ((), ())), preferred_element_type=F32)


def whole(shape):
    return pl.BlockSpec(shape, lambda *_: (0,) * len(shape))


def slot_rows(route, tokens):
    slots = route.shape[1]
    grid = (slots, slots)
    diagonal = lax.broadcasted_iota(jnp.int32, grid, 0) == lax.broadcasted_iota(jnp.int32, grid, 1)
    spread = jnp.broadcast_to(route.astype(F32), grid)
    column = jnp.sum(jnp.where(diagonal, spread, 0.0), axis=1, keepdims=True)
    lane = lax.broadcasted_iota(jnp.int32, (slots, tokens), 1).astype(F32)
    return jnp.where(lane == column, 1.0, 0.0).astype(BF)


def rows_kernel(route_ref, x_ref, out_ref):
    route = route_ref[...]
    slots, wide = route.shape[1], x_ref.shape[1]
    rows = dot(slot_rows(route, x_ref.shape[0]), x_ref[...]).astype(BF)
    half = slots // 2
    out_ref[0:half, 0:wide] = rows[0:half]
    out_ref[0:half, wide : 2 * wide] = rows[half:]
    live = jnp.sum(jnp.where(route >= 0, 1.0, 0.0), axis=1, keepdims=True)
    out_ref[half : half + 8, :] = jnp.broadcast_to(live, (8, 2 * wide)).astype(BF)


def teacher_kernel(
    core_ref, route_ref, attn_ref, mine_ref, other_ref,
    keep_ref, send_ref, keep_routed_ref, send_routed_ref, left_ref,
):
    tokens = attn_ref.shape[0]

    @pl.when(pl.program_id(0) == 0)
    def _():
        left_ref[0:tokens, :] = attn_ref[...]
        left_ref[tokens:, :] = dot(slot_rows(route_ref[...], tokens), attn_ref[...]).astype(BF)

    for weight_ref, out_ref, routed_ref in (
        (other_ref, send_ref, send_routed_ref),
        (mine_ref, keep_ref, keep_routed_ref),
    ):
        product = dot(left_ref[...], weight_ref[...]).astype(BF)
        out_ref[0] = product[0:tokens]
        routed_ref[0] = product[tokens:]


def copies_kernel(rows_ref, p1, p2, out_ref, q1, q2, sems):
    copies = [
        pltpu.make_async_copy(rows_ref, out_ref.at[s], sems.at[s]) for s in range(out_ref.shape[0])
    ]
    for copy in copies:
        copy.start()
    for copy in copies:
        copy.wait()


def core_sum_kernel(x_ref, *refs):
    ways = len(refs) // 3
    for j in range(ways):
        total = refs[j][...].astype(F32) + refs[ways + j][...].astype(F32)
        refs[2 * ways + j][...] = total.astype(BF).reshape(refs[2 * ways + j].shape)


def x_sum_kernel(*refs):
    total = refs[0][...].astype(F32)
    for ref in refs[1:-1]:
        total = total + ref[...].astype(F32)
    refs[-1][...] = total.astype(refs[-1].dtype)


def routed_sum_kernel(y_ref, route_ref, residual_ref, p1, p2, p3, *refs):
    ins, (send_ref, keep_ref) = refs[:8], refs[8:10]
    x_sum_kernel(*ins[:4], send_ref)
    x_sum_kernel(*ins[4:], keep_ref)
    hot = slot_rows(route_ref[...], residual_ref.shape[1])
    keep_ref[0] = keep_ref[0] + dot(hot, residual_ref[...], 1, 1)


def halves_kernel(x_ref, *refs):
    ins, (keep_a, send_a, keep_b, send_b) = refs[:8], refs[8:]
    sums = [(ins[m][0].astype(F32) + ins[4 + m][0].astype(F32)).astype(BF) for m in range(4)]
    for half, ref, order in ((0, keep_a, (0, 3)), (0, send_a, (1, 2)), (1, keep_b, (0, 1)), (1, send_b, (3, 2))):
        for i, m in enumerate(order):
            ref[i, 0] = sums[m][half]


def first_sum_kernel(keep_a, got_a, keep_b, got_b, own_a, on_a, own_b, on_b):
    for keep, got, own, on in ((keep_a, got_a, own_a, on_a), (keep_b, got_b, own_b, on_b)):
        own[...] = keep[0].astype(F32) + got[0].astype(F32)
        on[...] = (keep[1].astype(F32) + got[1].astype(F32)).astype(BF)


def second_sum_kernel(y_ref, *refs):
    ins, (send_ref, keep_ref) = refs[:8], refs[8:]
    for half in range(2):
        own, got, other_own, other_got = ins[4 * half : 4 * half + 4]
        send_ref[half] = (other_own[0] + other_got[0].astype(F32)).astype(BF)
        keep_ref[half] = own[0] + got[0].astype(F32)


def residual_kernel(residual_ref, keep_ref, got_ref, out_ref):
    summed = (keep_ref[...] + got_ref[...].astype(F32)).reshape(-1, keep_ref.shape[2])
    out_ref[...] = (residual_ref[...].astype(F32) + summed.T).astype(BF)


def up_kernel(
    group_ref, got_ref, gain_ref, gate_ref, up_ref, after_ref,
    out_ref, rows_ref, chosen_ref, padded_ref, weights_ref, sems,
):
    loads = [
        pltpu.make_async_copy(ref, weights_ref.at[i], sems.at[i])
        for i, ref in enumerate((gate_ref, up_ref))
    ]
    for load in loads:
        load.start()
    sources, height, wide = got_ref.shape
    groups = sources // 2
    half, side = height - 8, wide // 2
    slots = 2 * half
    per = out_ref.shape[1]
    total = groups * per

    for s in range(sources):
        g, d = s // 2, s % 2
        block = got_ref[s, 0:half, :]
        padded_ref[g * slots : g * slots + half, d * side : (d + 1) * side] = block[:, 0:side]
        padded_ref[g * slots + half : (g + 1) * slots, d * side : (d + 1) * side] = block[:, side:]
    at = half
    counts = [got_ref[2 * g, at : at + 8, 0 : 2 * slots].astype(F32)[0:1] for g in range(groups)]

    row = lax.broadcasted_iota(jnp.int32, (total, 2 * slots), 0)
    lane = lax.broadcasted_iota(jnp.int32, (total, 2 * slots), 1)
    second = lane >= slots
    slot = jnp.where(second, lane - slots, lane)
    slot_f = slot.astype(F32)
    shift = (row - slot).astype(F32)
    x = jnp.zeros((total, wide), F32)
    run = jnp.zeros_like(counts[0])
    for q in range(groups // 2):
        one, two = counts[2 * q], counts[2 * q + 1]
        start = jnp.where(second, run + one, run)
        count = jnp.where(second, two, one)
        run = run + one + two
        chosen = jnp.where((shift == start) & (slot_f < count), 1.0, 0.0).astype(BF)
        chosen_ref[:, 2 * q * slots : 2 * (q + 1) * slots] = chosen
        x = x + dot(chosen, padded_ref[2 * q * slots : 2 * (q + 1) * slots, :])

    square = jnp.sum(x * x, axis=1, keepdims=True)
    high = square.astype(BF)
    low = (square - high.astype(F32)).astype(BF)
    lane128 = lax.broadcasted_iota(jnp.int32, (total, 128), 1)
    squares = jnp.where(lane128 < 64, high.astype(F32), low.astype(F32)).astype(BF)
    scaled = (x * gain_ref[...]).astype(BF)
    rows_ref[...] = scaled
    for load in loads:
        load.wait()
    gate = dot(scaled, weights_ref[0]).astype(BF)
    up = dot(scaled, weights_ref[1]).astype(BF)
    at = 2 * wide + 128
    for g in range(groups):
        own = slice(g * per, (g + 1) * per)
        out_ref[g, :, 0:wide] = gate[own]
        out_ref[g, :, wide : 2 * wide] = up[own]
        out_ref[g, :, 2 * wide : at] = squares[own]


def hidden_kernel(
    features, got_ref, keep_ref, other_ref, p1, p2,
    out_ref, gate_ref, up_ref, scale_ref, q1, q2,
):
    per, wide = gate_ref.shape
    at = got_ref.shape[2]
    total = got_ref[0, :, 0:at].astype(F32)
    for g in range(1, got_ref.shape[0]):
        total = total + got_ref[g, :, 0:at].astype(F32)
    square = total[:, 2 * wide : 2 * wide + 1] + total[:, 2 * wide + 64 : 2 * wide + 65]
    scale = lax.rsqrt(square * (1.0 / features) + EPS)
    gate = total[:, 0:wide] * scale
    up = total[:, wide : 2 * wide] * scale
    gate_ref[...] = gate
    up_ref[...] = up
    scale_ref[...] = jnp.broadcast_to(scale, scale_ref.shape)
    hidden = (gate * jax.nn.sigmoid(gate) * up).astype(BF)
    routed = (keep_ref[0] + other_ref[0].astype(F32)).astype(BF)
    for g in range(out_ref.shape[0]):
        out_ref[g, 0:per, :] = hidden
        out_ref[g, per:, :] = routed


def down_kernel(
    group_ref, got_ref, down_ref, chosen_ref, projector_ref, after_ref,
    out_ref, hidden_ref, rows_ref,
):
    groups = got_ref.shape[0]
    per = hidden_ref.shape[0] // groups
    slots = got_ref.shape[1] - per
    for g in range(groups):
        hidden_ref[g * per : (g + 1) * per, :] = got_ref[g, 0:per, :]
        rows_ref[g * slots : (g + 1) * slots, :] = got_ref[g, per:, :]
    rows = dot(chosen_ref[...], rows_ref[...]).astype(BF)
    part = dot(hidden_ref[...], down_ref[...], 1, 1) - dot(rows, projector_ref[...])
    out_ref[...] = part.astype(BF).reshape(out_ref.shape)


def misfit_kernel(scale, got_ref, out_ref):
    total = got_ref[0].astype(F32)
    for s in range(1, got_ref.shape[0]):
        total = total + got_ref[s].astype(F32)
    grad = (total * scale).astype(BF)
    for s in range(out_ref.shape[0]):
        out_ref[s] = grad


def back_kernel(got_ref, down_ref, passed_ref, out_ref, same_ref):
    groups, per, wide = out_ref.shape
    part = dot(got_ref[...].reshape(groups * per, got_ref.shape[2]), down_ref[...])
    out_ref[...] = part.astype(BF).reshape(groups, per, wide)


def acts_kernel(got_ref, gate_ref, up_ref, scale_ref, out_ref):
    wide = gate_ref.shape[1]
    grad = got_ref[0].astype(F32)
    for g in range(1, got_ref.shape[0]):
        grad = grad + got_ref[g].astype(F32)
    grad = grad * scale_ref[:, 0:1]
    gate, up = gate_ref[...], up_ref[...]
    sigma = jax.nn.sigmoid(gate)
    grad_gate = (grad * up * sigma * (1.0 + gate * (1.0 - sigma))).astype(BF)
    grad_up = (grad * gate * sigma).astype(BF)
    for g in range(out_ref.shape[0]):
        out_ref[g, :, 0:wide] = grad_gate
        out_ref[g, :, wide : 2 * wide] = grad_up


def down_weights_kernel(grad_ref, hidden_ref, out_ref):
    rows, units = hidden_ref.shape
    out_ref[...] = dot(grad_ref[...].reshape(rows, out_ref.shape[0]), hidden_ref[...], 0, 0)


def weights_kernel(rows_ref, got_ref, gate_ref, up_ref):
    wide = gate_ref.shape[1]
    acts = got_ref[...].reshape(got_ref.shape[0] * got_ref.shape[1], 2 * wide)
    gate_ref[...] = dot(rows_ref[...], acts[:, 0:wide], 0, 0)
    up_ref[...] = dot(rows_ref[...], acts[:, wide:], 0, 0)


def on_device(
    attn_values,
    out_weight,
    residual_t,
    projector,
    student_input,
    norm_gain,
    w_gate,
    w_up,
    w_down,
    route_index,
):
    groups, parts = lax.axis_size("batch"), lax.axis_size("tensor")
    slots = route_index.shape[1]
    tokens, wide = attn_values.shape
    side = student_input.shape[1]
    features = norm_gain.shape[0]
    live = tokens * groups // 8
    per = live // groups
    units = w_gate.shape[1]
    extra = slots // 2 + 8
    group, part = lax.axis_index("batch"), lax.axis_index("tensor")
    core, x_at, y_at = part & 1, (part >> 1) & 3, part >> 3
    shape = jax.ShapeDtypeStruct
    vmem = pl.BlockSpec(memory_space=pltpu.VMEM)
    anywhere = pl.BlockSpec(memory_space=pl.ANY)

    def hbm(value):
        return pltpu.with_memory_space_constraint(value, pltpu.HBM)

    out_weight, w_gate, w_up, projector, student_input, route_index = (
        hbm(w) for w in (out_weight, w_gate, w_up, projector, student_input, route_index)
    )

    rows = pl.pallas_call(
        rows_kernel,
        out_shape=pltpu.HBM((extra, 2 * side), BF),
        cost_estimate=cost(2 * slots * tokens * side, MIB // 4),
        compiler_params=params(4),
        name="rows",
    )(route_index, student_input)
    pairs = [
        (b * parts + t, (t // 2) * parts + 2 * b + t % 2)
        for b in range(groups)
        for t in range(parts)
    ]
    rows = lax.ppermute(rows, ("batch", "tensor"), pairs)

    keep, send, keep_routed, send_routed = pl.pallas_call(
        teacher_kernel,
        grid_spec=pltpu.PrefetchScalarGridSpec(
            num_scalar_prefetch=1,
            grid=(parts // 2,),
            in_specs=[
                pl.BlockSpec(route_index.shape, lambda j, core: (0, 0)),
                pl.BlockSpec(attn_values.shape, lambda j, core: (0, 0)),
                pl.BlockSpec((wide, wide), lambda j, core: (0, 2 * j + core[0])),
                pl.BlockSpec((wide, wide), lambda j, core: (0, 2 * j + 1 - core[0])),
            ],
            out_specs=[pl.BlockSpec((1, tokens, wide), lambda j, core: (j, 0, 0))] * 2
            + [pl.BlockSpec((1, slots, wide), lambda j, core: (j, 0, 0))] * 2,
            scratch_shapes=[pltpu.VMEM((tokens + slots, wide), BF)],
        ),
        out_shape=[pltpu.HBM((parts // 2, tokens, wide), BF)] * 2
        + [pltpu.HBM((parts // 2, slots, wide), BF)] * 2,
        compiler_params=params(16),
        cost_estimate=cost(2 * (tokens + slots) * wide * wide * parts, 14 * MIB),
        name="teacher",
    )(core.reshape(1), route_index, hbm(attn_values), out_weight, out_weight)
    copies, send_routed, send = pl.pallas_call(
        copies_kernel,
        in_specs=[vmem] + [anywhere] * 2,
        out_specs=[anywhere] * 3,
        out_shape=[
            pltpu.HBM((parts, *rows.shape), BF),
            pltpu.HBM(send_routed.shape, BF),
            pltpu.HBM(send.shape, BF),
        ],
        scratch_shapes=[pltpu.SemaphoreType.DMA((parts,))],
        input_output_aliases={1: 1, 2: 2},
        compiler_params=params(4),
        cost_estimate=cost(0, MIB // 2),
        name="copies",
    )(rows, send_routed, send)
    every = lax.all_to_all(copies, "tensor", 0, 0, tiled=True)

    def along(value, move):
        return lax.ppermute(value, "tensor", [(t, move(t // 8, (t // 2) % 4, t % 2)) for t in range(parts)])

    def core_sum(keep, send, strip):
        got = along(send, lambda y, x, c: y * 8 + x * 2 + 1 - c)
        height = keep.shape[1]
        block = (1, strip, wide)
        return pl.pallas_call(
            core_sum_kernel,
            grid_spec=pltpu.PrefetchScalarGridSpec(
                num_scalar_prefetch=1,
                grid=(2, height // strip),
                in_specs=[
                    pl.BlockSpec(block, lambda y, i, x, j=j: (4 * y + ((x[0] + j) & 3), i, 0))
                    for j in range(4)
                ]
                * 2,
                out_specs=[pl.BlockSpec(block, lambda y, i, x: (y, i, 0))] * 4,
            ),
            out_shape=[pltpu.HBM((2, height, wide), BF)] * 4,
            compiler_params=params(16),
            cost_estimate=cost(MIB, 24 * height * wide * 2),
            name="core_sum",
        )(x_at.reshape(1), *[hbm(keep)] * 4, *[got] * 4)

    def along_x(own, moved):
        return [own] + [
            along(moved[j - 1], lambda y, x, c, j=j: y * 8 + (x + j) % 4 * 2 + c)
            for j in range(1, 4)
        ]

    def along_y(send):
        return along(send, lambda y, x, c: (1 - y) * 8 + x * 2 + c)

    def y_blocks(strip):
        block = (1, strip, wide)
        return [pl.BlockSpec(block, lambda i, y: (1 - y[0], i, 0))] * 4 + [
            pl.BlockSpec(block, lambda i, y: (y[0], i, 0))
        ] * 4

    half, strip = tokens // 2, tokens // 4
    got = along(send, lambda y, x, c: y * 8 + x * 2 + 1 - c)
    halves = (parts // 2, 2, half, wide)
    pair = pltpu.HBM((2, 2, half, wide), BF)
    keep_a, send_a, keep_b, send_b = pl.pallas_call(
        halves_kernel,
        grid_spec=pltpu.PrefetchScalarGridSpec(
            num_scalar_prefetch=1,
            grid=(2, half // strip),
            in_specs=[
                pl.BlockSpec(
                    (1, 2, strip, wide),
                    lambda y, n, x, m=m: (4 * y + lax.bitwise_xor(x[0], jnp.int32(m)), 0, n, 0),
                )
                for m in range(4)
            ]
            * 2,
            out_specs=[pl.BlockSpec((2, 1, strip, wide), lambda y, n, x: (0, y, n, 0))] * 4,
        ),
        out_shape=[pair] * 4,
        compiler_params=params(16),
        cost_estimate=cost(MIB, 6 * MIB),
        name="halves",
    )(x_at.reshape(1), *[hbm(keep.reshape(halves))] * 4, *[got.reshape(halves)] * 4)

    def along_x_by(value, mask):
        return along(value, lambda y, x, c: y * 8 + (x ^ mask) * 2 + c)

    packed = 2 * wide + 128
    sent, scaled, chosen = pl.pallas_call(
        up_kernel,
        grid_spec=pltpu.PrefetchScalarGridSpec(
            num_scalar_prefetch=1,
            grid=(1,),
            in_specs=[vmem, pl.BlockSpec((1, wide), lambda i, group: (0, group[0]))]
            + [anywhere] * 3,
            out_specs=[vmem] * 3,
            scratch_shapes=[
                pltpu.VMEM((groups * slots, wide), BF),
                pltpu.VMEM((2, wide, units), BF),
                pltpu.SemaphoreType.DMA((2,)),
            ],
        ),
        out_shape=[
            pltpu.HBM((groups, per, packed), BF),
            pltpu.HBM((live, wide), BF),
            pltpu.HBM((live, groups * slots), BF),
        ],
        compiler_params=params(16),
        cost_estimate=cost(800 * MIB, 4 * MIB),
        name="up",
    )(group.reshape(1), every, norm_gain[None], w_gate, w_up, hbm(keep_a))

    routed, *moved = core_sum(keep_routed, send_routed, slots)
    send_routed, keep_routed, sent, send_a, send_b = pl.pallas_call(
        routed_sum_kernel,
        grid_spec=pltpu.PrefetchScalarGridSpec(
            num_scalar_prefetch=1,
            grid=(1,),
            in_specs=[vmem] * 2 + [anywhere] * 3 + y_blocks(slots),
            out_specs=[pl.BlockSpec((1, slots, wide), lambda i, y: (0, 0, 0))] * 2
            + [anywhere] * 3,
        ),
        out_shape=[
            pltpu.HBM((1, slots, wide), BF),
            pltpu.HBM((1, slots, wide), F32),
            pltpu.HBM(sent.shape, BF),
        ]
        + [pair] * 2,
        input_output_aliases={3: 2, 4: 3, 5: 4},
        compiler_params=params(8),
        cost_estimate=cost(MIB, MIB),
        name="routed_sum",
    )(y_at.reshape(1), route_index, residual_t, sent, send_a, send_b, *along_x(routed, moved) * 2)
    other_routed = along_y(send_routed)

    got = lax.all_to_all(sent, "batch", 0, 0, tiled=True)

    flat = shape((per, units), F32)
    block = pl.BlockSpec((2, 2, strip, wide), lambda n: (0, 0, n, 0))
    line = pl.BlockSpec((2, strip, wide), lambda n: (0, n, 0))
    own_a, on_a, own_b, on_b = pl.pallas_call(
        first_sum_kernel,
        grid=(half // strip,),
        in_specs=[block] * 4,
        out_specs=[line] * 4,
        out_shape=[pltpu.HBM((2, half, wide), F32), pltpu.HBM((2, half, wide), BF)] * 2,
        compiler_params=params(16),
        cost_estimate=cost(MIB, 3 * MIB),
        name="first_sum",
    )(keep_a, along_x_by(send_a, 1), keep_b, along_x_by(send_b, 3))
    both, gate, up, scale, on_a, on_b = pl.pallas_call(
        lambda *refs: hidden_kernel(features, *refs),
        in_specs=[vmem] * 3 + [anywhere] * 2,
        out_specs=[vmem] * 4 + [anywhere] * 2,
        out_shape=[
            pltpu.HBM((groups, per + slots, units), BF),
            flat,
            flat,
            shape((per, 128), F32),
        ]
        + [pltpu.HBM((2, half, wide), BF)] * 2,
        input_output_aliases={3: 4, 4: 5},
        compiler_params=params(8),
        cost_estimate=cost(MIB, MIB),
        name="hidden",
    )(got, keep_routed, other_routed, on_a, on_b)
    got_a, got_b = along_x_by(on_a, 3), along_x_by(on_b, 1)
    here = pl.BlockSpec((1, strip, wide), lambda n, y: (y[0], n, 0))
    there = pl.BlockSpec((1, strip, wide), lambda n, y: (1 - y[0], n, 0))
    send, keep = pl.pallas_call(
        second_sum_kernel,
        grid_spec=pltpu.PrefetchScalarGridSpec(
            num_scalar_prefetch=1,
            grid=(half // strip,),
            in_specs=[here, here, there, there] * 2,
            out_specs=[pl.BlockSpec((2, strip, wide), lambda n, y: (0, n, 0))] * 2,
        ),
        out_shape=[pltpu.HBM((2, half, wide), BF), pltpu.HBM((2, half, wide), F32)],
        compiler_params=params(16),
        cost_estimate=cost(MIB, 3 * MIB),
        name="second_sum",
    )(y_at.reshape(1), *[own_a, got_a] * 2, *[own_b, got_b] * 2)
    other = along_y(send)
    both = lax.all_to_all(both, "batch", 0, 0, tiled=True)
    misfit, hidden = pl.pallas_call(
        down_kernel,
        grid_spec=pltpu.PrefetchScalarGridSpec(
            num_scalar_prefetch=1,
            grid=(1,),
            in_specs=[vmem] * 3
            + [pl.BlockSpec((wide, wide), lambda i, group: (0, group[0])), anywhere],
            out_specs=[vmem] * 2,
            scratch_shapes=[pltpu.VMEM((groups * slots, wide), BF)],
        ),
        out_shape=[
            pltpu.HBM((parts, live // parts, wide), BF),
            pltpu.HBM((live, units), BF),
        ],
        compiler_params=params(16),
        cost_estimate=cost(768 * MIB, 4 * MIB),
        name="down",
    )(group.reshape(1), both, w_down, chosen, projector, hbm(keep))
    misfit = lax.all_to_all(misfit, "tensor", 0, 0, tiled=True)
    loss_scale = 1.0 / math.sqrt(live)
    grad_out = pl.pallas_call(
        lambda *refs: misfit_kernel(loss_scale, *refs),
        out_shape=pltpu.HBM(misfit.shape, BF),
        compiler_params=params(8),
        cost_estimate=cost(MIB, MIB),
        name="misfit",
    )(misfit)
    grad_out = lax.all_to_all(grad_out, "tensor", 0, 0, tiled=True)

    teacher_hidden = pl.pallas_call(
        residual_kernel,
        out_shape=pltpu.HBM(residual_t.shape, BF),
        compiler_params=params(8),
        cost_estimate=cost(MIB, 2 * MIB),
        name="residual",
    )(residual_t, keep, other)
    back, teacher_hidden = pl.pallas_call(
        back_kernel,
        in_specs=[vmem] * 2 + [anywhere],
        out_specs=[vmem, anywhere],
        out_shape=[shape((groups, per, units), BF), pltpu.HBM(residual_t.shape, BF)],
        input_output_aliases={2: 1},
        compiler_params=params(16),
        cost_estimate=cost(256 * MIB, MIB),
        name="back",
    )(grad_out, w_down, teacher_hidden)
    back = lax.all_to_all(back, "batch", 0, 0, tiled=True)
    acts = pl.pallas_call(
        acts_kernel,
        out_shape=pltpu.HBM((groups, per, 2 * units), BF),
        compiler_params=params(8),
        cost_estimate=cost(MIB, MIB),
        name="acts",
    )(back, gate, up, scale)
    acts = lax.all_to_all(acts, "batch", 0, 0, tiled=True)
    grad_down = pl.pallas_call(
        down_weights_kernel,
        out_shape=shape((wide, units), F32),
        compiler_params=params(16),
        cost_estimate=cost(256 * MIB, 2 * MIB),
        name="down_weights",
    )(grad_out, hidden)
    grad_gate, grad_up = pl.pallas_call(
        weights_kernel,
        out_shape=[shape((wide, units), F32)] * 2,
        compiler_params=params(16),
        cost_estimate=cost(512 * MIB, 4 * MIB),
        name="weights",
    )(scaled, acts)
    return teacher_hidden, grad_gate, grad_up, grad_down


def solution(mesh):
    in_specs = (
        P("batch", "tensor"),
        P("tensor", None),
        P("tensor", "batch"),
        P("tensor", None),
        P("batch", "tensor"),
        P(),
        P("batch", "tensor"),
        P("batch", "tensor"),
        P("batch", "tensor"),
        P("batch", None),
    )
    out_specs = (P("tensor", "batch"),) + (P("batch", "tensor"),) * 3
    return jax.shard_map(
        on_device, mesh=mesh, in_specs=in_specs, out_specs=out_specs, check_vma=False
    )
```

```python
import math

import jax
import jax.numpy as jnp
from jax import lax
from jax.experimental import pallas as pl
from jax.experimental.pallas import tpu as pltpu
from jax.sharding import PartitionSpec as P

EPS = 1e-05
BF = jnp.bfloat16
F32 = jnp.float32
MIB = 1 << 20


def params(mib):
    return pltpu.CompilerParams(vmem_limit_bytes=mib * MIB)


def cost(flops, nbytes):
    return pl.CostEstimate(flops=flops // 1024, bytes_accessed=nbytes // 1024, transcendentals=0)


def dot(a, b, ca=1, cb=0):
    return lax.dot_general(a, b, (((ca,), (cb,)), ((), ())), preferred_element_type=F32)


def whole(shape):
    return pl.BlockSpec(shape, lambda *_: (0,) * len(shape))


def slot_rows(route, tokens):
    slots = route.shape[1]
    grid = (slots, slots)
    diagonal = lax.broadcasted_iota(jnp.int32, grid, 0) == lax.broadcasted_iota(jnp.int32, grid, 1)
    spread = jnp.broadcast_to(route.astype(F32), grid)
    column = jnp.sum(jnp.where(diagonal, spread, 0.0), axis=1, keepdims=True)
    lane = lax.broadcasted_iota(jnp.int32, (slots, tokens), 1).astype(F32)
    return jnp.where(lane == column, 1.0, 0.0).astype(BF)


def rows_kernel(route_ref, x_ref, out_ref):
    route = route_ref[...]
    slots, wide = route.shape[1], x_ref.shape[1]
    rows = dot(slot_rows(route, x_ref.shape[0]), x_ref[...]).astype(BF)
    half = slots // 2
    out_ref[0:half, 0:wide] = rows[0:half]
    out_ref[0:half, wide : 2 * wide] = rows[half:]
    live = jnp.sum(jnp.where(route >= 0, 1.0, 0.0), axis=1, keepdims=True)
    out_ref[half : half + 8, :] = jnp.broadcast_to(live, (8, 2 * wide)).astype(BF)


def teacher_kernel(
    core_ref, route_ref, attn_ref, weight_ref,
    keep_ref, send_ref, keep_routed_ref, send_routed_ref, left_ref, blocks_ref, sems,
):
    step = pl.program_id(0)
    tokens, wide = attn_ref.shape

    def load(i, first):
        source = weight_ref.at[:, pl.ds(first, wide)]
        return pltpu.make_async_copy(source, blocks_ref.at[i], sems.at[i])

    @pl.when(step == 0)
    def _():
        for i in range(blocks_ref.shape[0]):
            load(i, i * wide).start()
        left_ref[0:tokens, :] = attn_ref[...]
        left_ref[tokens:, :] = dot(slot_rows(route_ref[...], tokens), attn_ref[...]).astype(BF)

    for i in (2 * step, 2 * step + 1):
        load(i, pl.multiple_of(i * wide, wide)).wait()
    core = core_ref[0]
    for place, out_ref, routed_ref in (
        (1 - core, send_ref, send_routed_ref),
        (core, keep_ref, keep_routed_ref),
    ):
        product = dot(left_ref[...], blocks_ref[2 * step + place]).astype(BF)
        out_ref[0] = product[0:tokens]
        routed_ref[0] = product[tokens:]


def copies_kernel(rows_ref, p1, p2, out_ref, q1, q2, sems):
    copies = [
        pltpu.make_async_copy(rows_ref, out_ref.at[s], sems.at[s]) for s in range(out_ref.shape[0])
    ]
    for copy in copies:
        copy.start()
    for copy in copies:
        copy.wait()


def core_sum_kernel(x_ref, *refs):
    ways = len(refs) // 3
    for j in range(ways):
        total = refs[j][...].astype(F32) + refs[ways + j][...].astype(F32)
        refs[2 * ways + j][...] = total.astype(BF).reshape(refs[2 * ways + j].shape)


def x_sum_kernel(*refs):
    total = refs[0][...].astype(F32)
    for ref in refs[1:-1]:
        total = total + ref[...].astype(F32)
    refs[-1][...] = total.astype(refs[-1].dtype)


def routed_sum_kernel(y_ref, route_ref, residual_ref, p1, p2, p3, *refs):
    ins, (send_ref, keep_ref) = refs[:8], refs[8:10]
    x_sum_kernel(*ins[:4], send_ref)
    x_sum_kernel(*ins[4:], keep_ref)
    hot = slot_rows(route_ref[...], residual_ref.shape[1])
    keep_ref[0] = keep_ref[0] + dot(hot, residual_ref[...], 1, 1)


def halves_kernel(x_ref, *refs):
    ins, (keep_a, send_a, keep_b, send_b) = refs[:8], refs[8:]
    sums = [(ins[m][0].astype(F32) + ins[4 + m][0].astype(F32)).astype(BF) for m in range(4)]
    for half, ref, order in ((0, keep_a, (0, 3)), (0, send_a, (1, 2)), (1, keep_b, (0, 1)), (1, send_b, (3, 2))):
        for i, m in enumerate(order):
            ref[i, 0] = sums[m][half]


def first_sum_kernel(keep_a, got_a, keep_b, got_b, own_a, on_a, own_b, on_b):
    for keep, got, own, on in ((keep_a, got_a, own_a, on_a), (keep_b, got_b, own_b, on_b)):
        own[...] = keep[0].astype(F32) + got[0].astype(F32)
        on[...] = (keep[1].astype(F32) + got[1].astype(F32)).astype(BF)


def second_sum_kernel(y_ref, *refs):
    ins, (send_ref, keep_ref) = refs[:8], refs[8:]
    for half in range(2):
        own, got, other_own, other_got = ins[4 * half : 4 * half + 4]
        send_ref[half] = (other_own[0] + other_got[0].astype(F32)).astype(BF)
        keep_ref[half] = own[0] + got[0].astype(F32)


def residual_kernel(residual_ref, keep_ref, got_ref, out_ref):
    summed = (keep_ref[...] + got_ref[...].astype(F32)).reshape(-1, keep_ref.shape[2])
    out_ref[...] = (residual_ref[...].astype(F32) + summed.T).astype(BF)


def up_kernel(
    group_ref, got_ref, gain_ref, gate_ref, up_ref, after_ref,
    out_ref, rows_ref, chosen_ref, padded_ref, weights_ref, sems,
):
    loads = [
        pltpu.make_async_copy(ref, weights_ref.at[i], sems.at[i])
        for i, ref in enumerate((gate_ref, up_ref))
    ]
    for load in loads:
        load.start()
    sources, height, wide = got_ref.shape
    groups = sources // 2
    half, side = height - 8, wide // 2
    slots = 2 * half
    per = out_ref.shape[1]
    total = groups * per

    for s in range(sources):
        g, d = s // 2, s % 2
        block = got_ref[s, 0:half, :]
        padded_ref[g * slots : g * slots + half, d * side : (d + 1) * side] = block[:, 0:side]
        padded_ref[g * slots + half : (g + 1) * slots, d * side : (d + 1) * side] = block[:, side:]
    at = half
    counts = [got_ref[2 * g, at : at + 8, 0 : 2 * slots].astype(F32)[0:1] for g in range(groups)]

    row = lax.broadcasted_iota(jnp.int32, (total, 2 * slots), 0)
    lane = lax.broadcasted_iota(jnp.int32, (total, 2 * slots), 1)
    second = lane >= slots
    slot = jnp.where(second, lane - slots, lane)
    slot_f = slot.astype(F32)
    shift = (row - slot).astype(F32)
    x = jnp.zeros((total, wide), F32)
    run = jnp.zeros_like(counts[0])
    for q in range(groups // 2):
        one, two = counts[2 * q], counts[2 * q + 1]
        start = jnp.where(second, run + one, run)
        count = jnp.where(second, two, one)
        run = run + one + two
        chosen = jnp.where((shift == start) & (slot_f < count), 1.0, 0.0).astype(BF)
        chosen_ref[:, 2 * q * slots : 2 * (q + 1) * slots] = chosen
        x = x + dot(chosen, padded_ref[2 * q * slots : 2 * (q + 1) * slots, :])

    square = jnp.sum(x * x, axis=1, keepdims=True)
    high = square.astype(BF)
    low = (square - high.astype(F32)).astype(BF)
    lane128 = lax.broadcasted_iota(jnp.int32, (total, 128), 1)
    squares = jnp.where(lane128 < 64, high.astype(F32), low.astype(F32)).astype(BF)
    scaled = (x * gain_ref[...]).astype(BF)
    rows_ref[...] = scaled
    for load in loads:
        load.wait()
    gate = dot(scaled, weights_ref[0]).astype(BF)
    up = dot(scaled, weights_ref[1]).astype(BF)
    at = 2 * wide + 128
    for g in range(groups):
        own = slice(g * per, (g + 1) * per)
        out_ref[g, :, 0:wide] = gate[own]
        out_ref[g, :, wide : 2 * wide] = up[own]
        out_ref[g, :, 2 * wide : at] = squares[own]


def hidden_kernel(
    features, got_ref, keep_ref, other_ref, p1, p2,
    out_ref, gate_ref, up_ref, scale_ref, q1, q2,
):
    per, wide = gate_ref.shape
    at = got_ref.shape[2]
    total = got_ref[0, :, 0:at].astype(F32)
    for g in range(1, got_ref.shape[0]):
        total = total + got_ref[g, :, 0:at].astype(F32)
    square = total[:, 2 * wide : 2 * wide + 1] + total[:, 2 * wide + 64 : 2 * wide + 65]
    scale = lax.rsqrt(square * (1.0 / features) + EPS)
    gate = total[:, 0:wide] * scale
    up = total[:, wide : 2 * wide] * scale
    gate_ref[...] = gate
    up_ref[...] = up
    scale_ref[...] = jnp.broadcast_to(scale, scale_ref.shape)
    hidden = (gate * jax.nn.sigmoid(gate) * up).astype(BF)
    routed = (keep_ref[0] + other_ref[0].astype(F32)).astype(BF)
    for g in range(out_ref.shape[0]):
        out_ref[g, 0:per, :] = hidden
        out_ref[g, per:, :] = routed


def down_kernel(
    group_ref, got_ref, down_ref, chosen_ref, projector_ref, after_ref,
    out_ref, hidden_ref, rows_ref,
):
    groups = got_ref.shape[0]
    per = hidden_ref.shape[0] // groups
    slots = got_ref.shape[1] - per
    for g in range(groups):
        hidden_ref[g * per : (g + 1) * per, :] = got_ref[g, 0:per, :]
        rows_ref[g * slots : (g + 1) * slots, :] = got_ref[g, per:, :]
    rows = dot(chosen_ref[...], rows_ref[...]).astype(BF)
    part = dot(hidden_ref[...], down_ref[...], 1, 1) - dot(rows, projector_ref[...])
    out_ref[...] = part.astype(BF).reshape(out_ref.shape)


def misfit_kernel(scale, got_ref, out_ref):
    total = got_ref[0].astype(F32)
    for s in range(1, got_ref.shape[0]):
        total = total + got_ref[s].astype(F32)
    grad = (total * scale).astype(BF)
    for s in range(out_ref.shape[0]):
        out_ref[s] = grad


def back_kernel(got_ref, down_ref, passed_ref, out_ref, same_ref):
    groups, per, wide = out_ref.shape
    part = dot(got_ref[...].reshape(groups * per, got_ref.shape[2]), down_ref[...])
    out_ref[...] = part.astype(BF).reshape(groups, per, wide)


def acts_kernel(got_ref, gate_ref, up_ref, scale_ref, out_ref):
    wide = gate_ref.shape[1]
    grad = got_ref[0].astype(F32)
    for g in range(1, got_ref.shape[0]):
        grad = grad + got_ref[g].astype(F32)
    grad = grad * scale_ref[:, 0:1]
    gate, up = gate_ref[...], up_ref[...]
    sigma = jax.nn.sigmoid(gate)
    grad_gate = (grad * up * sigma * (1.0 + gate * (1.0 - sigma))).astype(BF)
    grad_up = (grad * gate * sigma).astype(BF)
    for g in range(out_ref.shape[0]):
        out_ref[g, :, 0:wide] = grad_gate
        out_ref[g, :, wide : 2 * wide] = grad_up


def down_weights_kernel(grad_ref, hidden_ref, out_ref):
    rows, units = hidden_ref.shape
    out_ref[...] = dot(grad_ref[...].reshape(rows, out_ref.shape[0]), hidden_ref[...], 0, 0)


def weights_kernel(rows_ref, got_ref, gate_ref, up_ref):
    wide = gate_ref.shape[1]
    acts = got_ref[...].reshape(got_ref.shape[0] * got_ref.shape[1], 2 * wide)
    gate_ref[...] = dot(rows_ref[...], acts[:, 0:wide], 0, 0)
    up_ref[...] = dot(rows_ref[...], acts[:, wide:], 0, 0)


def on_device(
    attn_values,
    out_weight,
    residual_t,
    projector,
    student_input,
    norm_gain,
    w_gate,
    w_up,
    w_down,
    route_index,
):
    groups, parts = lax.axis_size("batch"), lax.axis_size("tensor")
    slots = route_index.shape[1]
    tokens, wide = attn_values.shape
    side = student_input.shape[1]
    features = norm_gain.shape[0]
    live = tokens * groups // 8
    per = live // groups
    units = w_gate.shape[1]
    extra = slots // 2 + 8
    group, part = lax.axis_index("batch"), lax.axis_index("tensor")
    core, x_at, y_at = part & 1, (part >> 1) & 3, part >> 3
    shape = jax.ShapeDtypeStruct
    vmem = pl.BlockSpec(memory_space=pltpu.VMEM)
    anywhere = pl.BlockSpec(memory_space=pl.ANY)

    def hbm(value):
        return pltpu.with_memory_space_constraint(value, pltpu.HBM)

    out_weight, w_gate, w_up, projector, student_input, route_index = (
        hbm(w) for w in (out_weight, w_gate, w_up, projector, student_input, route_index)
    )

    rows = pl.pallas_call(
        rows_kernel,
        out_shape=pltpu.HBM((extra, 2 * side), BF),
        cost_estimate=cost(2 * slots * tokens * side, MIB // 4),
        compiler_params=params(4),
        name="rows",
    )(route_index, student_input)
    pairs = [
        (b * parts + t, (t // 2) * parts + 2 * b + t % 2)
        for b in range(groups)
        for t in range(parts)
    ]
    rows = lax.ppermute(rows, ("batch", "tensor"), pairs)

    keep, send, keep_routed, send_routed = pl.pallas_call(
        teacher_kernel,
        grid_spec=pltpu.PrefetchScalarGridSpec(
            num_scalar_prefetch=1,
            grid=(parts // 2,),
            in_specs=[
                pl.BlockSpec(route_index.shape, lambda j, core: (0, 0)),
                pl.BlockSpec(attn_values.shape, lambda j, core: (0, 0)),
                anywhere,
            ],
            out_specs=[pl.BlockSpec((1, tokens, wide), lambda j, core: (j, 0, 0))] * 2
            + [pl.BlockSpec((1, slots, wide), lambda j, core: (j, 0, 0))] * 2,
            scratch_shapes=[
                pltpu.VMEM((tokens + slots, wide), BF),
                pltpu.VMEM((parts, wide, wide), BF),
                pltpu.SemaphoreType.DMA((parts,)),
            ],
        ),
        out_shape=[pltpu.HBM((parts // 2, tokens, wide), BF)] * 2
        + [pltpu.HBM((parts // 2, slots, wide), BF)] * 2,
        compiler_params=params(20),
        cost_estimate=cost(2 * (tokens + slots) * wide * wide * parts, 14 * MIB),
        name="teacher",
    )(core.reshape(1), route_index, hbm(attn_values), out_weight)
    copies, send_routed, send = pl.pallas_call(
        copies_kernel,
        in_specs=[vmem] + [anywhere] * 2,
        out_specs=[anywhere] * 3,
        out_shape=[
            pltpu.HBM((parts, *rows.shape), BF),
            pltpu.HBM(send_routed.shape, BF),
            pltpu.HBM(send.shape, BF),
        ],
        scratch_shapes=[pltpu.SemaphoreType.DMA((parts,))],
        input_output_aliases={1: 1, 2: 2},
        compiler_params=params(4),
        cost_estimate=cost(0, MIB // 2),
        name="copies",
    )(rows, send_routed, send)
    every = lax.all_to_all(copies, "tensor", 0, 0, tiled=True)

    def along(value, move):
        return lax.ppermute(value, "tensor", [(t, move(t // 8, (t // 2) % 4, t % 2)) for t in range(parts)])

    def core_sum(keep, send, strip):
        got = along(send, lambda y, x, c: y * 8 + x * 2 + 1 - c)
        height = keep.shape[1]
        block = (1, strip, wide)
        return pl.pallas_call(
            core_sum_kernel,
            grid_spec=pltpu.PrefetchScalarGridSpec(
                num_scalar_prefetch=1,
                grid=(2, height // strip),
                in_specs=[
                    pl.BlockSpec(block, lambda y, i, x, j=j: (4 * y + ((x[0] + j) & 3), i, 0))
                    for j in range(4)
                ]
                * 2,
                out_specs=[pl.BlockSpec(block, lambda y, i, x: (y, i, 0))] * 4,
            ),
            out_shape=[pltpu.HBM((2, height, wide), BF)] * 4,
            compiler_params=params(16),
            cost_estimate=cost(MIB, 24 * height * wide * 2),
            name="core_sum",
        )(x_at.reshape(1), *[hbm(keep)] * 4, *[got] * 4)

    def along_x(own, moved):
        return [own] + [
            along(moved[j - 1], lambda y, x, c, j=j: y * 8 + (x + j) % 4 * 2 + c)
            for j in range(1, 4)
        ]

    def along_y(send):
        return along(send, lambda y, x, c: (1 - y) * 8 + x * 2 + c)

    def y_blocks(strip):
        block = (1, strip, wide)
        return [pl.BlockSpec(block, lambda i, y: (1 - y[0], i, 0))] * 4 + [
            pl.BlockSpec(block, lambda i, y: (y[0], i, 0))
        ] * 4

    half, strip = tokens // 2, tokens // 4
    got = along(send, lambda y, x, c: y * 8 + x * 2 + 1 - c)
    halves = (parts // 2, 2, half, wide)
    pair = pltpu.HBM((2, 2, half, wide), BF)
    keep_a, send_a, keep_b, send_b = pl.pallas_call(
        halves_kernel,
        grid_spec=pltpu.PrefetchScalarGridSpec(
            num_scalar_prefetch=1,
            grid=(2, half // strip),
            in_specs=[
                pl.BlockSpec(
                    (1, 2, strip, wide),
                    lambda y, n, x, m=m: (4 * y + lax.bitwise_xor(x[0], jnp.int32(m)), 0, n, 0),
                )
                for m in range(4)
            ]
            * 2,
            out_specs=[pl.BlockSpec((2, 1, strip, wide), lambda y, n, x: (0, y, n, 0))] * 4,
        ),
        out_shape=[pair] * 4,
        compiler_params=params(16),
        cost_estimate=cost(MIB, 6 * MIB),
        name="halves",
    )(x_at.reshape(1), *[hbm(keep.reshape(halves))] * 4, *[got.reshape(halves)] * 4)

    def along_x_by(value, mask):
        return along(value, lambda y, x, c: y * 8 + (x ^ mask) * 2 + c)

    packed = 2 * wide + 128
    sent, scaled, chosen = pl.pallas_call(
        up_kernel,
        grid_spec=pltpu.PrefetchScalarGridSpec(
            num_scalar_prefetch=1,
            grid=(1,),
            in_specs=[vmem, pl.BlockSpec((1, wide), lambda i, group: (0, group[0]))]
            + [anywhere] * 3,
            out_specs=[vmem] * 3,
            scratch_shapes=[
                pltpu.VMEM((groups * slots, wide), BF),
                pltpu.VMEM((2, wide, units), BF),
                pltpu.SemaphoreType.DMA((2,)),
            ],
        ),
        out_shape=[
            pltpu.HBM((groups, per, packed), BF),
            pltpu.HBM((live, wide), BF),
            pltpu.HBM((live, groups * slots), BF),
        ],
        compiler_params=params(16),
        cost_estimate=cost(800 * MIB, 4 * MIB),
        name="up",
    )(group.reshape(1), every, norm_gain[None], w_gate, w_up, hbm(keep_a))

    routed, *moved = core_sum(keep_routed, send_routed, slots)
    send_routed, keep_routed, sent, send_a, send_b = pl.pallas_call(
        routed_sum_kernel,
        grid_spec=pltpu.PrefetchScalarGridSpec(
            num_scalar_prefetch=1,
            grid=(1,),
            in_specs=[vmem] * 2 + [anywhere] * 3 + y_blocks(slots),
            out_specs=[pl.BlockSpec((1, slots, wide), lambda i, y: (0, 0, 0))] * 2
            + [anywhere] * 3,
        ),
        out_shape=[
            pltpu.HBM((1, slots, wide), BF),
            pltpu.HBM((1, slots, wide), F32),
            pltpu.HBM(sent.shape, BF),
        ]
        + [pair] * 2,
        input_output_aliases={3: 2, 4: 3, 5: 4},
        compiler_params=params(8),
        cost_estimate=cost(MIB, MIB),
        name="routed_sum",
    )(y_at.reshape(1), route_index, residual_t, sent, send_a, send_b, *along_x(routed, moved) * 2)
    other_routed = along_y(send_routed)

    got = lax.all_to_all(sent, "batch", 0, 0, tiled=True)

    flat = shape((per, units), F32)
    block = pl.BlockSpec((2, 2, strip, wide), lambda n: (0, 0, n, 0))
    line = pl.BlockSpec((2, strip, wide), lambda n: (0, n, 0))
    own_a, on_a, own_b, on_b = pl.pallas_call(
        first_sum_kernel,
        grid=(half // strip,),
        in_specs=[block] * 4,
        out_specs=[line] * 4,
        out_shape=[pltpu.HBM((2, half, wide), F32), pltpu.HBM((2, half, wide), BF)] * 2,
        compiler_params=params(16),
        cost_estimate=cost(MIB, 3 * MIB),
        name="first_sum",
    )(keep_a, along_x_by(send_a, 1), keep_b, along_x_by(send_b, 3))
    both, gate, up, scale, on_a, on_b = pl.pallas_call(
        lambda *refs: hidden_kernel(features, *refs),
        in_specs=[vmem] * 3 + [anywhere] * 2,
        out_specs=[vmem] * 4 + [anywhere] * 2,
        out_shape=[
            pltpu.HBM((groups, per + slots, units), BF),
            flat,
            flat,
            shape((per, 128), F32),
        ]
        + [pltpu.HBM((2, half, wide), BF)] * 2,
        input_output_aliases={3: 4, 4: 5},
        compiler_params=params(8),
        cost_estimate=cost(MIB, MIB),
        name="hidden",
    )(got, keep_routed, other_routed, on_a, on_b)
    got_a, got_b = along_x_by(on_a, 3), along_x_by(on_b, 1)
    here = pl.BlockSpec((1, strip, wide), lambda n, y: (y[0], n, 0))
    there = pl.BlockSpec((1, strip, wide), lambda n, y: (1 - y[0], n, 0))
    send, keep = pl.pallas_call(
        second_sum_kernel,
        grid_spec=pltpu.PrefetchScalarGridSpec(
            num_scalar_prefetch=1,
            grid=(half // strip,),
            in_specs=[here, here, there, there] * 2,
            out_specs=[pl.BlockSpec((2, strip, wide), lambda n, y: (0, n, 0))] * 2,
        ),
        out_shape=[pltpu.HBM((2, half, wide), BF), pltpu.HBM((2, half, wide), F32)],
        compiler_params=params(16),
        cost_estimate=cost(MIB, 3 * MIB),
        name="second_sum",
    )(y_at.reshape(1), *[own_a, got_a] * 2, *[own_b, got_b] * 2)
    other = along_y(send)
    both = lax.all_to_all(both, "batch", 0, 0, tiled=True)
    misfit, hidden = pl.pallas_call(
        down_kernel,
        grid_spec=pltpu.PrefetchScalarGridSpec(
            num_scalar_prefetch=1,
            grid=(1,),
            in_specs=[vmem] * 3
            + [pl.BlockSpec((wide, wide), lambda i, group: (0, group[0])), anywhere],
            out_specs=[vmem] * 2,
            scratch_shapes=[pltpu.VMEM((groups * slots, wide), BF)],
        ),
        out_shape=[
            pltpu.HBM((parts, live // parts, wide), BF),
            pltpu.HBM((live, units), BF),
        ],
        compiler_params=params(16),
        cost_estimate=cost(768 * MIB, 4 * MIB),
        name="down",
    )(group.reshape(1), both, w_down, chosen, projector, hbm(keep))
    misfit = lax.all_to_all(misfit, "tensor", 0, 0, tiled=True)
    loss_scale = 1.0 / math.sqrt(live)
    grad_out = pl.pallas_call(
        lambda *refs: misfit_kernel(loss_scale, *refs),
        out_shape=pltpu.HBM(misfit.shape, BF),
        compiler_params=params(8),
        cost_estimate=cost(MIB, MIB),
        name="misfit",
    )(misfit)
    grad_out = lax.all_to_all(grad_out, "tensor", 0, 0, tiled=True)

    teacher_hidden = pl.pallas_call(
        residual_kernel,
        out_shape=pltpu.HBM(residual_t.shape, BF),
        compiler_params=params(8),
        cost_estimate=cost(MIB, 2 * MIB),
        name="residual",
    )(residual_t, keep, other)
    back, teacher_hidden = pl.pallas_call(
        back_kernel,
        in_specs=[vmem] * 2 + [anywhere],
        out_specs=[vmem, anywhere],
        out_shape=[shape((groups, per, units), BF), pltpu.HBM(residual_t.shape, BF)],
        input_output_aliases={2: 1},
        compiler_params=params(16),
        cost_estimate=cost(256 * MIB, MIB),
        name="back",
    )(grad_out, w_down, teacher_hidden)
    back = lax.all_to_all(back, "batch", 0, 0, tiled=True)
    acts = pl.pallas_call(
        acts_kernel,
        out_shape=pltpu.HBM((groups, per, 2 * units), BF),
        compiler_params=params(8),
        cost_estimate=cost(MIB, MIB),
        name="acts",
    )(back, gate, up, scale)
    acts = lax.all_to_all(acts, "batch", 0, 0, tiled=True)
    grad_down = pl.pallas_call(
        down_weights_kernel,
        out_shape=shape((wide, units), F32),
        compiler_params=params(16),
        cost_estimate=cost(256 * MIB, 2 * MIB),
        name="down_weights",
    )(grad_out, hidden)
    grad_gate, grad_up = pl.pallas_call(
        weights_kernel,
        out_shape=[shape((wide, units), F32)] * 2,
        compiler_params=params(16),
        cost_estimate=cost(512 * MIB, 4 * MIB),
        name="weights",
    )(scaled, acts)
    return teacher_hidden, grad_gate, grad_up, grad_down


def solution(mesh):
    in_specs = (
        P("batch", "tensor"),
        P("tensor", None),
        P("tensor", "batch"),
        P("tensor", None),
        P("batch", "tensor"),
        P(),
        P("batch", "tensor"),
        P("batch", "tensor"),
        P("batch", "tensor"),
        P("batch", None),
    )
    out_specs = (P("tensor", "batch"),) + (P("batch", "tensor"),) * 3
    return jax.shard_map(
        on_device, mesh=mesh, in_specs=in_specs, out_specs=out_specs, check_vma=False
    )
```

```python
import math

import jax
import jax.numpy as jnp
from jax import lax
from jax.experimental import pallas as pl
from jax.experimental.pallas import tpu as pltpu
from jax.sharding import PartitionSpec as P

EPS = 1e-05
BF = jnp.bfloat16
F32 = jnp.float32
MIB = 1 << 20


def params(mib):
    return pltpu.CompilerParams(vmem_limit_bytes=mib * MIB)


def cost(flops, nbytes):
    return pl.CostEstimate(flops=flops // 1024, bytes_accessed=nbytes // 1024, transcendentals=0)


def dot(a, b, ca=1, cb=0):
    return lax.dot_general(a, b, (((ca,), (cb,)), ((), ())), preferred_element_type=F32)


def whole(shape):
    return pl.BlockSpec(shape, lambda *_: (0,) * len(shape))


def slot_rows(route, tokens):
    slots = route.shape[1]
    grid = (slots, slots)
    diagonal = lax.broadcasted_iota(jnp.int32, grid, 0) == lax.broadcasted_iota(jnp.int32, grid, 1)
    spread = jnp.broadcast_to(route.astype(F32), grid)
    column = jnp.sum(jnp.where(diagonal, spread, 0.0), axis=1, keepdims=True)
    lane = lax.broadcasted_iota(jnp.int32, (slots, tokens), 1).astype(F32)
    return jnp.where(lane == column, 1.0, 0.0).astype(BF)


def rows_kernel(route_ref, x_ref, out_ref):
    route = route_ref[...]
    slots, wide = route.shape[1], x_ref.shape[1]
    rows = dot(slot_rows(route, x_ref.shape[0]), x_ref[...]).astype(BF)
    half = slots // 2
    out_ref[0:half, 0:wide] = rows[0:half]
    out_ref[0:half, wide : 2 * wide] = rows[half:]
    live = jnp.sum(jnp.where(route >= 0, 1.0, 0.0), axis=1, keepdims=True)
    out_ref[half : half + 8, :] = jnp.broadcast_to(live, (8, 2 * wide)).astype(BF)


def teacher_kernel(
    core_ref, route_ref, attn_ref, weight_ref,
    keep_ref, send_ref, keep_routed_ref, send_routed_ref, left_ref, blocks_ref, sems,
):
    step = pl.program_id(0)
    tokens, wide = attn_ref.shape
    parts = blocks_ref.shape[0]

    def load(i, first):
        source = weight_ref.at[:, pl.ds(first, wide)]
        return pltpu.make_async_copy(source, blocks_ref.at[i], sems.at[i])

    @pl.when(step == 0)
    def _():
        rows = left_ref.at[0:tokens, :]
        acts = pltpu.make_async_copy(attn_ref, rows, sems.at[parts])
        acts.start()
        for i in range(parts):
            load(i, i * wide).start()
        hot = slot_rows(route_ref[...], tokens)
        acts.wait()
        left_ref[tokens:, :] = dot(hot, left_ref[0:tokens, :]).astype(BF)

    for i in (2 * step, 2 * step + 1):
        load(i, pl.multiple_of(i * wide, wide)).wait()
    core = core_ref[0]
    for place, out_ref, routed_ref in (
        (1 - core, send_ref, send_routed_ref),
        (core, keep_ref, keep_routed_ref),
    ):
        product = dot(left_ref[...], blocks_ref[2 * step + place]).astype(BF)
        out_ref[0] = product[0:tokens]
        routed_ref[0] = product[tokens:]


def copies_kernel(rows_ref, p1, p2, out_ref, q1, q2, sems):
    copies = [
        pltpu.make_async_copy(rows_ref, out_ref.at[s], sems.at[s]) for s in range(out_ref.shape[0])
    ]
    for copy in copies:
        copy.start()
    for copy in copies:
        copy.wait()


def core_sum_kernel(x_ref, *refs):
    ways = len(refs) // 3
    for j in range(ways):
        total = refs[j][...].astype(F32) + refs[ways + j][...].astype(F32)
        refs[2 * ways + j][...] = total.astype(BF).reshape(refs[2 * ways + j].shape)


def x_sum_kernel(*refs):
    total = refs[0][...].astype(F32)
    for ref in refs[1:-1]:
        total = total + ref[...].astype(F32)
    refs[-1][...] = total.astype(refs[-1].dtype)


def routed_sum_kernel(y_ref, route_ref, residual_ref, p1, p2, p3, *refs):
    ins, (send_ref, keep_ref) = refs[:8], refs[8:10]
    x_sum_kernel(*ins[:4], send_ref)
    x_sum_kernel(*ins[4:], keep_ref)
    hot = slot_rows(route_ref[...], residual_ref.shape[1])
    keep_ref[0] = keep_ref[0] + dot(hot, residual_ref[...], 1, 1)


def halves_kernel(x_ref, *refs):
    ins, (keep_a, send_a, keep_b, send_b) = refs[:8], refs[8:]
    sums = [(ins[m][0].astype(F32) + ins[4 + m][0].astype(F32)).astype(BF) for m in range(4)]
    for half, ref, order in ((0, keep_a, (0, 3)), (0, send_a, (1, 2)), (1, keep_b, (0, 1)), (1, send_b, (3, 2))):
        for i, m in enumerate(order):
            ref[i, 0] = sums[m][half]


def first_sum_kernel(keep_a, got_a, keep_b, got_b, own_a, on_a, own_b, on_b):
    for keep, got, own, on in ((keep_a, got_a, own_a, on_a), (keep_b, got_b, own_b, on_b)):
        own[...] = keep[0].astype(F32) + got[0].astype(F32)
        on[...] = (keep[1].astype(F32) + got[1].astype(F32)).astype(BF)


def second_sum_kernel(y_ref, *refs):
    ins, (send_ref, keep_ref) = refs[:8], refs[8:]
    for half in range(2):
        own, got, other_own, other_got = ins[4 * half : 4 * half + 4]
        send_ref[half] = (other_own[0] + other_got[0].astype(F32)).astype(BF)
        keep_ref[half] = own[0] + got[0].astype(F32)


def residual_kernel(residual_ref, keep_ref, got_ref, out_ref):
    summed = (keep_ref[...] + got_ref[...].astype(F32)).reshape(-1, keep_ref.shape[2])
    out_ref[...] = (residual_ref[...].astype(F32) + summed.T).astype(BF)


def up_kernel(
    group_ref, got_ref, gain_ref, gate_ref, up_ref, after_ref,
    out_ref, rows_ref, chosen_ref, padded_ref, weights_ref, sems,
):
    loads = [
        pltpu.make_async_copy(ref, weights_ref.at[i], sems.at[i])
        for i, ref in enumerate((gate_ref, up_ref))
    ]
    for load in loads:
        load.start()
    sources, height, wide = got_ref.shape
    groups = sources // 2
    half, side = height - 8, wide // 2
    slots = 2 * half
    per = out_ref.shape[1]
    total = groups * per

    for s in range(sources):
        g, d = s // 2, s % 2
        block = got_ref[s, 0:half, :]
        padded_ref[g * slots : g * slots + half, d * side : (d + 1) * side] = block[:, 0:side]
        padded_ref[g * slots + half : (g + 1) * slots, d * side : (d + 1) * side] = block[:, side:]
    at = half
    counts = [got_ref[2 * g, at : at + 8, 0 : 2 * slots].astype(F32)[0:1] for g in range(groups)]

    row = lax.broadcasted_iota(jnp.int32, (total, 2 * slots), 0)
    lane = lax.broadcasted_iota(jnp.int32, (total, 2 * slots), 1)
    second = lane >= slots
    slot = jnp.where(second, lane - slots, lane)
    slot_f = slot.astype(F32)
    shift = (row - slot).astype(F32)
    x = jnp.zeros((total, wide), F32)
    run = jnp.zeros_like(counts[0])
    for q in range(groups // 2):
        one, two = counts[2 * q], counts[2 * q + 1]
        start = jnp.where(second, run + one, run)
        count = jnp.where(second, two, one)
        run = run + one + two
        chosen = jnp.where((shift == start) & (slot_f < count), 1.0, 0.0).astype(BF)
        chosen_ref[:, 2 * q * slots : 2 * (q + 1) * slots] = chosen
        x = x + dot(chosen, padded_ref[2 * q * slots : 2 * (q + 1) * slots, :])

    square = jnp.sum(x * x, axis=1, keepdims=True)
    high = square.astype(BF)
    low = (square - high.astype(F32)).astype(BF)
    lane128 = lax.broadcasted_iota(jnp.int32, (total, 128), 1)
    squares = jnp.where(lane128 < 64, high.astype(F32), low.astype(F32)).astype(BF)
    scaled = (x * gain_ref[...]).astype(BF)
    rows_ref[...] = scaled
    for load in loads:
        load.wait()
    gate = dot(scaled, weights_ref[0]).astype(BF)
    up = dot(scaled, weights_ref[1]).astype(BF)
    at = 2 * wide + 128
    for g in range(groups):
        own = slice(g * per, (g + 1) * per)
        out_ref[g, :, 0:wide] = gate[own]
        out_ref[g, :, wide : 2 * wide] = up[own]
        out_ref[g, :, 2 * wide : at] = squares[own]


def hidden_kernel(
    features, got_ref, keep_ref, other_ref, p1, p2,
    out_ref, gate_ref, up_ref, scale_ref, q1, q2,
):
    per, wide = gate_ref.shape
    at = got_ref.shape[2]
    total = got_ref[0, :, 0:at].astype(F32)
    for g in range(1, got_ref.shape[0]):
        total = total + got_ref[g, :, 0:at].astype(F32)
    square = total[:, 2 * wide : 2 * wide + 1] + total[:, 2 * wide + 64 : 2 * wide + 65]
    scale = lax.rsqrt(square * (1.0 / features) + EPS)
    gate = total[:, 0:wide] * scale
    up = total[:, wide : 2 * wide] * scale
    gate_ref[...] = gate
    up_ref[...] = up
    scale_ref[...] = jnp.broadcast_to(scale, scale_ref.shape)
    hidden = (gate * jax.nn.sigmoid(gate) * up).astype(BF)
    routed = (keep_ref[0] + other_ref[0].astype(F32)).astype(BF)
    for g in range(out_ref.shape[0]):
        out_ref[g, 0:per, :] = hidden
        out_ref[g, per:, :] = routed


def down_kernel(
    group_ref, got_ref, down_ref, chosen_ref, projector_ref, after_ref,
    out_ref, hidden_ref, rows_ref, block_ref, sem,
):
    wide = block_ref.shape[1]
    first = pl.multiple_of(group_ref[0] * wide, wide)
    load = pltpu.make_async_copy(projector_ref.at[:, pl.ds(first, wide)], block_ref, sem)
    load.start()
    groups = got_ref.shape[0]
    per = hidden_ref.shape[0] // groups
    slots = got_ref.shape[1] - per
    for g in range(groups):
        hidden_ref[g * per : (g + 1) * per, :] = got_ref[g, 0:per, :]
        rows_ref[g * slots : (g + 1) * slots, :] = got_ref[g, per:, :]
    rows = dot(chosen_ref[...], rows_ref[...]).astype(BF)
    part = dot(hidden_ref[...], down_ref[...], 1, 1)
    load.wait()
    part = part - dot(rows, block_ref[...])
    out_ref[...] = part.astype(BF).reshape(out_ref.shape)


def misfit_kernel(scale, got_ref, out_ref):
    total = got_ref[0].astype(F32)
    for s in range(1, got_ref.shape[0]):
        total = total + got_ref[s].astype(F32)
    grad = (total * scale).astype(BF)
    for s in range(out_ref.shape[0]):
        out_ref[s] = grad


def back_kernel(got_ref, down_ref, passed_ref, out_ref, same_ref):
    groups, per, wide = out_ref.shape
    part = dot(got_ref[...].reshape(groups * per, got_ref.shape[2]), down_ref[...])
    out_ref[...] = part.astype(BF).reshape(groups, per, wide)


def acts_kernel(got_ref, gate_ref, up_ref, scale_ref, out_ref):
    wide = gate_ref.shape[1]
    grad = got_ref[0].astype(F32)
    for g in range(1, got_ref.shape[0]):
        grad = grad + got_ref[g].astype(F32)
    grad = grad * scale_ref[:, 0:1]
    gate, up = gate_ref[...], up_ref[...]
    sigma = jax.nn.sigmoid(gate)
    grad_gate = (grad * up * sigma * (1.0 + gate * (1.0 - sigma))).astype(BF)
    grad_up = (grad * gate * sigma).astype(BF)
    for g in range(out_ref.shape[0]):
        out_ref[g, :, 0:wide] = grad_gate
        out_ref[g, :, wide : 2 * wide] = grad_up


def down_weights_kernel(grad_ref, hidden_ref, out_ref):
    rows, units = hidden_ref.shape
    out_ref[...] = dot(grad_ref[...].reshape(rows, out_ref.shape[0]), hidden_ref[...], 0, 0)


def weights_kernel(rows_ref, got_ref, gate_ref, up_ref):
    wide = gate_ref.shape[1]
    acts = got_ref[...].reshape(got_ref.shape[0] * got_ref.shape[1], 2 * wide)
    gate_ref[...] = dot(rows_ref[...], acts[:, 0:wide], 0, 0)
    up_ref[...] = dot(rows_ref[...], acts[:, wide:], 0, 0)


def on_device(
    attn_values,
    out_weight,
    residual_t,
    projector,
    student_input,
    norm_gain,
    w_gate,
    w_up,
    w_down,
    route_index,
):
    groups, parts = lax.axis_size("batch"), lax.axis_size("tensor")
    slots = route_index.shape[1]
    tokens, wide = attn_values.shape
    side = student_input.shape[1]
    features = norm_gain.shape[0]
    live = tokens * groups // 8
    per = live // groups
    units = w_gate.shape[1]
    extra = slots // 2 + 8
    group, part = lax.axis_index("batch"), lax.axis_index("tensor")
    core, x_at, y_at = part & 1, (part >> 1) & 3, part >> 3
    shape = jax.ShapeDtypeStruct
    vmem = pl.BlockSpec(memory_space=pltpu.VMEM)
    anywhere = pl.BlockSpec(memory_space=pl.ANY)

    def hbm(value):
        return pltpu.with_memory_space_constraint(value, pltpu.HBM)

    out_weight, w_gate, w_up, projector, student_input, route_index = (
        hbm(w) for w in (out_weight, w_gate, w_up, projector, student_input, route_index)
    )

    rows = pl.pallas_call(
        rows_kernel,
        out_shape=pltpu.HBM((extra, 2 * side), BF),
        cost_estimate=cost(2 * slots * tokens * side, MIB // 4),
        compiler_params=params(4),
        name="rows",
    )(route_index, student_input)
    pairs = [
        (b * parts + t, (t // 2) * parts + 2 * b + t % 2)
        for b in range(groups)
        for t in range(parts)
    ]
    rows = lax.ppermute(rows, ("batch", "tensor"), pairs)

    keep, send, keep_routed, send_routed = pl.pallas_call(
        teacher_kernel,
        grid_spec=pltpu.PrefetchScalarGridSpec(
            num_scalar_prefetch=1,
            grid=(parts // 2,),
            in_specs=[
                pl.BlockSpec(route_index.shape, lambda j, core: (0, 0)),
                anywhere,
                anywhere,
            ],
            out_specs=[pl.BlockSpec((1, tokens, wide), lambda j, core: (j, 0, 0))] * 2
            + [pl.BlockSpec((1, slots, wide), lambda j, core: (j, 0, 0))] * 2,
            scratch_shapes=[
                pltpu.VMEM((tokens + slots, wide), BF),
                pltpu.VMEM((parts, wide, wide), BF),
                pltpu.SemaphoreType.DMA((parts + 1,)),
            ],
        ),
        out_shape=[pltpu.HBM((parts // 2, tokens, wide), BF)] * 2
        + [pltpu.HBM((parts // 2, slots, wide), BF)] * 2,
        compiler_params=params(20),
        cost_estimate=cost(2 * (tokens + slots) * wide * wide * parts, 14 * MIB),
        name="teacher",
    )(core.reshape(1), route_index, hbm(attn_values), out_weight)
    copies, send_routed, send = pl.pallas_call(
        copies_kernel,
        in_specs=[vmem] + [anywhere] * 2,
        out_specs=[anywhere] * 3,
        out_shape=[
            pltpu.HBM((parts, *rows.shape), BF),
            pltpu.HBM(send_routed.shape, BF),
            pltpu.HBM(send.shape, BF),
        ],
        scratch_shapes=[pltpu.SemaphoreType.DMA((parts,))],
        input_output_aliases={1: 1, 2: 2},
        compiler_params=params(4),
        cost_estimate=cost(0, MIB // 2),
        name="copies",
    )(rows, send_routed, send)
    every = lax.all_to_all(copies, "tensor", 0, 0, tiled=True)

    def along(value, move):
        return lax.ppermute(value, "tensor", [(t, move(t // 8, (t // 2) % 4, t % 2)) for t in range(parts)])

    def core_sum(keep, send, strip):
        got = along(send, lambda y, x, c: y * 8 + x * 2 + 1 - c)
        height = keep.shape[1]
        block = (1, strip, wide)
        return pl.pallas_call(
            core_sum_kernel,
            grid_spec=pltpu.PrefetchScalarGridSpec(
                num_scalar_prefetch=1,
                grid=(2, height // strip),
                in_specs=[
                    pl.BlockSpec(block, lambda y, i, x, j=j: (4 * y + ((x[0] + j) & 3), i, 0))
                    for j in range(4)
                ]
                * 2,
                out_specs=[pl.BlockSpec(block, lambda y, i, x: (y, i, 0))] * 4,
            ),
            out_shape=[pltpu.HBM((2, height, wide), BF)] * 4,
            compiler_params=params(16),
            cost_estimate=cost(MIB, 24 * height * wide * 2),
            name="core_sum",
        )(x_at.reshape(1), *[hbm(keep)] * 4, *[got] * 4)

    def along_x(own, moved):
        return [own] + [
            along(moved[j - 1], lambda y, x, c, j=j: y * 8 + (x + j) % 4 * 2 + c)
            for j in range(1, 4)
        ]

    def along_y(send):
        return along(send, lambda y, x, c: (1 - y) * 8 + x * 2 + c)

    def y_blocks(strip):
        block = (1, strip, wide)
        return [pl.BlockSpec(block, lambda i, y: (1 - y[0], i, 0))] * 4 + [
            pl.BlockSpec(block, lambda i, y: (y[0], i, 0))
        ] * 4

    half, strip = tokens // 2, tokens // 4
    got = along(send, lambda y, x, c: y * 8 + x * 2 + 1 - c)
    halves = (parts // 2, 2, half, wide)
    pair = pltpu.HBM((2, 2, half, wide), BF)
    keep_a, send_a, keep_b, send_b = pl.pallas_call(
        halves_kernel,
        grid_spec=pltpu.PrefetchScalarGridSpec(
            num_scalar_prefetch=1,
            grid=(2, half // strip),
            in_specs=[
                pl.BlockSpec(
                    (1, 2, strip, wide),
                    lambda y, n, x, m=m: (4 * y + lax.bitwise_xor(x[0], jnp.int32(m)), 0, n, 0),
                )
                for m in range(4)
            ]
            * 2,
            out_specs=[pl.BlockSpec((2, 1, strip, wide), lambda y, n, x: (0, y, n, 0))] * 4,
        ),
        out_shape=[pair] * 4,
        compiler_params=params(16),
        cost_estimate=cost(MIB, 6 * MIB),
        name="halves",
    )(x_at.reshape(1), *[hbm(keep.reshape(halves))] * 4, *[got.reshape(halves)] * 4)

    def along_x_by(value, mask):
        return along(value, lambda y, x, c: y * 8 + (x ^ mask) * 2 + c)

    packed = 2 * wide + 128
    sent, scaled, chosen = pl.pallas_call(
        up_kernel,
        grid_spec=pltpu.PrefetchScalarGridSpec(
            num_scalar_prefetch=1,
            grid=(1,),
            in_specs=[vmem, pl.BlockSpec((1, wide), lambda i, group: (0, group[0]))]
            + [anywhere] * 3,
            out_specs=[vmem] * 3,
            scratch_shapes=[
                pltpu.VMEM((groups * slots, wide), BF),
                pltpu.VMEM((2, wide, units), BF),
                pltpu.SemaphoreType.DMA((2,)),
            ],
        ),
        out_shape=[
            pltpu.HBM((groups, per, packed), BF),
            pltpu.HBM((live, wide), BF),
            pltpu.HBM((live, groups * slots), BF),
        ],
        compiler_params=params(16),
        cost_estimate=cost(800 * MIB, 4 * MIB),
        name="up",
    )(group.reshape(1), every, norm_gain[None], w_gate, w_up, hbm(keep_a))

    routed, *moved = core_sum(keep_routed, send_routed, slots)
    send_routed, keep_routed, sent, send_a, send_b = pl.pallas_call(
        routed_sum_kernel,
        grid_spec=pltpu.PrefetchScalarGridSpec(
            num_scalar_prefetch=1,
            grid=(1,),
            in_specs=[vmem] * 2 + [anywhere] * 3 + y_blocks(slots),
            out_specs=[pl.BlockSpec((1, slots, wide), lambda i, y: (0, 0, 0))] * 2
            + [anywhere] * 3,
        ),
        out_shape=[
            pltpu.HBM((1, slots, wide), BF),
            pltpu.HBM((1, slots, wide), F32),
            pltpu.HBM(sent.shape, BF),
        ]
        + [pair] * 2,
        input_output_aliases={3: 2, 4: 3, 5: 4},
        compiler_params=params(8),
        cost_estimate=cost(MIB, MIB),
        name="routed_sum",
    )(y_at.reshape(1), route_index, residual_t, sent, send_a, send_b, *along_x(routed, moved) * 2)
    other_routed = along_y(send_routed)

    got = lax.all_to_all(sent, "batch", 0, 0, tiled=True)

    flat = shape((per, units), F32)
    block = pl.BlockSpec((2, 2, strip, wide), lambda n: (0, 0, n, 0))
    line = pl.BlockSpec((2, strip, wide), lambda n: (0, n, 0))
    own_a, on_a, own_b, on_b = pl.pallas_call(
        first_sum_kernel,
        grid=(half // strip,),
        in_specs=[block] * 4,
        out_specs=[line] * 4,
        out_shape=[pltpu.HBM((2, half, wide), F32), pltpu.HBM((2, half, wide), BF)] * 2,
        compiler_params=params(16),
        cost_estimate=cost(MIB, 3 * MIB),
        name="first_sum",
    )(keep_a, along_x_by(send_a, 1), keep_b, along_x_by(send_b, 3))
    both, gate, up, scale, on_a, on_b = pl.pallas_call(
        lambda *refs: hidden_kernel(features, *refs),
        in_specs=[vmem] * 3 + [anywhere] * 2,
        out_specs=[vmem] * 4 + [anywhere] * 2,
        out_shape=[
            pltpu.HBM((groups, per + slots, units), BF),
            flat,
            flat,
            shape((per, 128), F32),
        ]
        + [pltpu.HBM((2, half, wide), BF)] * 2,
        input_output_aliases={3: 4, 4: 5},
        compiler_params=params(8),
        cost_estimate=cost(MIB, MIB),
        name="hidden",
    )(got, keep_routed, other_routed, on_a, on_b)
    got_a, got_b = along_x_by(on_a, 3), along_x_by(on_b, 1)
    here = pl.BlockSpec((1, strip, wide), lambda n, y: (y[0], n, 0))
    there = pl.BlockSpec((1, strip, wide), lambda n, y: (1 - y[0], n, 0))
    send, keep = pl.pallas_call(
        second_sum_kernel,
        grid_spec=pltpu.PrefetchScalarGridSpec(
            num_scalar_prefetch=1,
            grid=(half // strip,),
            in_specs=[here, here, there, there] * 2,
            out_specs=[pl.BlockSpec((2, strip, wide), lambda n, y: (0, n, 0))] * 2,
        ),
        out_shape=[pltpu.HBM((2, half, wide), BF), pltpu.HBM((2, half, wide), F32)],
        compiler_params=params(16),
        cost_estimate=cost(MIB, 3 * MIB),
        name="second_sum",
    )(y_at.reshape(1), *[own_a, got_a] * 2, *[own_b, got_b] * 2)
    other = along_y(send)
    both = lax.all_to_all(both, "batch", 0, 0, tiled=True)
    misfit, hidden = pl.pallas_call(
        down_kernel,
        grid_spec=pltpu.PrefetchScalarGridSpec(
            num_scalar_prefetch=1,
            grid=(1,),
            in_specs=[vmem] * 3 + [anywhere] * 2,
            out_specs=[vmem] * 2,
            scratch_shapes=[
                pltpu.VMEM((groups * slots, wide), BF),
                pltpu.VMEM((wide, wide), BF),
                pltpu.SemaphoreType.DMA,
            ],
        ),
        out_shape=[
            pltpu.HBM((parts, live // parts, wide), BF),
            pltpu.HBM((live, units), BF),
        ],
        compiler_params=params(16),
        cost_estimate=cost(768 * MIB, 4 * MIB),
        name="down",
    )(group.reshape(1), both, w_down, chosen, projector, hbm(keep))
    misfit = lax.all_to_all(misfit, "tensor", 0, 0, tiled=True)
    loss_scale = 1.0 / math.sqrt(live)
    grad_out = pl.pallas_call(
        lambda *refs: misfit_kernel(loss_scale, *refs),
        out_shape=pltpu.HBM(misfit.shape, BF),
        compiler_params=params(8),
        cost_estimate=cost(MIB, MIB),
        name="misfit",
    )(misfit)
    grad_out = lax.all_to_all(grad_out, "tensor", 0, 0, tiled=True)

    teacher_hidden = pl.pallas_call(
        residual_kernel,
        out_shape=pltpu.HBM(residual_t.shape, BF),
        compiler_params=params(8),
        cost_estimate=cost(MIB, 2 * MIB),
        name="residual",
    )(residual_t, keep, other)
    back, teacher_hidden = pl.pallas_call(
        back_kernel,
        in_specs=[vmem] * 2 + [anywhere],
        out_specs=[vmem, anywhere],
        out_shape=[shape((groups, per, units), BF), pltpu.HBM(residual_t.shape, BF)],
        input_output_aliases={2: 1},
        compiler_params=params(16),
        cost_estimate=cost(256 * MIB, MIB),
        name="back",
    )(grad_out, w_down, teacher_hidden)
    back = lax.all_to_all(back, "batch", 0, 0, tiled=True)
    acts = pl.pallas_call(
        acts_kernel,
        out_shape=pltpu.HBM((groups, per, 2 * units), BF),
        compiler_params=params(8),
        cost_estimate=cost(MIB, MIB),
        name="acts",
    )(back, gate, up, scale)
    acts = lax.all_to_all(acts, "batch", 0, 0, tiled=True)
    grad_down = pl.pallas_call(
        down_weights_kernel,
        out_shape=shape((wide, units), F32),
        compiler_params=params(16),
        cost_estimate=cost(256 * MIB, 2 * MIB),
        name="down_weights",
    )(grad_out, hidden)
    grad_gate, grad_up = pl.pallas_call(
        weights_kernel,
        out_shape=[shape((wide, units), F32)] * 2,
        compiler_params=params(16),
        cost_estimate=cost(512 * MIB, 4 * MIB),
        name="weights",
    )(scaled, acts)
    return teacher_hidden, grad_gate, grad_up, grad_down


def solution(mesh):
    in_specs = (
        P("batch", "tensor"),
        P("tensor", None),
        P("tensor", "batch"),
        P("tensor", None),
        P("batch", "tensor"),
        P(),
        P("batch", "tensor"),
        P("batch", "tensor"),
        P("batch", "tensor"),
        P("batch", None),
    )
    out_specs = (P("tensor", "batch"),) + (P("batch", "tensor"),) * 3
    return jax.shard_map(
        on_device, mesh=mesh, in_specs=in_specs, out_specs=out_specs, check_vma=False
    )
```

```python
import math

import jax
import jax.numpy as jnp
from jax import lax
from jax.experimental import pallas as pl
from jax.experimental.pallas import tpu as pltpu
from jax.sharding import PartitionSpec as P

EPS = 1e-05
BF = jnp.bfloat16
F32 = jnp.float32
MIB = 1 << 20


def params(mib):
    return pltpu.CompilerParams(vmem_limit_bytes=mib * MIB)


def cost(flops, nbytes):
    return pl.CostEstimate(flops=flops // 1024, bytes_accessed=nbytes // 1024, transcendentals=0)


def dot(a, b, ca=1, cb=0):
    return lax.dot_general(a, b, (((ca,), (cb,)), ((), ())), preferred_element_type=F32)


def whole(shape):
    return pl.BlockSpec(shape, lambda *_: (0,) * len(shape))


def slot_rows(route, tokens):
    slots = route.shape[1]
    grid = (slots, slots)
    diagonal = lax.broadcasted_iota(jnp.int32, grid, 0) == lax.broadcasted_iota(jnp.int32, grid, 1)
    spread = jnp.broadcast_to(route.astype(F32), grid)
    column = jnp.sum(jnp.where(diagonal, spread, 0.0), axis=1, keepdims=True)
    lane = lax.broadcasted_iota(jnp.int32, (slots, tokens), 1).astype(F32)
    return jnp.where(lane == column, 1.0, 0.0).astype(BF)


def rows_kernel(route_ref, x_ref, out_ref):
    route = route_ref[...]
    slots, wide = route.shape[1], x_ref.shape[1]
    rows = dot(slot_rows(route, x_ref.shape[0]), x_ref[...]).astype(BF)
    half = slots // 2
    out_ref[0:half, 0:wide] = rows[0:half]
    out_ref[0:half, wide : 2 * wide] = rows[half:]
    live = jnp.sum(jnp.where(route >= 0, 1.0, 0.0), axis=1, keepdims=True)
    out_ref[half : half + 8, :] = jnp.broadcast_to(live, (8, 2 * wide)).astype(BF)


def teacher_kernel(
    core_ref, route_ref, attn_ref, weight_ref,
    keep_ref, send_ref, keep_routed_ref, send_routed_ref, left_ref, blocks_ref, sems,
):
    step = pl.program_id(0)
    tokens, wide = attn_ref.shape
    parts = blocks_ref.shape[0]

    def load(i, first):
        source = weight_ref.at[:, pl.ds(first, wide)]
        return pltpu.make_async_copy(source, blocks_ref.at[i], sems.at[i])

    @pl.when(step == 0)
    def _():
        rows = left_ref.at[0:tokens, :]
        acts = pltpu.make_async_copy(attn_ref, rows, sems.at[parts])
        acts.start()
        for i in range(parts):
            load(i, i * wide).start()
        hot = slot_rows(route_ref[...], tokens)
        acts.wait()
        left_ref[tokens:, :] = dot(hot, left_ref[0:tokens, :]).astype(BF)

    for i in (2 * step, 2 * step + 1):
        load(i, pl.multiple_of(i * wide, wide)).wait()
    core = core_ref[0]
    for place, out_ref, routed_ref in (
        (1 - core, send_ref, send_routed_ref),
        (core, keep_ref, keep_routed_ref),
    ):
        product = dot(left_ref[...], blocks_ref[2 * step + place]).astype(BF)
        out_ref[0] = product[0:tokens]
        routed_ref[0] = product[tokens:]


def copies_kernel(rows_ref, p1, p2, out_ref, q1, q2, sems):
    copies = [
        pltpu.make_async_copy(rows_ref, out_ref.at[s], sems.at[s]) for s in range(out_ref.shape[0])
    ]
    for copy in copies:
        copy.start()
    for copy in copies:
        copy.wait()


def core_sum_kernel(x_ref, *refs):
    ways = len(refs) // 3
    for j in range(ways):
        total = refs[j][...].astype(F32) + refs[ways + j][...].astype(F32)
        refs[2 * ways + j][...] = total.astype(BF).reshape(refs[2 * ways + j].shape)


def x_sum_kernel(*refs):
    total = refs[0][...].astype(F32)
    for ref in refs[1:-1]:
        total = total + ref[...].astype(F32)
    refs[-1][...] = total.astype(refs[-1].dtype)


def routed_sum_kernel(y_ref, route_ref, residual_ref, passed_ref, *refs):
    ins, (send_ref, keep_ref) = refs[:8], refs[8:10]
    x_sum_kernel(*ins[:4], send_ref)
    x_sum_kernel(*ins[4:], keep_ref)
    hot = slot_rows(route_ref[...], residual_ref.shape[1])
    keep_ref[0] = keep_ref[0] + dot(hot, residual_ref[...], 1, 1)


def halves_kernel(x_ref, *refs):
    ins, (keep_a, send_a, keep_b, send_b) = refs[:8], refs[8:]
    sums = [(ins[m][0].astype(F32) + ins[4 + m][0].astype(F32)).astype(BF) for m in range(4)]
    for half, ref, order in ((0, keep_a, (0, 3)), (0, send_a, (1, 2)), (1, keep_b, (0, 1)), (1, send_b, (3, 2))):
        for i, m in enumerate(order):
            ref[i, 0] = sums[m][half]


def first_sum_kernel(keep_a, got_a, keep_b, got_b, own_a, on_a, own_b, on_b):
    for keep, got, own, on in ((keep_a, got_a, own_a, on_a), (keep_b, got_b, own_b, on_b)):
        own[...] = keep[0].astype(F32) + got[0].astype(F32)
        on[...] = (keep[1].astype(F32) + got[1].astype(F32)).astype(BF)


def second_sum_kernel(y_ref, *refs):
    ins, (send_ref, keep_ref) = refs[:8], refs[8:]
    for half in range(2):
        own, got, other_own, other_got = ins[4 * half : 4 * half + 4]
        send_ref[half] = (other_own[0] + other_got[0].astype(F32)).astype(BF)
        keep_ref[half] = own[0] + got[0].astype(F32)


def residual_kernel(residual_ref, keep_ref, got_ref, out_ref):
    summed = (keep_ref[...] + got_ref[...].astype(F32)).reshape(-1, keep_ref.shape[2])
    out_ref[...] = (residual_ref[...].astype(F32) + summed.T).astype(BF)


def up_kernel(
    group_ref, got_ref, gain_ref, gate_ref, up_ref, after_ref,
    out_ref, rows_ref, chosen_ref, padded_ref, weights_ref, sems,
):
    loads = [
        pltpu.make_async_copy(ref, weights_ref.at[i], sems.at[i])
        for i, ref in enumerate((gate_ref, up_ref))
    ]
    for load in loads:
        load.start()
    sources, height, wide = got_ref.shape
    groups = sources // 2
    half, side = height - 8, wide // 2
    slots = 2 * half
    per = out_ref.shape[1]
    total = groups * per

    for s in range(sources):
        g, d = s // 2, s % 2
        block = got_ref[s, 0:half, :]
        padded_ref[g * slots : g * slots + half, d * side : (d + 1) * side] = block[:, 0:side]
        padded_ref[g * slots + half : (g + 1) * slots, d * side : (d + 1) * side] = block[:, side:]
    at = half
    counts = [got_ref[2 * g, at : at + 8, 0 : 2 * slots].astype(F32)[0:1] for g in range(groups)]

    row = lax.broadcasted_iota(jnp.int32, (total, 2 * slots), 0)
    lane = lax.broadcasted_iota(jnp.int32, (total, 2 * slots), 1)
    second = lane >= slots
    slot = jnp.where(second, lane - slots, lane)
    slot_f = slot.astype(F32)
    shift = (row - slot).astype(F32)
    x = jnp.zeros((total, wide), F32)
    run = jnp.zeros_like(counts[0])
    for q in range(groups // 2):
        one, two = counts[2 * q], counts[2 * q + 1]
        start = jnp.where(second, run + one, run)
        count = jnp.where(second, two, one)
        run = run + one + two
        chosen = jnp.where((shift == start) & (slot_f < count), 1.0, 0.0).astype(BF)
        chosen_ref[:, 2 * q * slots : 2 * (q + 1) * slots] = chosen
        x = x + dot(chosen, padded_ref[2 * q * slots : 2 * (q + 1) * slots, :])

    square = jnp.sum(x * x, axis=1, keepdims=True)
    high = square.astype(BF)
    low = (square - high.astype(F32)).astype(BF)
    lane128 = lax.broadcasted_iota(jnp.int32, (total, 128), 1)
    squares = jnp.where(lane128 < 64, high.astype(F32), low.astype(F32)).astype(BF)
    scaled = (x * gain_ref[...]).astype(BF)
    rows_ref[...] = scaled
    for load in loads:
        load.wait()
    gate = dot(scaled, weights_ref[0]).astype(BF)
    up = dot(scaled, weights_ref[1]).astype(BF)
    at = 2 * wide + 128
    for g in range(groups):
        own = slice(g * per, (g + 1) * per)
        out_ref[g, :, 0:wide] = gate[own]
        out_ref[g, :, wide : 2 * wide] = up[own]
        out_ref[g, :, 2 * wide : at] = squares[own]


def hidden_kernel(
    features, got_ref, keep_ref, other_ref, p1, p2,
    out_ref, gate_ref, up_ref, scale_ref, q1, q2,
):
    per, wide = gate_ref.shape
    at = got_ref.shape[2]
    total = got_ref[0, :, 0:at].astype(F32)
    for g in range(1, got_ref.shape[0]):
        total = total + got_ref[g, :, 0:at].astype(F32)
    square = total[:, 2 * wide : 2 * wide + 1] + total[:, 2 * wide + 64 : 2 * wide + 65]
    scale = lax.rsqrt(square * (1.0 / features) + EPS)
    gate = total[:, 0:wide] * scale
    up = total[:, wide : 2 * wide] * scale
    gate_ref[...] = gate
    up_ref[...] = up
    scale_ref[...] = jnp.broadcast_to(scale, scale_ref.shape)
    hidden = (gate * jax.nn.sigmoid(gate) * up).astype(BF)
    routed = (keep_ref[0] + other_ref[0].astype(F32)).astype(BF)
    for g in range(out_ref.shape[0]):
        out_ref[g, 0:per, :] = hidden
        out_ref[g, per:, :] = routed


def down_kernel(
    group_ref, got_ref, down_ref, chosen_ref, projector_ref, after_ref,
    out_ref, hidden_ref, rows_ref, block_ref, sem,
):
    wide = block_ref.shape[1]
    first = pl.multiple_of(group_ref[0] * wide, wide)
    load = pltpu.make_async_copy(projector_ref.at[:, pl.ds(first, wide)], block_ref, sem)
    load.start()
    groups = got_ref.shape[0]
    per = hidden_ref.shape[0] // groups
    slots = got_ref.shape[1] - per
    for g in range(groups):
        hidden_ref[g * per : (g + 1) * per, :] = got_ref[g, 0:per, :]
        rows_ref[g * slots : (g + 1) * slots, :] = got_ref[g, per:, :]
    rows = dot(chosen_ref[...], rows_ref[...]).astype(BF)
    part = dot(hidden_ref[...], down_ref[...], 1, 1)
    load.wait()
    part = part - dot(rows, block_ref[...])
    out_ref[...] = part.astype(BF).reshape(out_ref.shape)


def misfit_kernel(scale, got_ref, out_ref):
    total = got_ref[0].astype(F32)
    for s in range(1, got_ref.shape[0]):
        total = total + got_ref[s].astype(F32)
    grad = (total * scale).astype(BF)
    for s in range(out_ref.shape[0]):
        out_ref[s] = grad


def back_kernel(got_ref, down_ref, passed_ref, out_ref, same_ref):
    groups, per, wide = out_ref.shape
    part = dot(got_ref[...].reshape(groups * per, got_ref.shape[2]), down_ref[...])
    out_ref[...] = part.astype(BF).reshape(groups, per, wide)


def acts_kernel(got_ref, gate_ref, up_ref, scale_ref, out_ref):
    wide = gate_ref.shape[1]
    grad = got_ref[0].astype(F32)
    for g in range(1, got_ref.shape[0]):
        grad = grad + got_ref[g].astype(F32)
    grad = grad * scale_ref[:, 0:1]
    gate, up = gate_ref[...], up_ref[...]
    sigma = jax.nn.sigmoid(gate)
    grad_gate = (grad * up * sigma * (1.0 + gate * (1.0 - sigma))).astype(BF)
    grad_up = (grad * gate * sigma).astype(BF)
    for g in range(out_ref.shape[0]):
        out_ref[g, :, 0:wide] = grad_gate
        out_ref[g, :, wide : 2 * wide] = grad_up


def down_weights_kernel(grad_ref, hidden_ref, out_ref):
    rows, units = hidden_ref.shape
    out_ref[...] = dot(grad_ref[...].reshape(rows, out_ref.shape[0]), hidden_ref[...], 0, 0)


def weights_kernel(rows_ref, got_ref, gate_ref, up_ref):
    wide = gate_ref.shape[1]
    acts = got_ref[...].reshape(got_ref.shape[0] * got_ref.shape[1], 2 * wide)
    gate_ref[...] = dot(rows_ref[...], acts[:, 0:wide], 0, 0)
    up_ref[...] = dot(rows_ref[...], acts[:, wide:], 0, 0)


def on_device(
    attn_values,
    out_weight,
    residual_t,
    projector,
    student_input,
    norm_gain,
    w_gate,
    w_up,
    w_down,
    route_index,
):
    groups, parts = lax.axis_size("batch"), lax.axis_size("tensor")
    slots = route_index.shape[1]
    tokens, wide = attn_values.shape
    side = student_input.shape[1]
    features = norm_gain.shape[0]
    live = tokens * groups // 8
    per = live // groups
    units = w_gate.shape[1]
    extra = slots // 2 + 8
    group, part = lax.axis_index("batch"), lax.axis_index("tensor")
    core, x_at, y_at = part & 1, (part >> 1) & 3, part >> 3
    shape = jax.ShapeDtypeStruct
    vmem = pl.BlockSpec(memory_space=pltpu.VMEM)
    anywhere = pl.BlockSpec(memory_space=pl.ANY)

    def hbm(value):
        return pltpu.with_memory_space_constraint(value, pltpu.HBM)

    out_weight, w_gate, w_up, projector, student_input, route_index = (
        hbm(w) for w in (out_weight, w_gate, w_up, projector, student_input, route_index)
    )

    rows = pl.pallas_call(
        rows_kernel,
        out_shape=pltpu.HBM((extra, 2 * side), BF),
        cost_estimate=cost(2 * slots * tokens * side, MIB // 4),
        compiler_params=params(4),
        name="rows",
    )(route_index, student_input)
    pairs = [
        (b * parts + t, (t // 2) * parts + 2 * b + t % 2)
        for b in range(groups)
        for t in range(parts)
    ]
    rows = lax.ppermute(rows, ("batch", "tensor"), pairs)

    keep, send, keep_routed, send_routed = pl.pallas_call(
        teacher_kernel,
        grid_spec=pltpu.PrefetchScalarGridSpec(
            num_scalar_prefetch=1,
            grid=(parts // 2,),
            in_specs=[
                pl.BlockSpec(route_index.shape, lambda j, core: (0, 0)),
                anywhere,
                anywhere,
            ],
            out_specs=[pl.BlockSpec((1, tokens, wide), lambda j, core: (j, 0, 0))] * 2
            + [pl.BlockSpec((1, slots, wide), lambda j, core: (j, 0, 0))] * 2,
            scratch_shapes=[
                pltpu.VMEM((tokens + slots, wide), BF),
                pltpu.VMEM((parts, wide, wide), BF),
                pltpu.SemaphoreType.DMA((parts + 1,)),
            ],
        ),
        out_shape=[pltpu.HBM((parts // 2, tokens, wide), BF)] * 2
        + [pltpu.HBM((parts // 2, slots, wide), BF)] * 2,
        compiler_params=params(20),
        cost_estimate=cost(2 * (tokens + slots) * wide * wide * parts, 14 * MIB),
        name="teacher",
    )(core.reshape(1), route_index, hbm(attn_values), out_weight)
    copies, send_routed, send = pl.pallas_call(
        copies_kernel,
        in_specs=[vmem] + [anywhere] * 2,
        out_specs=[anywhere] * 3,
        out_shape=[
            pltpu.HBM((parts, *rows.shape), BF),
            pltpu.HBM(send_routed.shape, BF),
            pltpu.HBM(send.shape, BF),
        ],
        scratch_shapes=[pltpu.SemaphoreType.DMA((parts,))],
        input_output_aliases={1: 1, 2: 2},
        compiler_params=params(4),
        cost_estimate=cost(0, MIB // 2),
        name="copies",
    )(rows, send_routed, send)
    every = lax.all_to_all(copies, "tensor", 0, 0, tiled=True)

    def along(value, move):
        return lax.ppermute(value, "tensor", [(t, move(t // 8, (t // 2) % 4, t % 2)) for t in range(parts)])

    def core_sum(keep, send, strip):
        got = along(send, lambda y, x, c: y * 8 + x * 2 + 1 - c)
        height = keep.shape[1]
        block = (1, strip, wide)
        return pl.pallas_call(
            core_sum_kernel,
            grid_spec=pltpu.PrefetchScalarGridSpec(
                num_scalar_prefetch=1,
                grid=(2, height // strip),
                in_specs=[
                    pl.BlockSpec(block, lambda y, i, x, j=j: (4 * y + ((x[0] + j) & 3), i, 0))
                    for j in range(4)
                ]
                * 2,
                out_specs=[pl.BlockSpec(block, lambda y, i, x: (y, i, 0))] * 4,
            ),
            out_shape=[pltpu.HBM((2, height, wide), BF)] * 4,
            compiler_params=params(16),
            cost_estimate=cost(MIB, 24 * height * wide * 2),
            name="core_sum",
        )(x_at.reshape(1), *[hbm(keep)] * 4, *[got] * 4)

    def along_x(own, moved):
        return [own] + [
            along(moved[j - 1], lambda y, x, c, j=j: y * 8 + (x + j) % 4 * 2 + c)
            for j in range(1, 4)
        ]

    def along_y(send):
        return along(send, lambda y, x, c: (1 - y) * 8 + x * 2 + c)

    def y_blocks(strip):
        block = (1, strip, wide)
        return [pl.BlockSpec(block, lambda i, y: (1 - y[0], i, 0))] * 4 + [
            pl.BlockSpec(block, lambda i, y: (y[0], i, 0))
        ] * 4

    half, strip = tokens // 2, tokens // 4
    got = along(send, lambda y, x, c: y * 8 + x * 2 + 1 - c)
    halves = (parts // 2, 2, half, wide)
    pair = pltpu.HBM((2, 2, half, wide), BF)
    keep_a, send_a, keep_b, send_b = pl.pallas_call(
        halves_kernel,
        grid_spec=pltpu.PrefetchScalarGridSpec(
            num_scalar_prefetch=1,
            grid=(2, half // strip),
            in_specs=[
                pl.BlockSpec(
                    (1, 2, strip, wide),
                    lambda y, n, x, m=m: (4 * y + lax.bitwise_xor(x[0], jnp.int32(m)), 0, n, 0),
                )
                for m in range(4)
            ]
            * 2,
            out_specs=[pl.BlockSpec((2, 1, strip, wide), lambda y, n, x: (0, y, n, 0))] * 4,
        ),
        out_shape=[pair] * 4,
        compiler_params=params(16),
        cost_estimate=cost(MIB, 6 * MIB),
        name="halves",
    )(x_at.reshape(1), *[hbm(keep.reshape(halves))] * 4, *[got.reshape(halves)] * 4)

    def along_x_by(value, mask):
        return along(value, lambda y, x, c: y * 8 + (x ^ mask) * 2 + c)

    packed = 2 * wide + 128
    sent, scaled, chosen = pl.pallas_call(
        up_kernel,
        grid_spec=pltpu.PrefetchScalarGridSpec(
            num_scalar_prefetch=1,
            grid=(1,),
            in_specs=[vmem, pl.BlockSpec((1, wide), lambda i, group: (0, group[0]))]
            + [anywhere] * 3,
            out_specs=[vmem] * 3,
            scratch_shapes=[
                pltpu.VMEM((groups * slots, wide), BF),
                pltpu.VMEM((2, wide, units), BF),
                pltpu.SemaphoreType.DMA((2,)),
            ],
        ),
        out_shape=[
            pltpu.HBM((groups, per, packed), BF),
            pltpu.HBM((live, wide), BF),
            pltpu.HBM((live, groups * slots), BF),
        ],
        compiler_params=params(16),
        cost_estimate=cost(800 * MIB, 4 * MIB),
        name="up",
    )(group.reshape(1), every, norm_gain[None], w_gate, w_up, hbm(keep_a))

    routed, *moved = core_sum(keep_routed, send_routed, slots)
    send_routed, keep_routed, sent = pl.pallas_call(
        routed_sum_kernel,
        grid_spec=pltpu.PrefetchScalarGridSpec(
            num_scalar_prefetch=1,
            grid=(1,),
            in_specs=[vmem] * 2 + [anywhere] + y_blocks(slots),
            out_specs=[pl.BlockSpec((1, slots, wide), lambda i, y: (0, 0, 0))] * 2 + [anywhere],
        ),
        out_shape=[
            pltpu.HBM((1, slots, wide), BF),
            pltpu.HBM((1, slots, wide), F32),
            pltpu.HBM(sent.shape, BF),
        ],
        input_output_aliases={3: 2},
        compiler_params=params(8),
        cost_estimate=cost(MIB, MIB),
        name="routed_sum",
    )(y_at.reshape(1), route_index, residual_t, sent, *along_x(routed, moved) * 2)
    other_routed = along_y(send_routed)

    got = lax.all_to_all(sent, "batch", 0, 0, tiled=True)

    flat = shape((per, units), F32)
    block = pl.BlockSpec((2, 2, strip, wide), lambda n: (0, 0, n, 0))
    line = pl.BlockSpec((2, strip, wide), lambda n: (0, n, 0))
    own_a, on_a, own_b, on_b = pl.pallas_call(
        first_sum_kernel,
        grid=(half // strip,),
        in_specs=[block] * 4,
        out_specs=[line] * 4,
        out_shape=[pltpu.HBM((2, half, wide), F32), pltpu.HBM((2, half, wide), BF)] * 2,
        compiler_params=params(16),
        cost_estimate=cost(MIB, 3 * MIB),
        name="first_sum",
    )(keep_a, along_x_by(send_a, 1), keep_b, along_x_by(send_b, 3))
    both, gate, up, scale, on_a, on_b = pl.pallas_call(
        lambda *refs: hidden_kernel(features, *refs),
        in_specs=[vmem] * 3 + [anywhere] * 2,
        out_specs=[vmem] * 4 + [anywhere] * 2,
        out_shape=[
            pltpu.HBM((groups, per + slots, units), BF),
            flat,
            flat,
            shape((per, 128), F32),
        ]
        + [pltpu.HBM((2, half, wide), BF)] * 2,
        input_output_aliases={3: 4, 4: 5},
        compiler_params=params(8),
        cost_estimate=cost(MIB, MIB),
        name="hidden",
    )(got, keep_routed, other_routed, on_a, on_b)
    got_a, got_b = along_x_by(on_a, 3), along_x_by(on_b, 1)
    here = pl.BlockSpec((1, strip, wide), lambda n, y: (y[0], n, 0))
    there = pl.BlockSpec((1, strip, wide), lambda n, y: (1 - y[0], n, 0))
    send, keep = pl.pallas_call(
        second_sum_kernel,
        grid_spec=pltpu.PrefetchScalarGridSpec(
            num_scalar_prefetch=1,
            grid=(half // strip,),
            in_specs=[here, here, there, there] * 2,
            out_specs=[pl.BlockSpec((2, strip, wide), lambda n, y: (0, n, 0))] * 2,
        ),
        out_shape=[pltpu.HBM((2, half, wide), BF), pltpu.HBM((2, half, wide), F32)],
        compiler_params=params(16),
        cost_estimate=cost(MIB, 3 * MIB),
        name="second_sum",
    )(y_at.reshape(1), *[own_a, got_a] * 2, *[own_b, got_b] * 2)
    other = along_y(send)
    both = lax.all_to_all(both, "batch", 0, 0, tiled=True)
    misfit, hidden = pl.pallas_call(
        down_kernel,
        grid_spec=pltpu.PrefetchScalarGridSpec(
            num_scalar_prefetch=1,
            grid=(1,),
            in_specs=[vmem] * 3 + [anywhere] * 2,
            out_specs=[vmem] * 2,
            scratch_shapes=[
                pltpu.VMEM((groups * slots, wide), BF),
                pltpu.VMEM((wide, wide), BF),
                pltpu.SemaphoreType.DMA,
            ],
        ),
        out_shape=[
            pltpu.HBM((parts, live // parts, wide), BF),
            pltpu.HBM((live, units), BF),
        ],
        compiler_params=params(16),
        cost_estimate=cost(768 * MIB, 4 * MIB),
        name="down",
    )(group.reshape(1), both, w_down, chosen, projector, hbm(keep))
    misfit = lax.all_to_all(misfit, "tensor", 0, 0, tiled=True)
    loss_scale = 1.0 / math.sqrt(live)
    grad_out = pl.pallas_call(
        lambda *refs: misfit_kernel(loss_scale, *refs),
        out_shape=pltpu.HBM(misfit.shape, BF),
        compiler_params=params(8),
        cost_estimate=cost(MIB, MIB),
        name="misfit",
    )(misfit)
    grad_out = lax.all_to_all(grad_out, "tensor", 0, 0, tiled=True)

    teacher_hidden = pl.pallas_call(
        residual_kernel,
        out_shape=pltpu.HBM(residual_t.shape, BF),
        compiler_params=params(8),
        cost_estimate=cost(MIB, 2 * MIB),
        name="residual",
    )(residual_t, keep, other)
    back, teacher_hidden = pl.pallas_call(
        back_kernel,
        in_specs=[vmem] * 2 + [anywhere],
        out_specs=[vmem, anywhere],
        out_shape=[shape((groups, per, units), BF), pltpu.HBM(residual_t.shape, BF)],
        input_output_aliases={2: 1},
        compiler_params=params(16),
        cost_estimate=cost(256 * MIB, MIB),
        name="back",
    )(grad_out, w_down, teacher_hidden)
    back = lax.all_to_all(back, "batch", 0, 0, tiled=True)
    acts = pl.pallas_call(
        acts_kernel,
        out_shape=pltpu.HBM((groups, per, 2 * units), BF),
        compiler_params=params(8),
        cost_estimate=cost(MIB, MIB),
        name="acts",
    )(back, gate, up, scale)
    acts = lax.all_to_all(acts, "batch", 0, 0, tiled=True)
    grad_down = pl.pallas_call(
        down_weights_kernel,
        out_shape=shape((wide, units), F32),
        compiler_params=params(16),
        cost_estimate=cost(256 * MIB, 2 * MIB),
        name="down_weights",
    )(grad_out, hidden)
    grad_gate, grad_up = pl.pallas_call(
        weights_kernel,
        out_shape=[shape((wide, units), F32)] * 2,
        compiler_params=params(16),
        cost_estimate=cost(512 * MIB, 4 * MIB),
        name="weights",
    )(scaled, acts)
    return teacher_hidden, grad_gate, grad_up, grad_down


def solution(mesh):
    in_specs = (
        P("batch", "tensor"),
        P("tensor", None),
        P("tensor", "batch"),
        P("tensor", None),
        P("batch", "tensor"),
        P(),
        P("batch", "tensor"),
        P("batch", "tensor"),
        P("batch", "tensor"),
        P("batch", None),
    )
    out_specs = (P("tensor", "batch"),) + (P("batch", "tensor"),) * 3
    return jax.shard_map(
        on_device, mesh=mesh, in_specs=in_specs, out_specs=out_specs, check_vma=False
    )
```

```python
import math

import jax
import jax.numpy as jnp
from jax import lax
from jax.experimental import pallas as pl
from jax.experimental.pallas import tpu as pltpu
from jax.sharding import PartitionSpec as P

EPS = 1e-05
BF = jnp.bfloat16
F32 = jnp.float32
MIB = 1 << 20


def params(mib):
    return pltpu.CompilerParams(vmem_limit_bytes=mib * MIB)


def cost(flops, nbytes):
    return pl.CostEstimate(flops=flops // 1024, bytes_accessed=nbytes // 1024, transcendentals=0)


def dot(a, b, ca=1, cb=0):
    return lax.dot_general(a, b, (((ca,), (cb,)), ((), ())), preferred_element_type=F32)


def whole(shape):
    return pl.BlockSpec(shape, lambda *_: (0,) * len(shape))


def slot_rows(route, tokens):
    slots = route.shape[1]
    grid = (slots, slots)
    diagonal = lax.broadcasted_iota(jnp.int32, grid, 0) == lax.broadcasted_iota(jnp.int32, grid, 1)
    spread = jnp.broadcast_to(route.astype(F32), grid)
    column = jnp.sum(jnp.where(diagonal, spread, 0.0), axis=1, keepdims=True)
    lane = lax.broadcasted_iota(jnp.int32, (slots, tokens), 1).astype(F32)
    return jnp.where(lane == column, 1.0, 0.0).astype(BF)


def rows_kernel(route_ref, x_ref, out_ref):
    route = route_ref[...]
    slots, wide = route.shape[1], x_ref.shape[1]
    rows = dot(slot_rows(route, x_ref.shape[0]), x_ref[...]).astype(BF)
    half = slots // 2
    out_ref[0:half, 0:wide] = rows[0:half]
    out_ref[0:half, wide : 2 * wide] = rows[half:]
    live = jnp.sum(jnp.where(route >= 0, 1.0, 0.0), axis=1, keepdims=True)
    out_ref[half : half + 8, :] = jnp.broadcast_to(live, (8, 2 * wide)).astype(BF)


def teacher_kernel(
    core_ref, route_ref, attn_ref, weight_ref,
    keep_ref, send_ref, keep_routed_ref, send_routed_ref, left_ref, blocks_ref, sems,
):
    step = pl.program_id(0)
    tokens, wide = attn_ref.shape
    parts = blocks_ref.shape[0]

    def load(i, first):
        source = weight_ref.at[:, pl.ds(first, wide)]
        return pltpu.make_async_copy(source, blocks_ref.at[i], sems.at[i])

    @pl.when(step == 0)
    def _():
        rows = left_ref.at[0:tokens, :]
        acts = pltpu.make_async_copy(attn_ref, rows, sems.at[parts])
        acts.start()
        for i in range(parts):
            load(i, i * wide).start()
        hot = slot_rows(route_ref[...], tokens)
        acts.wait()
        left_ref[tokens:, :] = dot(hot, left_ref[0:tokens, :]).astype(BF)

    for i in (2 * step, 2 * step + 1):
        load(i, pl.multiple_of(i * wide, wide)).wait()
    core = core_ref[0]
    for place, out_ref, routed_ref in (
        (1 - core, send_ref, send_routed_ref),
        (core, keep_ref, keep_routed_ref),
    ):
        product = dot(left_ref[...], blocks_ref[2 * step + place]).astype(BF)
        out_ref[0] = product[0:tokens]
        routed_ref[0] = product[tokens:]


def copies_kernel(rows_ref, p1, p2, out_ref, q1, q2, sems):
    copies = [
        pltpu.make_async_copy(rows_ref, out_ref.at[s], sems.at[s]) for s in range(out_ref.shape[0])
    ]
    for copy in copies:
        copy.start()
    for copy in copies:
        copy.wait()


def core_sum_kernel(x_ref, *refs):
    ways = len(refs) // 3
    for j in range(ways):
        total = refs[j][...].astype(F32) + refs[ways + j][...].astype(F32)
        refs[2 * ways + j][...] = total.astype(BF).reshape(refs[2 * ways + j].shape)


def x_sum_kernel(*refs):
    total = refs[0][...].astype(F32)
    for ref in refs[1:-1]:
        total = total + ref[...].astype(F32)
    refs[-1][...] = total.astype(refs[-1].dtype)


def routed_sum_kernel(y_ref, route_ref, residual_ref, passed_ref, *refs):
    ins, (send_ref, keep_ref) = refs[:8], refs[8:10]
    x_sum_kernel(*ins[:4], send_ref)
    x_sum_kernel(*ins[4:], keep_ref)
    hot = slot_rows(route_ref[...], residual_ref.shape[1])
    keep_ref[0] = keep_ref[0] + dot(hot, residual_ref[...], 1, 1)


def halves_kernel(x_ref, *refs):
    ins, (keep_a, send_a, keep_b, send_b) = refs[:8], refs[8:]
    sums = [(ins[m][0].astype(F32) + ins[4 + m][0].astype(F32)).astype(BF) for m in range(4)]
    for half, ref, order in ((0, keep_a, (0, 3)), (0, send_a, (1, 2)), (1, keep_b, (0, 1)), (1, send_b, (3, 2))):
        for i, m in enumerate(order):
            ref[i, 0] = sums[m][half]


def first_sum_kernel(keep_a, got_a, keep_b, got_b, own_a, on_a, own_b, on_b):
    for keep, got, own, on in ((keep_a, got_a, own_a, on_a), (keep_b, got_b, own_b, on_b)):
        own[...] = keep[0].astype(F32) + got[0].astype(F32)
        on[...] = (keep[1].astype(F32) + got[1].astype(F32)).astype(BF)


def second_sum_kernel(y_ref, *refs):
    ins, (send_ref, keep_ref) = refs[:8], refs[8:]
    for half in range(2):
        own, got, other_own, other_got = ins[4 * half : 4 * half + 4]
        send_ref[half] = (other_own[0] + other_got[0].astype(F32)).astype(BF)
        keep_ref[half] = own[0] + got[0].astype(F32)


def residual_kernel(residual_ref, keep_ref, got_ref, out_ref):
    summed = (keep_ref[...] + got_ref[...].astype(F32)).reshape(-1, keep_ref.shape[2])
    out_ref[...] = (residual_ref[...].astype(F32) + summed.T).astype(BF)


def up_kernel(
    group_ref, got_ref, gain_ref, gate_ref, up_ref, after_ref,
    out_ref, rows_ref, chosen_ref, padded_ref, weights_ref, sems,
):
    loads = [
        pltpu.make_async_copy(ref, weights_ref.at[i], sems.at[i])
        for i, ref in enumerate((gate_ref, up_ref))
    ]
    for load in loads:
        load.start()
    sources, height, wide = got_ref.shape
    groups = sources // 2
    half, side = height - 8, wide // 2
    slots = 2 * half
    per = out_ref.shape[1]
    total = groups * per

    for s in range(sources):
        g, d = s // 2, s % 2
        block = got_ref[s, 0:half, :]
        padded_ref[g * slots : g * slots + half, d * side : (d + 1) * side] = block[:, 0:side]
        padded_ref[g * slots + half : (g + 1) * slots, d * side : (d + 1) * side] = block[:, side:]
    at = half
    counts = [got_ref[2 * g, at : at + 8, 0 : 2 * slots].astype(F32)[0:1] for g in range(groups)]

    row = lax.broadcasted_iota(jnp.int32, (total, 2 * slots), 0)
    lane = lax.broadcasted_iota(jnp.int32, (total, 2 * slots), 1)
    second = lane >= slots
    slot = jnp.where(second, lane - slots, lane)
    slot_f = slot.astype(F32)
    shift = (row - slot).astype(F32)
    x = jnp.zeros((total, wide), F32)
    run = jnp.zeros_like(counts[0])
    for q in range(groups // 2):
        one, two = counts[2 * q], counts[2 * q + 1]
        start = jnp.where(second, run + one, run)
        count = jnp.where(second, two, one)
        run = run + one + two
        chosen = jnp.where((shift == start) & (slot_f < count), 1.0, 0.0).astype(BF)
        chosen_ref[:, 2 * q * slots : 2 * (q + 1) * slots] = chosen
        x = x + dot(chosen, padded_ref[2 * q * slots : 2 * (q + 1) * slots, :])

    square = jnp.sum(x * x, axis=1, keepdims=True)
    high = square.astype(BF)
    low = (square - high.astype(F32)).astype(BF)
    lane128 = lax.broadcasted_iota(jnp.int32, (total, 128), 1)
    squares = jnp.where(lane128 < 64, high.astype(F32), low.astype(F32)).astype(BF)
    scaled = (x * gain_ref[...]).astype(BF)
    rows_ref[...] = scaled
    for load in loads:
        load.wait()
    gate = dot(scaled, weights_ref[0]).astype(BF)
    up = dot(scaled, weights_ref[1]).astype(BF)
    at = 2 * wide + 128
    for g in range(groups):
        own = slice(g * per, (g + 1) * per)
        out_ref[g, :, 0:wide] = gate[own]
        out_ref[g, :, wide : 2 * wide] = up[own]
        out_ref[g, :, 2 * wide : at] = squares[own]


def hidden_kernel(
    features, got_ref, keep_ref, other_ref, p1, p2,
    out_ref, gate_ref, up_ref, scale_ref, q1, q2,
):
    per, wide = gate_ref.shape
    at = got_ref.shape[2]
    total = got_ref[0, :, 0:at].astype(F32)
    for g in range(1, got_ref.shape[0]):
        total = total + got_ref[g, :, 0:at].astype(F32)
    square = total[:, 2 * wide : 2 * wide + 1] + total[:, 2 * wide + 64 : 2 * wide + 65]
    scale = lax.rsqrt(square * (1.0 / features) + EPS)
    gate = total[:, 0:wide] * scale
    up = total[:, wide : 2 * wide] * scale
    gate_ref[...] = gate
    up_ref[...] = up
    scale_ref[...] = jnp.broadcast_to(scale, scale_ref.shape)
    hidden = (gate * jax.nn.sigmoid(gate) * up).astype(BF)
    routed = (keep_ref[0] + other_ref[0].astype(F32)).astype(BF)
    for g in range(out_ref.shape[0]):
        out_ref[g, 0:per, :] = hidden
        out_ref[g, per:, :] = routed


def down_kernel(
    group_ref, got_ref, down_ref, chosen_ref, projector_ref, after_ref,
    out_ref, hidden_ref, rows_ref, block_ref, sem,
):
    wide = block_ref.shape[1]
    first = pl.multiple_of(group_ref[0] * wide, wide)
    load = pltpu.make_async_copy(projector_ref.at[:, pl.ds(first, wide)], block_ref, sem)
    load.start()
    groups = got_ref.shape[0]
    per = hidden_ref.shape[0] // groups
    slots = got_ref.shape[1] - per
    for g in range(groups):
        hidden_ref[g * per : (g + 1) * per, :] = got_ref[g, 0:per, :]
        rows_ref[g * slots : (g + 1) * slots, :] = got_ref[g, per:, :]
    rows = dot(chosen_ref[...], rows_ref[...]).astype(BF)
    part = dot(hidden_ref[...], down_ref[...], 1, 1)
    load.wait()
    part = part - dot(rows, block_ref[...])
    out_ref[...] = part.astype(BF).reshape(out_ref.shape)


def misfit_kernel(scale, got_ref, out_ref):
    total = got_ref[0].astype(F32)
    for s in range(1, got_ref.shape[0]):
        total = total + got_ref[s].astype(F32)
    grad = (total * scale).astype(BF)
    for s in range(out_ref.shape[0]):
        out_ref[s] = grad


def back_kernel(got_ref, down_ref, passed_ref, out_ref, same_ref):
    groups, per, wide = out_ref.shape
    part = dot(got_ref[...].reshape(groups * per, got_ref.shape[2]), down_ref[...])
    out_ref[...] = part.astype(BF).reshape(groups, per, wide)


def acts_kernel(got_ref, gate_ref, up_ref, scale_ref, out_ref):
    wide = gate_ref.shape[1]
    grad = got_ref[0].astype(F32)
    for g in range(1, got_ref.shape[0]):
        grad = grad + got_ref[g].astype(F32)
    grad = grad * scale_ref[:, 0:1]
    gate, up = gate_ref[...], up_ref[...]
    sigma = jax.nn.sigmoid(gate)
    grad_gate = (grad * up * sigma * (1.0 + gate * (1.0 - sigma))).astype(BF)
    grad_up = (grad * gate * sigma).astype(BF)
    for g in range(out_ref.shape[0]):
        out_ref[g, :, 0:wide] = grad_gate
        out_ref[g, :, wide : 2 * wide] = grad_up


def down_weights_kernel(grad_ref, hidden_ref, out_ref):
    rows, units = hidden_ref.shape
    out_ref[...] = dot(grad_ref[...].reshape(rows, out_ref.shape[0]), hidden_ref[...], 0, 0)


def weights_kernel(rows_ref, got_ref, gate_ref, up_ref, parts_ref, sems):
    wide = gate_ref.shape[1]
    tall = parts_ref.shape[1]
    acts = got_ref[...].reshape(got_ref.shape[0] * got_ref.shape[1], 2 * wide)
    copies = []
    for i, out_ref in enumerate((gate_ref, up_ref)):
        for first in range(0, gate_ref.shape[0], tall):
            n = len(copies)
            rows = rows_ref[:, first : first + tall]
            parts_ref[n] = dot(rows, acts[:, i * wide : (i + 1) * wide], 0, 0)
            copy = pltpu.make_async_copy(
                parts_ref.at[n], out_ref.at[first : first + tall, :], sems.at[n]
            )
            copy.start()
            copies.append(copy)
    for copy in copies:
        copy.wait()


def on_device(
    attn_values,
    out_weight,
    residual_t,
    projector,
    student_input,
    norm_gain,
    w_gate,
    w_up,
    w_down,
    route_index,
):
    groups, parts = lax.axis_size("batch"), lax.axis_size("tensor")
    slots = route_index.shape[1]
    tokens, wide = attn_values.shape
    side = student_input.shape[1]
    features = norm_gain.shape[0]
    live = tokens * groups // 8
    per = live // groups
    units = w_gate.shape[1]
    extra = slots // 2 + 8
    group, part = lax.axis_index("batch"), lax.axis_index("tensor")
    core, x_at, y_at = part & 1, (part >> 1) & 3, part >> 3
    shape = jax.ShapeDtypeStruct
    vmem = pl.BlockSpec(memory_space=pltpu.VMEM)
    anywhere = pl.BlockSpec(memory_space=pl.ANY)

    def hbm(value):
        return pltpu.with_memory_space_constraint(value, pltpu.HBM)

    out_weight, w_gate, w_up, projector, student_input, route_index = (
        hbm(w) for w in (out_weight, w_gate, w_up, projector, student_input, route_index)
    )

    rows = pl.pallas_call(
        rows_kernel,
        out_shape=pltpu.HBM((extra, 2 * side), BF),
        cost_estimate=cost(2 * slots * tokens * side, MIB // 4),
        compiler_params=params(4),
        name="rows",
    )(route_index, student_input)
    pairs = [
        (b * parts + t, (t // 2) * parts + 2 * b + t % 2)
        for b in range(groups)
        for t in range(parts)
    ]
    rows = lax.ppermute(rows, ("batch", "tensor"), pairs)

    keep, send, keep_routed, send_routed = pl.pallas_call(
        teacher_kernel,
        grid_spec=pltpu.PrefetchScalarGridSpec(
            num_scalar_prefetch=1,
            grid=(parts // 2,),
            in_specs=[
                pl.BlockSpec(route_index.shape, lambda j, core: (0, 0)),
                anywhere,
                anywhere,
            ],
            out_specs=[pl.BlockSpec((1, tokens, wide), lambda j, core: (j, 0, 0))] * 2
            + [pl.BlockSpec((1, slots, wide), lambda j, core: (j, 0, 0))] * 2,
            scratch_shapes=[
                pltpu.VMEM((tokens + slots, wide), BF),
                pltpu.VMEM((parts, wide, wide), BF),
                pltpu.SemaphoreType.DMA((parts + 1,)),
            ],
        ),
        out_shape=[pltpu.HBM((parts // 2, tokens, wide), BF)] * 2
        + [pltpu.HBM((parts // 2, slots, wide), BF)] * 2,
        compiler_params=params(20),
        cost_estimate=cost(2 * (tokens + slots) * wide * wide * parts, 14 * MIB),
        name="teacher",
    )(core.reshape(1), route_index, hbm(attn_values), out_weight)
    copies, send_routed, send = pl.pallas_call(
        copies_kernel,
        in_specs=[vmem] + [anywhere] * 2,
        out_specs=[anywhere] * 3,
        out_shape=[
            pltpu.HBM((parts, *rows.shape), BF),
            pltpu.HBM(send_routed.shape, BF),
            pltpu.HBM(send.shape, BF),
        ],
        scratch_shapes=[pltpu.SemaphoreType.DMA((parts,))],
        input_output_aliases={1: 1, 2: 2},
        compiler_params=params(4),
        cost_estimate=cost(0, MIB // 2),
        name="copies",
    )(rows, send_routed, send)
    every = lax.all_to_all(copies, "tensor", 0, 0, tiled=True)

    def along(value, move):
        return lax.ppermute(value, "tensor", [(t, move(t // 8, (t // 2) % 4, t % 2)) for t in range(parts)])

    def core_sum(keep, send, height):
        got = along(send, lambda y, x, c: y * 8 + x * 2 + 1 - c)
        block = (2, 1, height, wide)
        return pl.pallas_call(
            core_sum_kernel,
            grid_spec=pltpu.PrefetchScalarGridSpec(
                num_scalar_prefetch=1,
                grid=(1,),
                in_specs=[
                    pl.BlockSpec(block, lambda i, x, j=j: (0, (x[0] + j) & 3, 0, 0))
                    for j in range(4)
                ]
                * 2,
                out_specs=[pl.BlockSpec((2, height, wide), lambda i, x: (0, 0, 0))] * 4,
            ),
            out_shape=[pltpu.HBM((2, height, wide), BF)] * 4,
            compiler_params=params(16),
            cost_estimate=cost(MIB, 24 * height * wide * 2),
            name="core_sum",
        )(
            x_at.reshape(1),
            *[hbm(keep.reshape(2, 4, height, wide))] * 4,
            *[got.reshape(2, 4, height, wide)] * 4,
        )

    def along_x(own, moved):
        return [own] + [
            along(moved[j - 1], lambda y, x, c, j=j: y * 8 + (x + j) % 4 * 2 + c)
            for j in range(1, 4)
        ]

    def along_y(send):
        return along(send, lambda y, x, c: (1 - y) * 8 + x * 2 + c)

    def y_blocks(strip):
        block = (1, strip, wide)
        return [pl.BlockSpec(block, lambda i, y: (1 - y[0], i, 0))] * 4 + [
            pl.BlockSpec(block, lambda i, y: (y[0], i, 0))
        ] * 4

    half, strip = tokens // 2, tokens // 4
    got = along(send, lambda y, x, c: y * 8 + x * 2 + 1 - c)
    halves = (parts // 2, 2, half, wide)
    pair = pltpu.HBM((2, 2, half, wide), BF)
    keep_a, send_a, keep_b, send_b = pl.pallas_call(
        halves_kernel,
        grid_spec=pltpu.PrefetchScalarGridSpec(
            num_scalar_prefetch=1,
            grid=(2, half // strip),
            in_specs=[
                pl.BlockSpec(
                    (1, 2, strip, wide),
                    lambda y, n, x, m=m: (4 * y + lax.bitwise_xor(x[0], jnp.int32(m)), 0, n, 0),
                )
                for m in range(4)
            ]
            * 2,
            out_specs=[pl.BlockSpec((2, 1, strip, wide), lambda y, n, x: (0, y, n, 0))] * 4,
        ),
        out_shape=[pair] * 4,
        compiler_params=params(16),
        cost_estimate=cost(MIB, 6 * MIB),
        name="halves",
    )(x_at.reshape(1), *[hbm(keep.reshape(halves))] * 4, *[got.reshape(halves)] * 4)

    def along_x_by(value, mask):
        return along(value, lambda y, x, c: y * 8 + (x ^ mask) * 2 + c)

    packed = 2 * wide + 128
    sent, scaled, chosen = pl.pallas_call(
        up_kernel,
        grid_spec=pltpu.PrefetchScalarGridSpec(
            num_scalar_prefetch=1,
            grid=(1,),
            in_specs=[vmem, pl.BlockSpec((1, wide), lambda i, group: (0, group[0]))]
            + [anywhere] * 3,
            out_specs=[vmem] * 3,
            scratch_shapes=[
                pltpu.VMEM((groups * slots, wide), BF),
                pltpu.VMEM((2, wide, units), BF),
                pltpu.SemaphoreType.DMA((2,)),
            ],
        ),
        out_shape=[
            pltpu.HBM((groups, per, packed), BF),
            pltpu.HBM((live, wide), BF),
            pltpu.HBM((live, groups * slots), BF),
        ],
        compiler_params=params(16),
        cost_estimate=cost(800 * MIB, 4 * MIB),
        name="up",
    )(group.reshape(1), every, norm_gain[None], w_gate, w_up, hbm(keep_a))

    routed, *moved = core_sum(keep_routed, send_routed, slots)
    send_routed, keep_routed, sent = pl.pallas_call(
        routed_sum_kernel,
        grid_spec=pltpu.PrefetchScalarGridSpec(
            num_scalar_prefetch=1,
            grid=(1,),
            in_specs=[vmem] * 2 + [anywhere] + y_blocks(slots),
            out_specs=[pl.BlockSpec((1, slots, wide), lambda i, y: (0, 0, 0))] * 2 + [anywhere],
        ),
        out_shape=[
            pltpu.HBM((1, slots, wide), BF),
            pltpu.HBM((1, slots, wide), F32),
            pltpu.HBM(sent.shape, BF),
        ],
        input_output_aliases={3: 2},
        compiler_params=params(8),
        cost_estimate=cost(MIB, MIB),
        name="routed_sum",
    )(y_at.reshape(1), route_index, residual_t, sent, *along_x(routed, moved) * 2)
    other_routed = along_y(send_routed)

    got = lax.all_to_all(sent, "batch", 0, 0, tiled=True)

    flat = shape((per, units), F32)
    block = pl.BlockSpec((2, 2, strip, wide), lambda n: (0, 0, n, 0))
    line = pl.BlockSpec((2, strip, wide), lambda n: (0, n, 0))
    own_a, on_a, own_b, on_b = pl.pallas_call(
        first_sum_kernel,
        grid=(half // strip,),
        in_specs=[block] * 4,
        out_specs=[line] * 4,
        out_shape=[pltpu.HBM((2, half, wide), F32), pltpu.HBM((2, half, wide), BF)] * 2,
        compiler_params=params(16),
        cost_estimate=cost(MIB, 3 * MIB),
        name="first_sum",
    )(keep_a, along_x_by(send_a, 1), keep_b, along_x_by(send_b, 3))
    both, gate, up, scale, on_a, on_b = pl.pallas_call(
        lambda *refs: hidden_kernel(features, *refs),
        in_specs=[vmem] * 3 + [anywhere] * 2,
        out_specs=[vmem] * 4 + [anywhere] * 2,
        out_shape=[
            pltpu.HBM((groups, per + slots, units), BF),
            flat,
            flat,
            shape((per, 128), F32),
        ]
        + [pltpu.HBM((2, half, wide), BF)] * 2,
        input_output_aliases={3: 4, 4: 5},
        compiler_params=params(8),
        cost_estimate=cost(MIB, MIB),
        name="hidden",
    )(got, keep_routed, other_routed, on_a, on_b)
    got_a, got_b = along_x_by(on_a, 3), along_x_by(on_b, 1)
    here = pl.BlockSpec((1, strip, wide), lambda n, y: (y[0], n, 0))
    there = pl.BlockSpec((1, strip, wide), lambda n, y: (1 - y[0], n, 0))
    send, keep = pl.pallas_call(
        second_sum_kernel,
        grid_spec=pltpu.PrefetchScalarGridSpec(
            num_scalar_prefetch=1,
            grid=(half // strip,),
            in_specs=[here, here, there, there] * 2,
            out_specs=[pl.BlockSpec((2, strip, wide), lambda n, y: (0, n, 0))] * 2,
        ),
        out_shape=[pltpu.HBM((2, half, wide), BF), pltpu.HBM((2, half, wide), F32)],
        compiler_params=params(16),
        cost_estimate=cost(MIB, 3 * MIB),
        name="second_sum",
    )(y_at.reshape(1), *[own_a, got_a] * 2, *[own_b, got_b] * 2)
    other = along_y(send)
    both = lax.all_to_all(both, "batch", 0, 0, tiled=True)
    misfit, hidden = pl.pallas_call(
        down_kernel,
        grid_spec=pltpu.PrefetchScalarGridSpec(
            num_scalar_prefetch=1,
            grid=(1,),
            in_specs=[vmem] * 3 + [anywhere] * 2,
            out_specs=[vmem] * 2,
            scratch_shapes=[
                pltpu.VMEM((groups * slots, wide), BF),
                pltpu.VMEM((wide, wide), BF),
                pltpu.SemaphoreType.DMA,
            ],
        ),
        out_shape=[
            pltpu.HBM((parts, live // parts, wide), BF),
            pltpu.HBM((live, units), BF),
        ],
        compiler_params=params(16),
        cost_estimate=cost(768 * MIB, 4 * MIB),
        name="down",
    )(group.reshape(1), both, w_down, chosen, projector, hbm(keep))
    misfit = lax.all_to_all(misfit, "tensor", 0, 0, tiled=True)
    loss_scale = 1.0 / math.sqrt(live)
    grad_out = pl.pallas_call(
        lambda *refs: misfit_kernel(loss_scale, *refs),
        out_shape=pltpu.HBM(misfit.shape, BF),
        compiler_params=params(8),
        cost_estimate=cost(MIB, MIB),
        name="misfit",
    )(misfit)
    grad_out = lax.all_to_all(grad_out, "tensor", 0, 0, tiled=True)

    teacher_hidden = pl.pallas_call(
        residual_kernel,
        out_shape=pltpu.HBM(residual_t.shape, BF),
        compiler_params=params(8),
        cost_estimate=cost(MIB, 2 * MIB),
        name="residual",
    )(residual_t, keep, other)
    back, teacher_hidden = pl.pallas_call(
        back_kernel,
        in_specs=[vmem] * 2 + [anywhere],
        out_specs=[vmem, anywhere],
        out_shape=[shape((groups, per, units), BF), pltpu.HBM(residual_t.shape, BF)],
        input_output_aliases={2: 1},
        compiler_params=params(16),
        cost_estimate=cost(256 * MIB, MIB),
        name="back",
    )(grad_out, w_down, teacher_hidden)
    back = lax.all_to_all(back, "batch", 0, 0, tiled=True)
    acts = pl.pallas_call(
        acts_kernel,
        out_shape=pltpu.HBM((groups, per, 2 * units), BF),
        compiler_params=params(8),
        cost_estimate=cost(MIB, MIB),
        name="acts",
    )(back, gate, up, scale)
    acts = lax.all_to_all(acts, "batch", 0, 0, tiled=True)
    grad_down = pl.pallas_call(
        down_weights_kernel,
        out_shape=shape((wide, units), F32),
        compiler_params=params(16),
        cost_estimate=cost(256 * MIB, 2 * MIB),
        name="down_weights",
    )(grad_out, hidden)
    grad_gate, grad_up = pl.pallas_call(
        weights_kernel,
        in_specs=[vmem] * 2,
        out_specs=[anywhere] * 2,
        out_shape=[pltpu.HBM((wide, units), F32)] * 2,
        scratch_shapes=[
            pltpu.VMEM((4, wide // 2, units), F32),
            pltpu.SemaphoreType.DMA((4,)),
        ],
        compiler_params=params(16),
        cost_estimate=cost(512 * MIB, 4 * MIB),
        name="weights",
    )(scaled, acts)
    return teacher_hidden, grad_gate, grad_up, grad_down


def solution(mesh):
    in_specs = (
        P("batch", "tensor"),
        P("tensor", None),
        P("tensor", "batch"),
        P("tensor", None),
        P("batch", "tensor"),
        P(),
        P("batch", "tensor"),
        P("batch", "tensor"),
        P("batch", "tensor"),
        P("batch", None),
    )
    out_specs = (P("tensor", "batch"),) + (P("batch", "tensor"),) * 3
    return jax.shard_map(
        on_device, mesh=mesh, in_specs=in_specs, out_specs=out_specs, check_vma=False
    )
```
